32 devices in a mesh: dp: 8 (over z, x), mp: 4 (over y, core).
Axes of the slice: x: 2, y: 2, z: 4, core: 2. Of those that a mesh axis runs over, the one named last changes fastest.
Arguments:
- inputs: bfloat16 [2, 16384, 768], P(None, ('dp', 'mp')), may hold values from -6 to 6
- lengths: int32 [2, 32], P(None, 'dp'), may hold values from 64 to 512
- membership: int32 [2, 32, 8], replicated, may hold values from 0 to 1, as said below
- w_query: bfloat16 [768, 768], P(None, 'mp'), may hold values from -0.21875 to 0.21875
- b_query: bfloat16 [768], P('mp'), may hold values from -1.75 to 1.75
- w_key: bfloat16 [768, 768], P(None, 'mp'), may hold values from -0.21875 to 0.21875
- w_value: bfloat16 [768, 768], P(None, 'mp'), may hold values from -0.21875 to 0.21875
- b_value: bfloat16 [768], P('mp'), may hold values from -1.75 to 1.75
- w_output: bfloat16 [768, 768], P('mp'), may hold values from -0.875 to 0.875
- b_output: bfloat16 [768], replicated, may hold values from -0.625 to 0.625
- gain_first: bfloat16 [768], replicated, may hold values from 0.5 to 1.5
- bias_first: bfloat16 [768], replicated, may hold values from -0.625 to 0.625
- w_inner: bfloat16 [768, 3072], P(None, 'mp'), may hold values from -0.21875 to 0.21875
- b_inner: bfloat16 [3072], P('mp'), may hold values from -1.75 to 1.75
- w_outer: bfloat16 [3072, 768], P('mp'), may hold values from -0.109375 to 0.109375
- b_outer: bfloat16 [768], replicated, may hold values from -0.625 to 0.625
- gain_second: bfloat16 [768], replicated, may hold values from 0.5 to 1.5
- bias_second: bfloat16 [768], replicated, may hold values from -0.625 to 0.625
Outputs:
- outputs: bfloat16 [2, 16384, 768], P(None, ('dp', 'mp'))
- loss_total: float32 [], replicated
- grad_inputs: float32 [2, 16384, 768], P(None, ('dp', 'mp'))
- grad_w_query: float32 [768, 768], P(None, 'mp')
- grad_b_query: float32 [768], P('mp')
- grad_w_key: float32 [768, 768], P(None, 'mp')
- grad_w_value: float32 [768, 768], P(None, 'mp')
- grad_b_value: float32 [768], P('mp')
- grad_w_output: float32 [768, 768], P('mp')
- grad_b_output: float32 [768], replicated
- grad_gain_first: float32 [768], replicated
- grad_bias_first: float32 [768], replicated
- grad_w_inner: float32 [768, 3072], P(None, 'mp')
- grad_b_inner: float32 [3072], P('mp')
- grad_w_outer: float32 [3072, 768], P('mp')
- grad_b_outer: float32 [768], replicated
- grad_gain_second: float32 [768], replicated
- grad_bias_second: float32 [768], replicated
The draws below stay inside these ranges and needn't reach their ends.
Inputs may be any that keep to these rules, and one draw needn't show every extreme that they name: `membership`: each row has a single 1. Each of the 8 groups holds 2 to 7 sentences, and some group holds exactly 7 in every draw.
All inputs are finite; a program needn't handle non-finite values.
Results may differ from the reference program's by a relative error of at most 0.015.
Values may be sent and summed in bfloat16 or wider, within the bound.
No kernel may reach another device: no remote copies, remote signals or barrier semaphores. Data moves between devices by JAX's collectives and lax.ppermute only.
A program may use at most 192 MiB of HBM per device.

```python
import math
from functools import partial
import jax
import jax.numpy as jnp
from jax import lax

D = 768
HEADS = 12
HEAD_DIM = 64
FF = 3072
SEQ_LEN = 512
MICRO = 2
SENTS = 32
TOKENS = 16384
GROUPS = 8


def draw_membership(key, part):
    pieces = []
    for micro_index in range(MICRO):
        micro_key = jax.random.fold_in(key, 11 + micro_index)
        ordering = jax.random.permutation(micro_key, SENTS)
        rank_ids = jnp.arange(SENTS, dtype=jnp.int32)
        block_ids = rank_ids // 16
        within = rank_ids % 16
        slot_ids = (within >= 2).astype(jnp.int32) + (within >= 4).astype(jnp.int32) + (within >= 9).astype(jnp.int32)
        group_of_rank = block_ids * 4 + slot_ids
        group_of_sentence = jnp.zeros((SENTS,), jnp.int32).at[ordering].set(group_of_rank)
        relabel = jax.random.permutation(jax.random.fold_in(micro_key, 5), GROUPS)
        group_ids = relabel[group_of_sentence]
        onehot = (group_ids[:, None] == jnp.arange(GROUPS, dtype=jnp.int32)[None, :]).astype(jnp.int32)
        pieces.append(onehot)
    return jnp.stack(pieces)


def with_ends(values, own_key, low, largest):
    index_at = [jax.random.randint(jax.random.fold_in(own_key, axis), (), 0, length) for axis, length in enumerate(values.shape)]
    widest = values.shape.index(max(values.shape))
    neighbour = index_at[:widest] + [(index_at[widest] + 1) % values.shape[widest]] + index_at[widest + 1:]
    return values.at[tuple(index_at)].set(low).at[tuple(neighbour)].set(largest)


def shard_levels(own_key, dims, cuts, smallest, high):
    level = 1.0
    for position, blocks in cuts:
        steps = jax.random.uniform(jax.random.fold_in(jax.random.fold_in(own_key, 6), position), (blocks,), jnp.float32, smallest / len(cuts), high / len(cuts))
        level = level * jnp.repeat(jnp.exp(steps), dims[position] // blocks).reshape((-1,) + (1,) * (len(dims) - 1 - position))
    return level


def bell_draw(stream_key, extent, scale, limit, cuts=(), kind=jnp.bfloat16):
    values = jax.random.normal(stream_key, extent, jnp.float32) * scale
    if len(cuts) > 0:
        values = shard_levels(stream_key, extent, cuts, -0.22, 0.18) * values
    return jnp.clip(values, min=-limit, max=limit).astype(kind)


def setup_inputs(seed: int = 0) -> dict:
    streams_of = jax.random.split(jax.random.key(seed), 19)
    inputs = bell_draw(streams_of[0], (MICRO, TOKENS, D), 1.0, 6.0, ((1, 32),))
    lengths = with_ends(jax.random.randint(streams_of[1], (MICRO, SENTS), SEQ_LEN // 8, SEQ_LEN + 1), jax.random.fold_in(streams_of[1], 1), SEQ_LEN // 8, SEQ_LEN).astype(jnp.int32)
    membership = draw_membership(jax.random.fold_in(streams_of[18], 71), 0)
    w_query = bell_draw(streams_of[3], (D, D), D ** -0.5, 0.21875, ((1, 4),))
    b_query = bell_draw(streams_of[4], (D,), 0.3, 1.75, ((0, 4),))
    w_key = bell_draw(streams_of[5], (D, D), D ** -0.5, 0.21875, ((1, 4),))
    w_value = bell_draw(streams_of[6], (D, D), D ** -0.5, 0.21875, ((1, 4),))
    b_value = bell_draw(streams_of[7], (D,), 0.3, 1.75, ((0, 4),))
    w_output = bell_draw(streams_of[8], (D, D), (min(D, D * 32 // SEQ_LEN)) ** -0.5, 0.875, ((0, 4),))
    b_output = bell_draw(streams_of[9], (D,), 0.1, 0.625)
    gain_first = jnp.clip(1.0 + 0.1 * jax.random.normal(streams_of[10], (D,), jnp.float32), 0.5, 1.5).astype(jnp.bfloat16)
    bias_first = bell_draw(streams_of[11], (D,), 0.1, 0.625)
    w_inner = bell_draw(streams_of[12], (D, FF), D ** -0.5, 0.21875, ((1, 4),))
    b_inner = bell_draw(streams_of[13], (FF,), 0.3, 1.75, ((0, 4),))
    w_outer = bell_draw(streams_of[14], (FF, D), FF ** -0.5, 0.109375, ((0, 4),))
    b_outer = bell_draw(streams_of[15], (D,), 0.1, 0.625)
    gain_second = jnp.clip(1.0 + 0.1 * jax.random.normal(streams_of[16], (D,), jnp.float32), 0.5, 1.5).astype(jnp.bfloat16)
    bias_second = bell_draw(streams_of[17], (D,), 0.1, 0.625)
    return {"inputs": inputs, "lengths": lengths, "membership": membership, "w_query": w_query, "b_query": b_query, "w_key": w_key, "w_value": w_value, "b_value": b_value, "w_output": w_output, "b_output": b_output, "gain_first": gain_first, "bias_first": bias_first, "w_inner": w_inner, "b_inner": b_inner, "w_outer": w_outer, "b_outer": b_outer, "gain_second": gain_second, "bias_second": bias_second}


@jax.custom_vjp
def low(v):
    return lax.optimization_barrier(v.astype(jnp.bfloat16)).astype(jnp.float32)

@jax.custom_vjp
def low_back(v):
    return v

def low_keep(v):
    return (low(v), None)

def low_pass(kept, grad):
    return (grad,)

def back_keep(v):
    return (v, None)

def back_low(kept, grad):
    return (low(grad),)
low.defvjp(low_keep, low_pass)
low_back.defvjp(back_keep, back_low)
eps_norm = 1e-05
eps_unit = 1e-06
cos_scale = 20.0
block_sents = 8

def matmul(left, right):
    return jnp.dot(left, right, precision=lax.Precision.HIGHEST, preferred_element_type=jnp.float32)

def layer_norm(row_values, norm_gain, norm_bias):
    centred = row_values - lax.optimization_barrier(jnp.mean(row_values, axis=-1, keepdims=True))
    spread = lax.optimization_barrier(jnp.mean(centred * centred, axis=-1, keepdims=True))
    return centred * lax.rsqrt(spread + eps_norm) * norm_gain + norm_bias

def attend(queries, key_rows, values, length):
    inv_root = 1.0 / math.sqrt(HEAD_DIM)
    query_heads = queries.reshape(SEQ_LEN, HEADS, HEAD_DIM)
    key_heads = key_rows.reshape(SEQ_LEN, HEADS, HEAD_DIM)
    value_heads = values.reshape(SEQ_LEN, HEADS, HEAD_DIM)
    raw_scores = jnp.einsum('qhd,khd->hqk', query_heads, key_heads, precision=lax.Precision.HIGHEST) * inv_root
    scores = low_back(raw_scores)
    allowed = jnp.arange(SEQ_LEN) < length
    masked = jnp.where(allowed[None, None, :], scores, -1e+30)
    row_top = lax.optimization_barrier(jnp.max(masked, axis=-1, keepdims=True))
    raised = jnp.exp(masked - row_top)
    prob_rows = raised / lax.optimization_barrier(jnp.sum(raised, axis=-1, keepdims=True))
    context = jnp.einsum('hqk,khd->qhd', low(prob_rows), value_heads, precision=lax.Precision.HIGHEST)
    return context.reshape(SEQ_LEN, D)

def block_forward(weights, packed):
    row_values, sent_lengths = packed
    w_query, b_query, w_key, w_value, b_value, w_output, b_output, gain_first, bias_first, w_inner, b_inner, w_outer, b_outer, gain_second, bias_second = weights
    number = sent_lengths.shape[0]
    queries = low(low_back(matmul(row_values, w_query) + b_query))
    key_rows = low(low_back(matmul(row_values, w_key)))
    values = low(low_back(matmul(row_values, w_value) + b_value))
    context = jax.vmap(attend)(queries.reshape(number, SEQ_LEN, D), key_rows.reshape(number, SEQ_LEN, D), values.reshape(number, SEQ_LEN, D), sent_lengths)
    context = low(low_back(context.reshape(number * SEQ_LEN, D)))
    attn_sum = low_back(matmul(context, w_output))
    first_norm = layer_norm(attn_sum + b_output + row_values, gain_first, bias_first)
    inner_pre = low_back(matmul(low(first_norm), w_inner) + b_inner)
    hidden = low(jax.nn.gelu(inner_pre, approximate=False))
    ffn_sum = low_back(matmul(hidden, w_outer))
    second_norm = layer_norm(ffn_sum + b_outer + first_norm, gain_second, bias_second)
    valid_mask = (jnp.arange(SEQ_LEN)[None, :] < sent_lengths[:, None]).astype(jnp.float32)
    pooled = lax.optimization_barrier(jnp.sum(second_norm.reshape(number, SEQ_LEN, D) * valid_mask[:, :, None], axis=1)) / sent_lengths[:, None].astype(jnp.float32)
    return (second_norm, pooled)

def micro_loss(unit_rows, groups_all):
    same_group = matmul(groups_all, groups_all.T)
    itself = jnp.eye(SENTS, dtype=same_group.dtype)
    positive = same_group - itself
    logits = cos_scale * matmul(unit_rows, unit_rows.T)
    others = jnp.where(itself > 0.5, -1e+30, logits)
    row_top = lax.optimization_barrier(jnp.max(others, axis=1, keepdims=True))
    raised = jnp.exp(others - row_top)
    log_all = jnp.log(lax.optimization_barrier(jnp.sum(raised, axis=1)))
    log_pos = jnp.log(lax.optimization_barrier(jnp.sum(raised * positive, axis=1)))
    return jnp.sum(log_all - log_pos)

def reference(inputs, lengths, membership, w_query, b_query, w_key, w_value, b_value, w_output, b_output, gain_first, bias_first, w_inner, b_inner, w_outer, b_outer, gain_second, bias_second):
    weights = tuple((weight_item.astype(jnp.float32) for weight_item in (w_query, b_query, w_key, w_value, b_value, w_output, b_output, gain_first, bias_first, w_inner, b_inner, w_outer, b_outer, gain_second, bias_second)))
    rows_all = inputs.astype(jnp.float32)

    def objective(rows_all, weights):
        loss_sum = jnp.zeros((), jnp.float32)
        outputs_list = []
        for micro_index in range(MICRO):
            row_blocks = rows_all[micro_index].reshape(SENTS // block_sents, block_sents * SEQ_LEN, D)
            length_blocks = lengths[micro_index].reshape(SENTS // block_sents, block_sents)
            second_norm, pooled = lax.map(jax.checkpoint(partial(block_forward, weights)), (row_blocks, length_blocks))
            pooled = pooled.reshape(SENTS, D)
            unit_rows = pooled * lax.rsqrt(lax.optimization_barrier(jnp.sum(pooled * pooled, axis=1, keepdims=True)) + eps_unit)
            loss_sum = loss_sum + micro_loss(unit_rows, membership[micro_index].astype(jnp.float32))
            outputs_list.append(second_norm.reshape(TOKENS, D))
        return (loss_sum, jnp.stack(outputs_list))
    loss_total, back_fn, outputs = jax.vjp(objective, rows_all, weights, has_aux=True)
    grad_rows, grad_weights = back_fn(jnp.ones_like(loss_total))
    return (outputs.astype(jnp.bfloat16), loss_total, grad_rows, grad_weights[0], grad_weights[1], grad_weights[2], grad_weights[3], grad_weights[4], grad_weights[5], grad_weights[6], grad_weights[7], grad_weights[8], grad_weights[9], grad_weights[10], grad_weights[11], grad_weights[12], grad_weights[13], grad_weights[14])
```

```python
import functools
import math

import jax
import jax.numpy as jnp
from jax import lax
from jax.experimental import pallas as pl
from jax.experimental.pallas import tpu as pltpu
from jax.sharding import PartitionSpec as P

HEAD = 64
SEQ = 512
EPS_NORM = 1e-5
EPS_UNIT = 1e-6
COS_SCALE = 20.0
LOG2E = 1.4426950408889634
NEG = -1e30
F32 = jnp.float32
BF16 = jnp.bfloat16
VMEM_LIMIT = 56 << 20
CORE, YBIT, XBIT = 1, 2, 4
PAD = 16


def dot(a, b, ca, cb, precision=None):
    return lax.dot_general(
        a, b, (((ca,), (cb,)), ((), ())), preferred_element_type=F32, precision=precision
    )


def mm(a, b):
    return dot(a, b, 1, 0)


def mm_nt(a, b):
    return dot(a, b, 1, 1)


def mm_tn(a, b):
    return dot(a, b, 0, 0)


def column(row):
    return jnp.broadcast_to(row, (8, row.shape[1])).T[:, :1]


def call(kernel, grid, ins, outs, scratch=(), prefetch=0, name=None, us=10):
    def spec(block, index):
        return pl.BlockSpec(block, index)

    def whole(a):
        rank = len(a)
        return pl.BlockSpec(tuple(a), lambda *_: (0,) * rank)

    def run(*args):
        in_specs = []
        for item, arg in zip(ins, args[prefetch:]):
            in_specs.append(whole(arg.shape) if item is None else spec(*item))
        out_specs = [whole(o[0]) if len(o) == 2 else spec(*o[2:]) for o in outs]
        return pl.pallas_call(
            kernel,
            out_shape=[jax.ShapeDtypeStruct(o[0], o[1]) for o in outs],
            grid_spec=pltpu.PrefetchScalarGridSpec(
                num_scalar_prefetch=prefetch,
                grid=grid,
                in_specs=in_specs,
                out_specs=out_specs,
                scratch_shapes=list(scratch),
            ),
            compiler_params=pltpu.CompilerParams(vmem_limit_bytes=VMEM_LIMIT),
            cost_estimate=pl.CostEstimate(flops=int(us * 1.1e9), transcendentals=0, bytes_accessed=1000),
            name=name,
        )(*args)

    return run


def pack_att_kernel(bits_ref, wq, wk, wv, wo, bq, bv, att_ref, send_ref):
    n = wo.shape[0]
    att_ref[0:n, :] = wq[...]
    att_ref[n : 2 * n, :] = wk[...]
    att_ref[2 * n : 3 * n, :] = wv[...]
    att_ref[3 * n : 4 * n, :] = wo[...]
    rows = att_ref.shape[0] - 4 * n
    att_ref[4 * n :, :] = jnp.zeros_like(att_ref[4 * n :, :])
    att_ref[4 * n :, 0:n] = jnp.broadcast_to(bq[...], (rows, n))
    att_ref[4 * n :, 2 * n : 3 * n] = jnp.broadcast_to(bv[...], (rows, n))
    half = att_ref.shape[0] // 2
    send_ref[...] = att_ref[pl.ds(pl.multiple_of(bits_ref[0] * half, 16), half), :]


def pack_ffn_kernel(bits_ref, win, bin_, wout, in_ref, out_ref, in_send, out_send):
    x = bits_ref[0]
    units = win.shape[1] // 2
    size = units + PAD
    for piece in range(2):
        take = pl.multiple_of((x if piece == 0 else 1 - x) * units, 128)
        base = piece * size
        in_ref[base : base + units, :] = win[:, pl.ds(take, units)].T
        in_ref[base + units : base + size, :] = jnp.zeros((PAD, in_ref.shape[1]), BF16)
        in_ref[base + units : base + size, 0:units] = jnp.broadcast_to(
            bin_[:, pl.ds(take, units)], (PAD, units)
        )
        out_ref[piece * units : (piece + 1) * units, :] = wout[pl.ds(take, units), :]
    in_send[...] = in_ref[0:size, :]
    out_send[...] = out_ref[0:units, :]


def key_rows(length, ones):
    row = lax.broadcasted_iota(jnp.int32, (PAD, SEQ), 0)
    pos = lax.broadcasted_iota(jnp.int32, (PAD, SEQ), 1)
    base = jnp.where((row >= 1) & (row <= ones), 1.0, 0.0)
    return jnp.where((row == 0) & (pos >= length), NEG, base).astype(BF16)


def split_rows(first, value):
    row = lax.broadcasted_iota(jnp.int32, (PAD, SEQ), 0)
    high = value.astype(BF16).astype(F32)
    middle = (value - high).astype(BF16).astype(F32)
    lower = value - high - middle
    out = jnp.where(row == 0, first, 0.0)
    for i, part in enumerate((high, middle, lower)):
        out = jnp.where(row == i + 1, part, out)
    return out.astype(BF16)


def stack(*parts):
    return jnp.concatenate(parts, axis=0)


def attention_forward(len_ref, x_ref, packs, qkv_ref, ctx_ref, lse_ref, csum_ref, wo_scr, per):
    length = len_ref[pl.program_id(0)]
    scale = LOG2E / math.sqrt(HEAD)
    n = per * HEAD

    @pl.when(pl.program_id(0) == 0)
    def _():
        for r, w in enumerate(packs):
            wo_scr[r * n : (r + 1) * n, :] = w[3 * n : 4 * n, :]
        csum_ref[...] = jnp.zeros_like(csum_ref)

    keys = key_rows(length, 0)
    ones = jnp.ones((PAD, SEQ), BF16)
    x = x_ref[...]
    for r, w in enumerate(packs):
        bias = column(w[4 * n : 4 * n + 1, 0 : 3 * n].astype(F32))
        qkv_ref[3 * n * r : 3 * n * (r + 1), :] = (mm_nt(w[0 : 3 * n, :], x) + bias).astype(BF16)
    for r in range(len(packs)):
        for h in range(per):
            a = 3 * n * r + h * HEAD
            q = stack(qkv_ref[a : a + HEAD, :], ones)
            k = stack(qkv_ref[n + a : n + a + HEAD, :], keys)
            v = stack(qkv_ref[2 * n + a : 2 * n + a + HEAD, :], ones)
            s = mm_tn(k, q)
            top = jnp.max(s, axis=0, keepdims=True)
            e = jnp.exp2(s * scale - top * scale).astype(BF16)
            c = mm(v, e)
            total = c[HEAD : HEAD + 1, :]
            b = n * r + h * HEAD
            ctx_ref[b : b + HEAD, :] = (c[0:HEAD, :] * (1.0 / total)).astype(BF16)
            lse_ref[r * per + h : r * per + h + 1, :] = top + jnp.log2(total) * (1.0 / scale)
    ctx = ctx_ref[...]
    csum_ref[...] += mm_nt(jnp.ones((8, SEQ), BF16), ctx)
    return mm_tn(ctx, wo_scr[...])


def attend_near_kernel(
    len_ref, x_ref, w0, w1, qkv_ref, ctx_ref, lse_ref, csum_ref, attn_ref, xsum_ref, wo_scr, *, per
):
    attn_ref[...] = attention_forward(
        len_ref, x_ref, (w0, w1), qkv_ref, ctx_ref, lse_ref, csum_ref, wo_scr, per
    )

    @pl.when(pl.program_id(0) == 0)
    def _():
        xsum_ref[...] = jnp.zeros_like(xsum_ref)

    xsum_ref[0:1, :] += jnp.sum(x_ref[...].astype(F32), axis=0, keepdims=True)


def normalise(v):
    mean = jnp.mean(v, axis=-1, keepdims=True)
    centred = v - mean
    inv = lax.rsqrt(jnp.mean(centred * centred, axis=-1, keepdims=True) + EPS_NORM)
    return centred * inv, inv


def attend_far_kernel(
    len_ref, x_ref, w0, w1, prev_ref, vec_ref,
    qkv_ref, ctx_ref, lse_ref, csum_ref, norm_ref, inv_ref, low_ref, lsum_ref, wo_scr, *, per
):
    attn = attention_forward(
        len_ref, x_ref, (w0, w1), qkv_ref, ctx_ref, lse_ref, csum_ref, wo_scr, per
    )
    pre = attn + prev_ref[...] + vec_ref[0:1, :] + x_ref[...].astype(F32)
    normal, inv = normalise(pre)
    norm_ref[...] = normal
    inv_ref[...] = jnp.broadcast_to(inv, inv_ref.shape)
    first = normal * vec_ref[1:2, :] + vec_ref[2:3, :]
    low_ref[...] = first.astype(BF16)

    @pl.when(pl.program_id(0) == 0)
    def _():
        lsum_ref[...] = jnp.zeros_like(lsum_ref)

    lsum_ref[0:1, :] += jnp.sum(first, axis=0, keepdims=True)


def gelu_pair(u):
    cdf = 0.5 * lax.erf(u * (1.0 / math.sqrt(2.0))) + 0.5
    density = jnp.exp2(u * u * (-0.5 * LOG2E)) * (1.0 / math.sqrt(2.0 * math.pi))
    return u * cdf, cdf + u * density


def join(ins, outs, wi, wo, bias, units):
    for i in range(2):
        part = slice(i * units, (i + 1) * units)
        wi[part, :] = ins[i][0:units, :]
        wo[part, :] = outs[i][...]
        if bias is not None:
            bias[:, part] = ins[i][units : units + 8, 0:units].astype(F32)


def feed_forward(low, groups, hid_ref, slope_ref, hsum_ref, wi, wo, bias, units):
    @pl.when(pl.program_id(0) == 0)
    def _():
        for g, (ins, outs) in enumerate(groups):
            join(ins, outs, wi.at[g], wo.at[g], bias.at[g], units)
        hsum_ref[...] = jnp.zeros_like(hsum_ref)

    out = None
    for g in range(len(groups)):
        pre = mm_nt(low, wi[g]) + bias[g, 0:1, :]
        hidden, slope = gelu_pair(pre)
        cols = slice(2 * units * g, 2 * units * (g + 1))
        hsum_ref[0:1, cols] += jnp.sum(hidden, axis=0, keepdims=True)
        hidden = hidden.astype(BF16)
        hid_ref[:, cols] = hidden
        slope_ref[:, cols] = slope.astype(BF16)
        part = mm(hidden, wo[g])
        out = part if out is None else out + part
    return out


def ffn_near_kernel(
    low_ref, i0, o0, i1, o1, i2, o2, i3, o3, hid_ref, slope_ref, hsum_ref, out_ref, wi, wo, bias, *, units
):
    groups = (((i0, i1), (o0, o1)), ((i2, i3), (o2, o3)))
    out_ref[...] = feed_forward(
        low_ref[...], groups, hid_ref, slope_ref, hsum_ref, wi, wo, bias, units
    )


def ffn_far_kernel(
    len_ref, low_ref, i0, o0, i1, o1, i2, o2, i3, o3, prev_ref, norm_ref, vec_ref,
    hid_ref, slope_ref, hsum_ref, out_ref, norm2_ref, inv2_ref, pool_ref, wi, wo, bias, *, units, blocks
):
    step = pl.program_id(0)
    sent, block = step // blocks, step % blocks
    groups = (((i0, i1), (o0, o1)), ((i2, i3), (o2, o3)))
    ffn = feed_forward(low_ref[...], groups, hid_ref, slope_ref, hsum_ref, wi, wo, bias, units)
    first = norm_ref[...] * vec_ref[1:2, :] + vec_ref[2:3, :]
    normal, inv = normalise(ffn + prev_ref[...] + vec_ref[3:4, :] + first)
    norm2_ref[...] = normal
    inv2_ref[...] = jnp.broadcast_to(inv, inv2_ref.shape)
    second = normal * vec_ref[4:5, :] + vec_ref[5:6, :]
    out_ref[...] = second.astype(BF16)
    rows = low_ref.shape[0]
    position = block * rows + lax.broadcasted_iota(jnp.int32, (rows, 1), 0)
    part = jnp.sum(jnp.where(position < len_ref[sent], second, 0.0), axis=0, keepdims=True)

    @pl.when(step == 0)
    def _():
        pool_ref[...] = jnp.zeros_like(pool_ref)

    pool_ref[pl.ds(sent, 1), :] += part / len_ref[sent].astype(F32)


def loss_kernel(
    len_ref, bits_ref, unit_ref, pool_ref, member_ref, norm_ref, inv_ref, vec_ref,
    dpre_ref, dlow_ref, sums_ref, loss_ref, grad_scr, *, micro
):
    step = pl.program_id(0)

    @pl.when(step == 0)
    def _():
        high = lax.Precision.HIGHEST
        units = unit_ref[...]
        count = units.shape[0]
        sents = count // micro
        me = bits_ref[1]
        row = lax.broadcasted_iota(jnp.int32, (count, count), 0)
        col = lax.broadcasted_iota(jnp.int32, (count, count), 1)
        source = jnp.where(col // sents == row % micro, col % sents, -1)
        pick = (source == jnp.bitwise_xor(me, row // micro)).astype(F32)
        member = dot(pick, member_ref[...].astype(F32), 1, 0)
        same = dot(member, member, 1, 1)
        own = row == col
        apart = own | (row % micro != col % micro)
        positive = jnp.where(apart, 0.0, same)
        logits = COS_SCALE * dot(units, units, 1, 1, high)
        others = jnp.where(apart, NEG, logits)
        top = jnp.max(others, axis=1, keepdims=True)
        raised = jnp.exp(others - top)
        total = jnp.sum(raised, axis=1, keepdims=True)
        chosen = raised * positive
        total_pos = jnp.sum(chosen, axis=1, keepdims=True)
        each = jnp.log(total) - jnp.log(total_pos)
        loss_ref[...] = jnp.broadcast_to(jnp.sum(each[0:micro], axis=0, keepdims=True), loss_ref.shape)
        dlogits = raised / total - chosen / total_pos
        both = dlogits[0:micro, :] + dlogits.T[0:micro, :]
        dunits = COS_SCALE * dot(both, units, 1, 0, high)
        pooled = pool_ref[0:micro, :]
        rscale = lax.rsqrt(jnp.sum(pooled * pooled, axis=1, keepdims=True) + EPS_UNIT)
        unit = pooled * rscale
        grad_scr[0:micro, :] = rscale * (dunits - unit * jnp.sum(unit * dunits, axis=1, keepdims=True))
        sums_ref[...] = jnp.zeros_like(sums_ref)

    length = len_ref[step]
    spread = grad_scr[pl.ds(step, 1), :] * (1.0 / length.astype(F32))
    normal = norm_ref[...]
    g = spread * vec_ref[4:5, :]
    valid = lax.broadcasted_iota(jnp.int32, (SEQ, 1), 0) < length
    along = jnp.mean(g * normal, axis=1, keepdims=True)
    dpre = jnp.where(valid, inv_ref[:, 0:1] * (g - jnp.mean(g) - normal * along), 0.0)
    dpre_ref[...] = dpre
    dlow_ref[...] = dpre.astype(BF16)
    sums_ref[0:1, :] += jnp.sum(dpre, axis=0, keepdims=True)
    sums_ref[1:2, :] += spread * jnp.sum(jnp.where(valid, normal, 0.0), axis=0, keepdims=True)
    sums_ref[2:3, :] += spread * length.astype(F32)


def ffn_back(dlow, low, hid_ref, slope_ref, ins, outs, wi, wo, acc, gb_ref, units):
    @pl.when(pl.program_id(0) == 0)
    def _():
        join(ins, outs, wi, wo, None, units)
        acc[...] = jnp.zeros_like(acc)
        gb_ref[...] = jnp.zeros_like(gb_ref)

    di = mm_nt(dlow, wo[...]) * slope_ref[...].astype(F32)
    gb_ref[0:1, :] += jnp.sum(di, axis=0, keepdims=True)
    dil = di.astype(BF16)
    acc[1] += mm_tn(hid_ref[...], dlow)
    acc[0] += mm_tn(dil, low)
    return mm(dil, wi[...])


def centre_ffn(g_ref, acc, gb_ref, mean_ref, bsum, units, rows):
    for i, r in enumerate(rows):
        part = slice(i * units, (i + 1) * units)
        g_ref[i, 0:units, :] = (acc[0, part, :] - column(gb_ref[0:1, part]) * mean_ref[1:2, :]).astype(BF16)
        centre = column(mean_ref[r[0] : r[0] + 1, r[1] : r[1] + units])
        g_ref[i, units : 2 * units, :] = (acc[1, part, :] - centre * bsum).astype(BF16)


def ffn_back_kernel(
    dlow_ref, low_ref, hid_ref, slope_ref, i0, o0, i1, o1, prev_ref, mean_ref, bsum_ref,
    g_ref, gb_ref, sum_ref, wi, wo, acc, *, units, rows
):
    sum_ref[...] = prev_ref[...] + ffn_back(
        dlow_ref[...], low_ref[...], hid_ref, slope_ref, (i0, i1), (o0, o1), wi, wo, acc, gb_ref, units
    )

    @pl.when(pl.program_id(0) == pl.num_programs(0) - 1)
    def _():
        centre_ffn(g_ref, acc, gb_ref, mean_ref, bsum_ref[0:1, :], units, rows)


def ffn_back_last_kernel(
    dlow_ref, low_ref, hid_ref, slope_ref, i0, o0, i1, o1, prev_ref, mean_ref, bsum_ref,
    norm_ref, inv_ref, vec_ref,
    g_ref, gb_ref, dpre_ref, dattn_ref, sums_ref, wi, wo, acc, *, units, rows
):
    @pl.when(pl.program_id(0) == 0)
    def _():
        sums_ref[...] = jnp.zeros_like(sums_ref)

    dfirst = prev_ref[...] + ffn_back(
        dlow_ref[...], low_ref[...], hid_ref, slope_ref, (i0, i1), (o0, o1), wi, wo, acc, gb_ref, units
    )
    normal = norm_ref[...]
    g = dfirst * vec_ref[1:2, :]
    along = jnp.mean(g * normal, axis=1, keepdims=True)
    dpre = inv_ref[:, 0:1] * (g - jnp.mean(g, axis=1, keepdims=True) - normal * along)
    dpre_ref[...] = dpre
    dattn_ref[...] = dpre.astype(BF16)
    sums_ref[0:1, :] += jnp.sum(dpre, axis=0, keepdims=True)
    sums_ref[1:2, :] += jnp.sum(dfirst * normal, axis=0, keepdims=True)
    sums_ref[2:3, :] += jnp.sum(dfirst, axis=0, keepdims=True)

    @pl.when(pl.program_id(0) == pl.num_programs(0) - 1)
    def _():
        centre_ffn(g_ref, acc, gb_ref, mean_ref, bsum_ref[0:1, :], units, rows)


def attend_back_kernel(
    len_ref, x_ref, dattn_ref, w0, w1, qkv_ref, ctx_ref, lse_ref, prev_ref, mean_ref, bsum_ref,
    g_ref, gb_ref, dx_ref, acc, grad_scr, w_scr, *, per, rows
):
    step = pl.program_id(0)
    n = per * HEAD

    @pl.when(step == 0)
    def _():
        acc[...] = jnp.zeros_like(acc)
        gb_ref[...] = jnp.zeros_like(gb_ref)
        for r, w in enumerate((w0, w1)):
            w_scr[3 * n * r : 3 * n * (r + 1), :] = w[0 : 3 * n, :]
            w_scr[6 * n + n * r : 6 * n + n * (r + 1), :] = w[3 * n : 4 * n, :]

    inv_root = 1.0 / math.sqrt(HEAD)
    scale = LOG2E * inv_root
    keys = key_rows(len_ref[step], 3)
    row = lax.broadcasted_iota(jnp.int32, (PAD, SEQ), 0)
    ones = jnp.where((row >= 1) & (row <= 3), 1.0, 0.0).astype(BF16)
    x = x_ref[...]
    dattn = dattn_ref[...]
    dctx = mm_nt(w_scr[6 * n : 8 * n, :], dattn).astype(BF16)
    acc[6 * n : 8 * n, :] += mm(ctx_ref[...], dattn)
    for r in range(2):
        for h in range(per):
            a = 3 * n * r + h * HEAD
            b = n * r + h * HEAD
            q = qkv_ref[a : a + HEAD, :]
            k = qkv_ref[n + a : n + a + HEAD, :]
            v = qkv_ref[2 * n + a : 2 * n + a + HEAD, :]
            do = dctx[b : b + HEAD, :]
            o = ctx_ref[b : b + HEAD, :]
            lse = lse_ref[r * per + h : r * per + h + 1, :]
            weighted = jnp.sum(o.astype(F32) * do.astype(F32), axis=0, keepdims=True)
            s = mm_tn(stack(k, keys), stack(q, split_rows(1.0, -lse)))
            p = jnp.exp2(s * scale)
            dp = mm_tn(stack(v, ones), stack(do, split_rows(0.0, -weighted)))
            ds = (p * dp).astype(BF16)
            grad_scr[2 * n + a : 2 * n + a + HEAD, :] = mm_nt(p.astype(BF16), do).T.astype(BF16)
            grad_scr[n + a : n + a + HEAD, :] = (mm_nt(ds, q) * inv_root).T.astype(BF16)
            grad_scr[a : a + HEAD, :] = (mm(k, ds) * inv_root).astype(BF16)
    grads = grad_scr[...]
    gb_ref[...] += jnp.sum(grads.astype(F32), axis=1, keepdims=True)
    acc[0 : 6 * n, :] += mm(grads, x)
    dx_ref[...] = prev_ref[...] + mm_tn(grads, w_scr[0 : 6 * n, :])

    @pl.when(step == pl.num_programs(0) - 1)
    def _():
        for r, place in enumerate(rows):
            part = slice(3 * n * r, 3 * n * (r + 1))
            g_ref[r, 0 : 3 * n, :] = (acc[part, :] - gb_ref[part, :] * mean_ref[0:1, :]).astype(BF16)
            centre = column(mean_ref[place[0] : place[0] + 1, place[1] : place[1] + n])
            base = 6 * n + n * r
            g_ref[r, 3 * n : 4 * n, :] = (
                acc[base : base + n, :] - centre * bsum_ref[0:1, :]
            ).astype(BF16)


def fence(*values):
    return lax.optimization_barrier(values)


def shards(
    inputs, lengths, membership, w_query, b_query, w_key, w_value, b_value, w_output, b_output,
    gain_first, bias_first, w_inner, b_inner, w_outer, b_outer, gain_second, bias_second,
):
    total = lax.axis_size("dp") * lax.axis_size("mp")
    mp = lax.axis_index("mp")
    dp = lax.axis_index("dp")
    me = dp * lax.axis_size("mp") + mp
    xbit = dp % 2

    def flip(value, mask):
        return lax.ppermute(value, ("dp", "mp"), [(i, i ^ mask) for i in range(total)])

    def ordered(a, b, axis=0):
        return jnp.where(xbit == 0, jnp.concatenate([a, b], axis), jnp.concatenate([b, a], axis))

    micro, own, width = inputs.shape
    rows = micro * own
    n = w_query.shape[1]
    per = n // HEAD
    units = w_inner.shape[1] // 2
    att_rows = 4 * n + 32
    in_size = units + PAD

    bits = jnp.stack([xbit, me]).astype(jnp.int32)
    sent_lengths = lax.dynamic_slice_in_dim(lengths, mp, 1, 1).reshape(-1)
    x = inputs.reshape(rows, width)
    vectors = jnp.stack(
        [b_output, gain_first, bias_first, b_outer, gain_second, bias_second, b_outer, b_outer]
    ).astype(F32)

    row_block = lambda r, c: ((r, c), lambda s, *_: (s, 0))
    sent_block = lambda a: ((None, a, SEQ), lambda s, *_: (s, 0, 0))
    piece = lambda r, p: ((r, width), lambda s, *_: (p, 0))

    att_own, att_send = call(
        pack_att_kernel, (1,), [None] * 6,
        [((att_rows, width), BF16), ((att_rows // 2, width), BF16)],
        prefetch=1, name="pack_att", us=2,
    )(bits, w_query.T, w_key.T, w_value.T, w_output, b_query[None], b_value[None])
    att_y = flip(att_send, YBIT)
    att_sib = flip(att_own, CORE)
    in_own, out_own, in_send, out_send = call(
        pack_ffn_kernel, (1,), [None] * 3,
        [
            ((2 * in_size, width), BF16), ((2 * units, width), BF16),
            ((in_size, width), BF16), ((units, width), BF16),
        ],
        prefetch=1, name="pack_ffn", us=4,
    )(bits, w_inner, b_inner[None], w_outer)
    att_sib, in_own, out_own, in_send, out_send, x_a = fence(
        att_sib, in_own, out_own, in_send, out_send, x
    )

    attn_outs = [
        ((micro, 6 * n, SEQ), BF16, *sent_block(6 * n)),
        ((micro, 2 * n, SEQ), BF16, *sent_block(2 * n)),
        ((micro, 2 * per, SEQ), F32, *sent_block(2 * per)),
        ((8, 2 * n), F32),
    ]
    qkv_a, ctx_a, lse_a, csum_a, attn_a, xsum = call(
        functools.partial(attend_near_kernel, per=per), (micro,),
        [row_block(SEQ, width), None, None],
        attn_outs + [((rows, width), F32, *row_block(SEQ, width)), ((8, width), F32)],
        scratch=[pltpu.VMEM((2 * n, width), BF16)],
        prefetch=1, name="attend_near",
    )(sent_lengths, x_a, att_own, att_sib)

    att_y, attn_a, in_send, out_send = fence(att_y, attn_a, in_send, out_send)
    att_x = flip(att_y, XBIT)
    in_y = flip(in_send, YBIT)
    in_sib = flip(in_own, CORE)
    out_sib = flip(out_own, CORE)
    att_far = ordered(att_y, att_x)
    att_far_sib = flip(att_far, CORE)
    att_far, att_far_sib, attn_a, in_y, out_send, in_sib, out_sib = fence(
        att_far, att_far_sib, attn_a, in_y, out_send, in_sib, out_sib
    )
    in_x = flip(in_y, XBIT)
    out_y = flip(out_send, YBIT)
    qkv_b, ctx_b, lse_b, csum_b, norm1, inv1, low, lsum = call(
        functools.partial(attend_far_kernel, per=per), (micro,),
        [row_block(SEQ, width), None, None, row_block(SEQ, width), None],
        attn_outs + [
            ((rows, width), F32, *row_block(SEQ, width)),
            ((rows, 128), F32, *row_block(SEQ, 128)),
            ((rows, width), BF16, *row_block(SEQ, width)),
            ((8, width), F32),
        ],
        scratch=[pltpu.VMEM((2 * n, width), BF16)],
        prefetch=1, name="attend_far",
    )(sent_lengths, x, att_far, att_far_sib, attn_a, vectors)
    low, in_x, out_y, in_y = fence(low, in_x, out_y, in_y)

    out_x = flip(out_y, XBIT)
    in_y_sib = flip(in_y, CORE)
    out_y_sib = flip(out_y, CORE)
    in_x_sib = flip(in_x, CORE)
    block = 256
    steps = rows // block
    ffn_outs = [
        ((rows, 4 * units), BF16, *row_block(block, 4 * units)),
        ((rows, 4 * units), BF16, *row_block(block, 4 * units)),
        ((8, 4 * units), F32),
    ]
    ffn_scratch = [
        pltpu.VMEM((2, 2 * units, width), BF16),
        pltpu.VMEM((2, 2 * units, width), BF16),
        pltpu.VMEM((2, 8, 2 * units), F32),
    ]
    near_specs = []
    near = []
    for p in range(2):
        near_specs += [piece(in_size, p), piece(units, p)] * 2
        near += [in_own, out_own, in_sib, out_sib]
    hid_near, slope_near, hsum_near, ffn_a = call(
        functools.partial(ffn_near_kernel, units=units), (steps,),
        [row_block(block, width)] + near_specs,
        ffn_outs + [((rows, width), F32, *row_block(block, width))],
        scratch=ffn_scratch, name="ffn_near",
    )(low, *near)
    out_x, in_y_sib, out_y_sib, in_x_sib, ffn_a = fence(out_x, in_y_sib, out_y_sib, in_x_sib, ffn_a)
    out_x_sib = flip(out_x, CORE)

    far = [in_y, out_y, in_y_sib, out_y_sib, in_x, out_x, in_x_sib, out_x_sib]
    hid_far, slope_far, hsum_far, out_rows, norm2, inv2, pooled = call(
        functools.partial(ffn_far_kernel, units=units, blocks=SEQ // block), (steps,),
        [row_block(block, width)] + [None] * 8
        + [row_block(block, width), row_block(block, width), None],
        ffn_outs + [
            ((rows, width), BF16, *row_block(block, width)),
            ((rows, width), F32, *row_block(block, width)),
            ((rows, 128), F32, *row_block(block, 128)),
            ((8, width), F32),
        ],
        scratch=ffn_scratch, prefetch=1, name="ffn_far",
    )(sent_lengths, low, *far, ffn_a, norm1, vectors)

    pool = pooled[0:micro]
    unit = pool * lax.rsqrt(jnp.sum(pool * pool, axis=1, keepdims=True) + EPS_UNIT)
    share = 1.0 / (rows * total)
    by_quarter = lambda v: v.reshape(2, 2, units).transpose(1, 0, 2).reshape(2, 2 * units)
    means = share * jnp.concatenate(
        [
            xsum[0:1],
            lsum[0:1],
            jnp.concatenate([csum_a[0:1], csum_b[0:1]], axis=1),
            by_quarter(hsum_near[0]),
            by_quarter(hsum_far[0]),
            jnp.zeros((1, width), F32),
        ]
    )

    def swap_slots(v, mask, pieces):
        if mask == CORE:
            return v.reshape(2, 2, -1)[:, ::-1].reshape(v.shape)
        if mask == YBIT:
            return v.reshape(2, 2, -1)[::-1].reshape(v.shape)
        if mask == XBIT and pieces:
            return v.reshape(4, 2, -1)[:, ::-1].reshape(v.shape)
        return v

    def other_means(v, mask):
        return jnp.concatenate(
            [
                v[0:2],
                swap_slots(v[2].reshape(4, n), mask, False).reshape(1, width),
                swap_slots(v[3:7], mask, True),
                v[7:8],
            ]
        )

    bundle = jnp.concatenate([means, unit], axis=0)
    mask = 1
    while mask < total:
        other = flip(bundle, mask)
        bundle = jnp.concatenate(
            [bundle[0:8] + other_means(other[0:8], mask), bundle[8:], other[8:]], axis=0
        )
        mask *= 2
    means = bundle[0:8]
    every_unit = bundle[8:]

    dpre2, dlow, sums2, loss = call(
        functools.partial(loss_kernel, micro=micro), (micro,),
        [None, None, None, row_block(SEQ, width), row_block(SEQ, 128), None],
        [
            ((rows, width), F32, *row_block(SEQ, width)),
            ((rows, width), BF16, *row_block(SEQ, width)),
            ((8, width), F32),
            ((8, 128), F32),
        ],
        scratch=[pltpu.VMEM((8, width), F32)], prefetch=2, name="loss",
    )(sent_lengths, bits, every_unit, pooled, membership.reshape(-1, membership.shape[2]), norm2, inv2, vectors)

    back_rows = SEQ

    def ffn_part(half, p, prev, last=False):
        hidden, slope, arrays, specs, base = half
        part = lambda s, *_: (s, p)
        block_of = lambda c: row_block(back_rows, c)
        ins = [block_of(width), block_of(width)] + [((back_rows, 2 * units), part)] * 2
        ins += specs + [block_of(width), None, None]
        places = ((base, p * units), (base + 1, p * units))
        outs = [((2, 2 * units, width), BF16), ((8, 2 * units), F32)]
        args = [dlow, low, hidden, slope, *arrays, prev, means, sums2]
        if last:
            ins += [block_of(width), block_of(128), None]
            args += [norm1, inv1, vectors]
            outs += [
                ((rows, width), F32, *block_of(width)),
                ((rows, width), BF16, *block_of(width)),
                ((8, width), F32),
            ]
        else:
            outs += [((rows, width), F32, *block_of(width))]
        return call(
            functools.partial(
                ffn_back_last_kernel if last else ffn_back_kernel, units=units, rows=places
            ),
            (rows // back_rows,), ins, outs,
            scratch=[
                pltpu.VMEM((2 * units, width), BF16), pltpu.VMEM((2 * units, width), BF16),
                pltpu.VMEM((2, 2 * units, width), F32),
            ],
            name="ffn_back",
        )(*args)

    near_half = lambda p: (
        hid_near, slope_near, near[0:4], [piece(in_size, p), piece(units, p)] * 2, 3
    )
    far_half = lambda p: (hid_far, slope_far, far[4 * p : 4 * p + 4], [None] * 4, 5)

    def add(*values):
        out = values[0].astype(F32)
        for v in values[1:]:
            out = out + v.astype(F32)
        return out.astype(BF16)

    def rest_split(a, mask):
        half = a.shape[0] // 2
        bit = (me // mask) % 2
        if 2 * mask < total:
            bit = (bit + (me // (2 * mask)) % 2) % 2
        keep = lax.dynamic_slice_in_dim(a, bit * half, half, 0)
        send = lax.dynamic_slice_in_dim(a, (1 - bit) * half, half, 0)
        return bit, keep, send

    def rest_finish(bit, part, mask):
        inner = mask * 2
        while inner < total:
            part = add(part, flip(part, inner | mask if inner == 2 * mask else inner))
            inner *= 2
        other = flip(part, mask)
        return jnp.where(
            bit == 0, jnp.concatenate([part, other], 0), jnp.concatenate([other, part], 0)
        )

    rest = 2 * XBIT
    top, bottom = slice(0, units), slice(units, 2 * units)
    g_f1, gb_f1, acc = ffn_part(far_half(1), 1, dpre2)
    f1 = add(g_f1[0], flip(g_f1[1], CORE))
    f1a, f1b, acc = fence(f1[top], f1[bottom], acc)

    y1a = flip(f1a, YBIT)
    g_f0, gb_f0, acc = ffn_part(far_half(0), 0, acc)
    y1a, g_f0, acc, f1b = fence(y1a, g_f0, acc, f1b)

    y1b = flip(f1b, YBIT)
    c_f0 = flip(g_f0[1], CORE)
    g_n1, gb_n1, acc = ffn_part(near_half(1), 1, acc)
    f0 = add(g_f0[0], c_f0)
    y1b, f0a, f0b, g_n1, acc = fence(y1b, f0[top], f0[bottom], g_n1, acc)

    y0a = flip(f0a, YBIT)
    c_n1 = flip(g_n1[1], CORE)
    g_n0, gb_n0, dpre1, dattn, sums1 = ffn_part(near_half(0), 0, acc, True)
    s1a = add(g_n1[0][top], c_n1[top], y1a)
    s1b = add(g_n1[0][bottom], c_n1[bottom], y1b)
    y0a, s1a, s1b, g_n0, dattn, f0b = fence(y0a, s1a, s1b, g_n0, dattn, f0b)

    def attend_part(w, qkv, ctx, lse, prev, places):
        return call(
            functools.partial(attend_back_kernel, per=per, rows=places), (micro,),
            [
                row_block(SEQ, width), row_block(SEQ, width), None, None, sent_block(6 * n),
                sent_block(2 * n), sent_block(2 * per), row_block(SEQ, width), None, None,
            ],
            [
                ((2, 4 * n, width), BF16), ((6 * n, 1), F32),
                ((rows, width), F32, *row_block(SEQ, width)),
            ],
            scratch=[
                pltpu.VMEM((8 * n, width), F32), pltpu.VMEM((6 * n, SEQ), BF16),
                pltpu.VMEM((8 * n, width), BF16),
            ],
            prefetch=1, name="attend_back",
        )(sent_lengths, x, dattn, *w, qkv, ctx, lse, prev, means, sums1)

    y0b = flip(f0b, YBIT)
    x1a = flip(s1a, XBIT)
    c_n0 = flip(g_n0[1], CORE)
    g_af, gb_af, dx = attend_part(
        (att_far, att_far_sib), qkv_b, ctx_b, lse_b, dpre1, ((2, 2 * n), (2, 3 * n))
    )
    y0b, x1a, c_n0, g_af, dx, s1b = fence(y0b, x1a, c_n0, g_af, dx, s1b)

    af = add(g_af[0], flip(g_af[1], CORE))
    ra = add(g_n0[0][top], c_n0[top], y0a, x1a)
    bit_a, keep_a, send_a = rest_split(ra, rest)
    af_a, af_b, keep_a, send_a, dx, s1b = fence(af[top], af[bottom], keep_a, send_a, dx, s1b)

    y_afa = flip(af_a, YBIT)
    x1b = flip(s1b, XBIT)
    z_a = flip(send_a, rest)
    g_an, gb_an, dx = attend_part((att_own, att_sib), qkv_a, ctx_a, lse_a, dx, ((2, 0), (2, n)))
    y_afa, x1b, z_a, g_an, dx, af_b = fence(y_afa, x1b, z_a, g_an, dx, af_b)

    y_afb = flip(af_b, YBIT)
    c_an = flip(g_an[1], CORE)
    rb = add(g_n0[0][bottom], c_n0[bottom], y0b, x1b)
    bit_b, keep_b, send_b = rest_split(rb, rest)
    z_b = flip(send_b, rest)
    r_in = rest_finish(bit_a, add(keep_a, z_a), rest)
    r_out = rest_finish(bit_b, add(keep_b, z_b), rest)
    r_in_x = flip(r_in, XBIT)
    r_out_x = flip(r_out, XBIT)

    def att_sum(s):
        cut = s.shape[0] // 2
        keep = lax.dynamic_slice_in_dim(s, xbit * cut, cut, 0)
        send = lax.dynamic_slice_in_dim(s, (1 - xbit) * cut, cut, 0)
        mine = add(keep, flip(send, XBIT))
        bit, keep, send = rest_split(mine, rest)
        mine = rest_finish(bit, add(keep, flip(send, rest)), rest)
        return ordered(mine, flip(mine, XBIT))

    g_att_a = att_sum(add(g_an[0][top], c_an[top], y_afa))
    g_att_b = att_sum(add(g_an[0][bottom], c_an[bottom], y_afb))
    g_att = jnp.concatenate([g_att_a, g_att_b], axis=0).astype(F32)
    g_in = ordered(r_in, r_in_x).astype(F32)
    g_out = ordered(r_out, r_out_x).astype(F32)
    grad_inputs = dx.reshape(micro, own, width)

    gb_att = jnp.concatenate([gb_an, gb_af]).reshape(4, 3 * n)
    side = lambda a, b: jnp.concatenate([a[0].reshape(2, units), b[0].reshape(2, units)], axis=1)
    gb_ffn = jnp.concatenate([side(gb_n0, gb_n1), side(gb_f0, gb_f1)])
    att_len, ffn_len = gb_att.size, gb_ffn.size
    base = jnp.concatenate([sums1[0:3].reshape(-1), sums2[0:3].reshape(-1), loss[0, 0:128]])
    small = jnp.concatenate([base, gb_att.reshape(-1), gb_ffn.reshape(-1)]).reshape(-1, 128)

    def other_small(v, mask):
        v = v.reshape(-1)
        b = base.size
        return jnp.concatenate(
            [
                v[:b],
                swap_slots(v[b : b + att_len].reshape(4, 3 * n), mask, False).reshape(-1),
                swap_slots(v[b + att_len :].reshape(4, 2 * units), mask, True).reshape(-1),
            ]
        ).reshape(-1, 128)

    mask = 1
    while mask < total:
        small = small + other_small(flip(small, mask), mask)
        mask *= 2
    small = small.reshape(-1)
    shared = small[: 6 * width].reshape(6, width)
    b_att = small[base.size : base.size + 3 * n]
    b_ffn = small[base.size + att_len : base.size + att_len + 2 * units]
    grad_binner = ordered(b_ffn[:units], b_ffn[units:])
    hidden_mean = ordered(means[3, :units], means[3, units:])

    g_qkv = g_att[: 3 * n] + b_att[:, None] * means[0][None]
    grad_wout = g_att[3 * n :] + means[2, :n][:, None] * shared[0][None]
    grad_inner = (g_in + grad_binner[:, None] * means[1][None]).T
    grad_outer = g_out + hidden_mean[:, None] * shared[3][None]

    return (
        out_rows.reshape(micro, own, width),
        small[6 * width],
        grad_inputs,
        g_qkv[:n].T,
        b_att[:n],
        g_qkv[n : 2 * n].T,
        g_qkv[2 * n :].T,
        b_att[2 * n :],
        grad_wout,
        shared[0],
        shared[1],
        shared[2],
        grad_inner,
        grad_binner,
        grad_outer,
        shared[3],
        shared[4],
        shared[5],
    )


def solution(mesh):
    rows = P(None, ("dp", "mp"), None)
    cols = P(None, "mp")
    split = P("mp")
    whole = P()
    placed = (rows, P(None, "dp"), whole, cols, split, cols, cols, split, P("mp", None))
    placed += (whole, whole, whole, cols, split, P("mp", None), whole, whole, whole)
    results = (rows, whole, rows, cols, split, cols, cols, split, P("mp", None))
    results += (whole, whole, whole, cols, split, P("mp", None), whole, whole, whole)
    return jax.shard_map(shards, mesh=mesh, in_specs=placed, out_specs=results, check_vma=False)
```

```python
import functools
import math

import jax
import jax.numpy as jnp
from jax import lax
from jax.experimental import pallas as pl
from jax.experimental.pallas import tpu as pltpu
from jax.sharding import PartitionSpec as P

HEAD = 64
SEQ = 512
EPS_NORM = 1e-5
EPS_UNIT = 1e-6
COS_SCALE = 20.0
LOG2E = 1.4426950408889634
NEG = -1e30
F32 = jnp.float32
BF16 = jnp.bfloat16
CORE, YBIT, XBIT = 1, 2, 4
PAD = 16


def dot(a, b, ca, cb, precision=None):
    return lax.dot_general(
        a, b, (((ca,), (cb,)), ((), ())), preferred_element_type=F32, precision=precision
    )


def mm(a, b):
    return dot(a, b, 1, 0)


def mm_nt(a, b):
    return dot(a, b, 1, 1)


def mm_tn(a, b):
    return dot(a, b, 0, 0)


def column(row):
    return jnp.broadcast_to(row, (8, row.shape[1])).T[:, :1]


def call(kernel, grid, ins, outs, scratch=(), prefetch=0, name=None, us=7, mib=44, keep=(), held=()):
    def spec(block, index):
        return pl.BlockSpec(block, index)

    def whole(a, **mode):
        rank = len(a)
        return pl.BlockSpec(tuple(a), lambda *_: (0,) * rank, **mode)

    def run(*args):
        in_specs, placed = [], list(args[:prefetch])
        for i, (item, arg) in enumerate(zip(ins, args[prefetch:])):
            big = arg.size > 1 << 16
            single = {"pipeline_mode": pl.Buffered(1)} if big else {}
            in_specs.append(whole(arg.shape, **single) if item is None else spec(*item))
            placed.append(
                pltpu.with_memory_space_constraint(arg, pltpu.HBM) if big and i not in held else arg
            )
        out_specs = [whole(o[0]) if len(o) == 2 else spec(*o[2:]) for o in outs]
        shapes = []
        for i, o in enumerate(outs):
            if i in keep:
                shapes.append(pltpu.VMEM(o[0], o[1]))
            elif math.prod(o[0]) > 1 << 16:
                shapes.append(pltpu.HBM(o[0], o[1]))
            else:
                shapes.append(jax.ShapeDtypeStruct(o[0], o[1]))
        return pl.pallas_call(
            kernel,
            out_shape=shapes,
            grid_spec=pltpu.PrefetchScalarGridSpec(
                num_scalar_prefetch=prefetch,
                grid=grid,
                in_specs=in_specs,
                out_specs=out_specs,
                scratch_shapes=list(scratch),
            ),
            compiler_params=pltpu.CompilerParams(vmem_limit_bytes=mib << 20),
            cost_estimate=pl.CostEstimate(flops=int(us * 1.1e9), transcendentals=0, bytes_accessed=1000),
            name=name,
        )(*placed)

    return run


def pack_att_kernel(bits_ref, wq, wk, wv, wo, bq, bv, att_ref, send_ref):
    n = wo.shape[0]
    att_ref[0:n, :] = wq[...]
    att_ref[n : 2 * n, :] = wk[...]
    att_ref[2 * n : 3 * n, :] = wv[...]
    att_ref[3 * n : 4 * n, :] = wo[...]
    rows = att_ref.shape[0] - 4 * n
    att_ref[4 * n :, :] = jnp.zeros_like(att_ref[4 * n :, :])
    att_ref[4 * n :, 0:n] = jnp.broadcast_to(bq[...], (rows, n))
    att_ref[4 * n :, 2 * n : 3 * n] = jnp.broadcast_to(bv[...], (rows, n))
    half = att_ref.shape[0] // 2
    send_ref[...] = att_ref[pl.ds(pl.multiple_of(bits_ref[0] * half, 16), half), :]


def pack_ffn_kernel(bits_ref, win, bin_, wout, in_ref, out_ref, in_send, out_send):
    x = bits_ref[0]
    units = win.shape[1] // 2
    size = units + PAD
    for piece in range(2):
        take = pl.multiple_of((x if piece == 0 else 1 - x) * units, 128)
        base = piece * size
        in_ref[base : base + units, :] = win[:, pl.ds(take, units)].T
        in_ref[base + units : base + size, :] = jnp.zeros((PAD, in_ref.shape[1]), BF16)
        in_ref[base + units : base + size, 0:units] = jnp.broadcast_to(
            bin_[:, pl.ds(take, units)], (PAD, units)
        )
        out_ref[piece * units : (piece + 1) * units, :] = wout[pl.ds(take, units), :]
    in_send[...] = in_ref[0:size, :]
    out_send[...] = out_ref[0:units, :]


def key_rows(length, ones):
    row = lax.broadcasted_iota(jnp.int32, (PAD, SEQ), 0)
    pos = lax.broadcasted_iota(jnp.int32, (PAD, SEQ), 1)
    base = jnp.where((row >= 1) & (row <= ones), 1.0, 0.0)
    return jnp.where((row == 0) & (pos >= length), NEG, base).astype(BF16)


def split_rows(first, value):
    row = lax.broadcasted_iota(jnp.int32, (PAD, SEQ), 0)
    high = value.astype(BF16).astype(F32)
    middle = (value - high).astype(BF16).astype(F32)
    lower = value - high - middle
    out = jnp.where(row == 0, first, 0.0)
    for i, part in enumerate((high, middle, lower)):
        out = jnp.where(row == i + 1, part, out)
    return out.astype(BF16)


def stack(*parts):
    return jnp.concatenate(parts, axis=0)


def attention_forward(len_ref, x_ref, packs, qkv_ref, ctx_ref, lse_ref, csum_ref, per):
    length = len_ref[pl.program_id(0)]
    scale = LOG2E / math.sqrt(HEAD)
    n = per * HEAD

    @pl.when(pl.program_id(0) == 0)
    def _():
        csum_ref[...] = jnp.zeros_like(csum_ref)

    keys = key_rows(length, 0)
    ones = jnp.ones((PAD, SEQ), BF16)
    x = x_ref[...]
    for r, w in enumerate(packs):
        bias = column(w[4 * n : 4 * n + 1, 0 : 3 * n].astype(F32))
        qkv_ref[3 * n * r : 3 * n * (r + 1), :] = (mm_nt(w[0 : 3 * n, :], x) + bias).astype(BF16)
    for r in range(len(packs)):
        for h in range(per):
            a = 3 * n * r + h * HEAD
            q = stack(qkv_ref[a : a + HEAD, :], ones)
            k = stack(qkv_ref[n + a : n + a + HEAD, :], keys)
            v = stack(qkv_ref[2 * n + a : 2 * n + a + HEAD, :], ones)
            s = mm_tn(k, q)
            top = jnp.max(s, axis=0, keepdims=True)
            e = jnp.exp2(s * scale - top * scale).astype(BF16)
            c = mm(v, e)
            total = c[HEAD : HEAD + 1, :]
            b = n * r + h * HEAD
            ctx_ref[b : b + HEAD, :] = (c[0:HEAD, :] * (1.0 / total)).astype(BF16)
            lse_ref[r * per + h : r * per + h + 1, :] = top + jnp.log2(total) * (1.0 / scale)
    csum_ref[...] += mm_nt(jnp.ones((8, SEQ), BF16), ctx_ref[...])


def attend_first_kernel(
    len_ref, x_ref, w0, qkv_ref, ctx_ref, lse_ref, csum_ref, xsum_ref, *, per
):
    attention_forward(len_ref, x_ref, (w0,), qkv_ref, ctx_ref, lse_ref, csum_ref, per)

    @pl.when(pl.program_id(0) == 0)
    def _():
        xsum_ref[...] = jnp.zeros_like(xsum_ref)

    xsum_ref[0:1, :] += jnp.sum(x_ref[...].astype(F32), axis=0, keepdims=True)


def attend_next_kernel(len_ref, x_ref, w0, qkv_ref, ctx_ref, lse_ref, csum_ref, *, per):
    attention_forward(len_ref, x_ref, (w0,), qkv_ref, ctx_ref, lse_ref, csum_ref, per)


def normalise(v):
    mean = jnp.mean(v, axis=-1, keepdims=True)
    centred = v - mean
    inv = lax.rsqrt(jnp.mean(centred * centred, axis=-1, keepdims=True) + EPS_NORM)
    return centred * inv, inv


def attend_last_kernel(
    len_ref, bits_ref, x_ref, y0, x0, y1, x1, wa, wb, ctxa_ref, ctxb_ref, vec_ref,
    qkv_ref, ctx_ref, lse_ref, csum_ref, pack_ref, norm_ref, inv_ref, low_ref, lsum_ref,
    wo_scr, all_scr, *, per
):
    n = per * HEAD

    @pl.when(pl.program_id(0) == 0)
    def _():
        half = y0.shape[0]
        near = pl.multiple_of(bits_ref[0] * half, 16)
        away = pl.multiple_of((1 - bits_ref[0]) * half, 16)
        for r, (a, b) in enumerate(((y0, x0), (y1, x1))):
            pack_ref[r, pl.ds(near, half), :] = a[...]
            pack_ref[r, pl.ds(away, half), :] = b[...]
        for r, w in enumerate((wa, wb, pack_ref.at[0], pack_ref.at[1])):
            wo_scr[r * n : (r + 1) * n, :] = w[3 * n : 4 * n, :]
        lsum_ref[...] = jnp.zeros_like(lsum_ref)

    packs = (pack_ref.at[0], pack_ref.at[1])
    attention_forward(len_ref, x_ref, packs, qkv_ref, ctx_ref, lse_ref, csum_ref, per)
    all_scr[0:n, :] = ctxa_ref[...]
    all_scr[n : 2 * n, :] = ctxb_ref[...]
    all_scr[2 * n : 4 * n, :] = ctx_ref[...]
    pre = mm_tn(all_scr[...], wo_scr[...]) + vec_ref[0:1, :] + x_ref[...].astype(F32)
    normal, inv = normalise(pre)
    norm_ref[...] = normal
    inv_ref[...] = jnp.broadcast_to(inv, inv_ref.shape)
    first = normal * vec_ref[1:2, :] + vec_ref[2:3, :]
    low_ref[...] = first.astype(BF16)
    lsum_ref[0:1, :] += jnp.sum(first, axis=0, keepdims=True)


def gelu_pair(u):
    cdf = 0.5 * lax.erf(u * (1.0 / math.sqrt(2.0))) + 0.5
    density = jnp.exp2(u * u * (-0.5 * LOG2E)) * (1.0 / math.sqrt(2.0 * math.pi))
    return u * cdf, cdf + u * density


def join(ins, outs, wi, wo, bias, units):
    for i in range(2):
        part = slice(i * units, (i + 1) * units)
        wi[part, :] = ins[i][0:units, :]
        wo[part, :] = outs[i][...]
        if bias is not None:
            bias[:, part] = ins[i][units : units + 8, 0:units].astype(F32)


def feed_forward(low, groups, hid_ref, slope_ref, hsum_ref, wi, wo, bias, units):
    @pl.when(pl.program_id(0) == 0)
    def _():
        for g, (ins, outs) in enumerate(groups):
            join(ins, outs, wi.at[g], wo.at[g], bias.at[g], units)
        hsum_ref[...] = jnp.zeros_like(hsum_ref)

    out = None
    for g in range(len(groups)):
        pre = mm_nt(low, wi[g]) + bias[g, 0:1, :]
        hidden, slope = gelu_pair(pre)
        cols = slice(2 * units * g, 2 * units * (g + 1))
        hsum_ref[0:1, cols] += jnp.sum(hidden, axis=0, keepdims=True)
        hidden = hidden.astype(BF16)
        hid_ref[:, cols] = hidden
        slope_ref[:, cols] = slope.astype(BF16)
        part = mm(hidden, wo[g])
        out = part if out is None else out + part
    return out


def ffn_near_kernel(
    low_ref, i0, o0, i1, o1, i2, o2, i3, o3, hid_ref, slope_ref, hsum_ref, out_ref, wi, wo, bias, *, units
):
    groups = (((i0, i1), (o0, o1)), ((i2, i3), (o2, o3)))
    out_ref[...] = feed_forward(
        low_ref[...], groups, hid_ref, slope_ref, hsum_ref, wi, wo, bias, units
    )


def ffn_far_kernel(
    len_ref, low_ref, i0, o0, i1, o1, i2, o2, i3, o3, prev_ref, norm_ref, vec_ref,
    hid_ref, slope_ref, hsum_ref, out_ref, norm2_ref, inv2_ref, pool_ref, wi, wo, bias, *, units, blocks
):
    step = pl.program_id(0)
    sent, block = step // blocks, step % blocks
    groups = (((i0, i1), (o0, o1)), ((i2, i3), (o2, o3)))
    ffn = feed_forward(low_ref[...], groups, hid_ref, slope_ref, hsum_ref, wi, wo, bias, units)
    first = norm_ref[...] * vec_ref[1:2, :] + vec_ref[2:3, :]
    normal, inv = normalise(ffn + prev_ref[...] + vec_ref[3:4, :] + first)
    norm2_ref[...] = normal
    inv2_ref[...] = jnp.broadcast_to(inv, inv2_ref.shape)
    second = normal * vec_ref[4:5, :] + vec_ref[5:6, :]
    out_ref[...] = second.astype(BF16)
    rows = low_ref.shape[0]
    position = block * rows + lax.broadcasted_iota(jnp.int32, (rows, 1), 0)
    part = jnp.sum(jnp.where(position < len_ref[sent], second, 0.0), axis=0, keepdims=True)

    @pl.when(step == 0)
    def _():
        pool_ref[...] = jnp.zeros_like(pool_ref)

    pool_ref[pl.ds(sent, 1), :] += part / len_ref[sent].astype(F32)


def loss_kernel(
    len_ref, bits_ref, *refs, micro, blocks
):
    unit_refs = refs[:blocks]
    (pool_ref, member_ref, norm_ref, inv_ref, vec_ref, dpre_ref, dlow_ref, sums_ref,
     grad_scr) = refs[blocks:]
    step = pl.program_id(0)

    @pl.when(step == 0)
    def _():
        high = lax.Precision.HIGHEST
        units = jnp.concatenate([ref[...] for ref in unit_refs], axis=0)
        count = units.shape[0]
        sents = count // micro
        me = bits_ref[1]
        row = lax.broadcasted_iota(jnp.int32, (count, count), 0)
        col = lax.broadcasted_iota(jnp.int32, (count, count), 1)
        source = jnp.where(col // sents == row % micro, col % sents, -1)
        pick = (source == jnp.bitwise_xor(me, row // micro)).astype(F32)
        member = dot(pick, member_ref[...].astype(F32), 1, 0)
        same = dot(member, member, 1, 1)
        own = row == col
        apart = own | (row % micro != col % micro)
        positive = jnp.where(apart, 0.0, same)
        logits = COS_SCALE * dot(units, units, 1, 1, high)
        others = jnp.where(apart, NEG, logits)
        top = jnp.max(others, axis=1, keepdims=True)
        raised = jnp.exp(others - top)
        total = jnp.sum(raised, axis=1, keepdims=True)
        chosen = raised * positive
        total_pos = jnp.sum(chosen, axis=1, keepdims=True)
        each = jnp.log(total) - jnp.log(total_pos)
        loss = jnp.sum(each[0:micro], axis=0, keepdims=True)
        dlogits = raised / total - chosen / total_pos
        both = dlogits[0:micro, :] + dlogits.T[0:micro, :]
        dunits = COS_SCALE * dot(both, units, 1, 0, high)
        pooled = pool_ref[0:micro, :]
        rscale = lax.rsqrt(jnp.sum(pooled * pooled, axis=1, keepdims=True) + EPS_UNIT)
        unit = pooled * rscale
        grad_scr[0:micro, :] = rscale * (dunits - unit * jnp.sum(unit * dunits, axis=1, keepdims=True))
        sums_ref[...] = jnp.zeros_like(sums_ref)
        sums_ref[3:4, :] = jnp.broadcast_to(loss, (1, sums_ref.shape[1]))

    length = len_ref[step]
    spread = grad_scr[pl.ds(step, 1), :] * (1.0 / length.astype(F32))
    normal = norm_ref[...]
    g = spread * vec_ref[4:5, :]
    valid = lax.broadcasted_iota(jnp.int32, (SEQ, 1), 0) < length
    along = jnp.mean(g * normal, axis=1, keepdims=True)
    dpre = jnp.where(valid, inv_ref[:, 0:1] * (g - jnp.mean(g) - normal * along), 0.0)
    dpre_ref[...] = dpre
    dlow_ref[...] = dpre.astype(BF16)
    sums_ref[0:1, :] += jnp.sum(dpre, axis=0, keepdims=True)
    sums_ref[1:2, :] += spread * jnp.sum(jnp.where(valid, normal, 0.0), axis=0, keepdims=True)
    sums_ref[2:3, :] += spread * length.astype(F32)


def ffn_back(dlow, low, hid_ref, slope_ref, outs, wo, acc, gb_ref, units):
    @pl.when(pl.program_id(0) == 0)
    def _():
        for i in range(2):
            wo[i * units : (i + 1) * units, :] = outs[i][...]
        acc[...] = jnp.zeros_like(acc)
        gb_ref[...] = jnp.zeros_like(gb_ref)

    di = mm_nt(dlow, wo[...]) * slope_ref[...].astype(F32)
    gb_ref[0:1, :] += jnp.sum(di, axis=0, keepdims=True)
    dil = di.astype(BF16)
    acc[1] += mm_tn(hid_ref[...], dlow)
    acc[0] += mm_tn(dil, low)
    return dil


def centre_ffn(keep_ref, send_ref, acc, gb_ref, mean_ref, bsum, units, rows):
    for i, (r, g_ref) in enumerate(zip(rows, (keep_ref, send_ref))):
        part = slice(i * units, (i + 1) * units)
        g_ref[0:units, :] = (acc[0, part, :] - column(gb_ref[0:1, part]) * mean_ref[1:2, :]).astype(BF16)
        centre = column(mean_ref[r[0] : r[0] + 1, r[1] : r[1] + units])
        g_ref[units : 2 * units, :] = (acc[1, part, :] - centre * bsum).astype(BF16)


def ffn_back_kernel(
    dlow_ref, low_ref, hid_ref, slope_ref, o0, o1, mean_ref, bsum_ref,
    keep_ref, send_ref, gb_ref, di_ref, wo, acc, *, units, rows
):
    di_ref[...] = ffn_back(
        dlow_ref[...], low_ref[...], hid_ref, slope_ref, (o0, o1), wo, acc, gb_ref, units
    )

    @pl.when(pl.program_id(0) == pl.num_programs(0) - 1)
    def _():
        centre_ffn(keep_ref, send_ref, acc, gb_ref, mean_ref, bsum_ref[0:1, :], units, rows)


def ffn_back_last_kernel(
    dlow_ref, low_ref, hid_ref, slope_ref, o0, o1, mean_ref, bsum_ref,
    d0, d1, d2, i0, i1, i2, i3, i4, i5, i6, i7, prev_ref, norm_ref, inv_ref, vec_ref,
    keep_ref, send_ref, gb_ref, dpre_ref, dattn_ref, sums_ref, wo, acc, wi, *, units, rows
):
    @pl.when(pl.program_id(0) == 0)
    def _():
        sums_ref[...] = jnp.zeros_like(sums_ref)
        for i, ref in enumerate((i0, i1, i2, i3, i4, i5, i6, i7)):
            wi[i * units : (i + 1) * units, :] = ref[0:units, :]

    dil = ffn_back(
        dlow_ref[...], low_ref[...], hid_ref, slope_ref, (o0, o1), wo, acc, gb_ref, units
    )
    dfirst = prev_ref[...]
    for i, part in enumerate((d0[...], d1[...], d2[...], dil)):
        dfirst = dfirst + mm(part, wi[2 * units * i : 2 * units * (i + 1), :])
    normal = norm_ref[...]
    g = dfirst * vec_ref[1:2, :]
    along = jnp.mean(g * normal, axis=1, keepdims=True)
    dpre = inv_ref[:, 0:1] * (g - jnp.mean(g, axis=1, keepdims=True) - normal * along)
    dpre_ref[...] = dpre
    dattn_ref[...] = dpre.astype(BF16)
    sums_ref[0:1, :] += jnp.sum(dpre, axis=0, keepdims=True)
    sums_ref[1:2, :] += jnp.sum(dfirst * normal, axis=0, keepdims=True)
    sums_ref[2:3, :] += jnp.sum(dfirst, axis=0, keepdims=True)

    @pl.when(pl.program_id(0) == pl.num_programs(0) - 1)
    def _():
        centre_ffn(keep_ref, send_ref, acc, gb_ref, mean_ref, bsum_ref[0:1, :], units, rows)


def attend_back_kernel(
    len_ref, x_ref, dattn_ref, w_ref, qkv_ref, ctx_ref, lse_ref, mean_ref, bsum_ref,
    g_ref, gb_ref, grad_ref, acc, *, per, base, place
):
    step = pl.program_id(0)
    n = per * HEAD

    @pl.when(step == 0)
    def _():
        acc[...] = jnp.zeros_like(acc)
        gb_ref[...] = jnp.zeros_like(gb_ref)

    inv_root = 1.0 / math.sqrt(HEAD)
    scale = LOG2E * inv_root
    keys = key_rows(len_ref[step], 3)
    row = lax.broadcasted_iota(jnp.int32, (PAD, SEQ), 0)
    ones = jnp.where((row >= 1) & (row <= 3), 1.0, 0.0).astype(BF16)
    x = x_ref[...]
    dattn = dattn_ref[...]
    dctx = mm_nt(w_ref[3 * n : 4 * n, :], dattn).astype(BF16)
    acc[3 * n : 4 * n, :] += mm(ctx_ref[base * n : (base + 1) * n, :], dattn)
    for h in range(per):
        a = 3 * n * base + h * HEAD
        b = n * base + h * HEAD
        c = h * HEAD
        q = qkv_ref[a : a + HEAD, :]
        k = qkv_ref[n + a : n + a + HEAD, :]
        v = qkv_ref[2 * n + a : 2 * n + a + HEAD, :]
        do = dctx[c : c + HEAD, :]
        o = ctx_ref[b : b + HEAD, :]
        lse = lse_ref[base * per + h : base * per + h + 1, :]
        weighted = jnp.sum(o.astype(F32) * do.astype(F32), axis=0, keepdims=True)
        s = mm_tn(stack(k, keys), stack(q, split_rows(1.0, -lse)))
        p = jnp.exp2(s * scale)
        dp = mm_tn(stack(v, ones), stack(do, split_rows(0.0, -weighted)))
        ds = (p * dp).astype(BF16)
        grad_ref[2 * n + c : 2 * n + c + HEAD, :] = mm_nt(do, p.astype(BF16)).astype(BF16)
        grad_ref[n + c : n + c + HEAD, :] = (mm_nt(q, ds) * inv_root).astype(BF16)
        grad_ref[c : c + HEAD, :] = (mm(k, ds) * inv_root).astype(BF16)
    grads = grad_ref[...]
    gb_ref[:, 0 : 3 * n] += mm_nt(jnp.ones((8, SEQ), BF16), grads)
    acc[0 : 3 * n, :] += mm(grads, x)

    @pl.when(step == pl.num_programs(0) - 1)
    def _():
        g_ref[0 : 3 * n, :] = (acc[0 : 3 * n, :] - column(gb_ref[0:1, 0 : 3 * n]) * mean_ref[0:1, :]).astype(BF16)
        centre = column(mean_ref[2:3, place * n : (place + 1) * n])
        g_ref[3 * n : 4 * n, :] = (acc[3 * n : 4 * n, :] - centre * bsum_ref[0:1, :]).astype(BF16)


def input_grad_kernel(prev_ref, g0, g1, g2, g3, w0, w1, w2, w3, out_ref):
    out = prev_ref[...]
    for g, w in ((g0, w0), (g1, w1), (g2, w2), (g3, w3)):
        out = out + mm_tn(g[...], w[0 : g.shape[0], :])
    out_ref[...] = out


def fence(*values):
    return lax.optimization_barrier(values)


def shards(
    inputs, lengths, membership, w_query, b_query, w_key, w_value, b_value, w_output, b_output,
    gain_first, bias_first, w_inner, b_inner, w_outer, b_outer, gain_second, bias_second,
):
    total = lax.axis_size("dp") * lax.axis_size("mp")
    mp = lax.axis_index("mp")
    dp = lax.axis_index("dp")
    me = dp * lax.axis_size("mp") + mp
    xbit = dp % 2

    def flip(value, mask):
        return lax.ppermute(value, ("dp", "mp"), [(i, i ^ mask) for i in range(total)])

    def flip_hbm(value, mask):
        return flip(pltpu.with_memory_space_constraint(value, pltpu.HBM), mask)

    def ordered(a, b, axis=0):
        return jnp.where(xbit == 0, jnp.concatenate([a, b], axis), jnp.concatenate([b, a], axis))

    micro, own, width = inputs.shape
    rows = micro * own
    n = w_query.shape[1]
    per = n // HEAD
    units = w_inner.shape[1] // 2
    att_rows = 4 * n + 32
    in_size = units + PAD

    rest = 2 * XBIT
    zbit = (me // rest) % 2
    if 2 * rest < total:
        zbit = (zbit + (me // (2 * rest)) % 2) % 2
    bits = jnp.stack([xbit, me, zbit]).astype(jnp.int32)
    sent_lengths = lax.dynamic_slice_in_dim(lengths, mp, 1, 1).reshape(-1)
    x = inputs.reshape(rows, width)
    vectors = jnp.stack(
        [b_output, gain_first, bias_first, b_outer, gain_second, bias_second, b_outer, b_outer]
    ).astype(F32)

    row_block = lambda r, c: ((r, c), lambda s, *_: (s, 0))
    sent_block = lambda a: ((None, a, SEQ), lambda s, *_: (s, 0, 0))
    piece = lambda r, p: ((r, width), lambda s, *_: (p, 0))

    att_own, att_send = call(
        pack_att_kernel, (1,), [None] * 6,
        [((att_rows, width), BF16), ((att_rows // 2, width), BF16)],
        prefetch=1, name="pack_att", us=2, mib=14, keep=(1,), held=range(6),
    )(bits, w_query.T, w_key.T, w_value.T, w_output, b_query[None], b_value[None])
    att_own, att_send, x, w_inner = fence(att_own, att_send, x, w_inner)

    def attn_outs(count):
        return [
            ((micro, 3 * n * count, SEQ), BF16, *sent_block(3 * n * count)),
            ((micro, n * count, SEQ), BF16, *sent_block(n * count)),
            ((micro, per * count, SEQ), F32, *sent_block(per * count)),
            ((8, n * count), F32),
        ]

    att_y = flip(att_send, YBIT)
    att_sib = flip_hbm(att_own, CORE)
    in_own, out_own, in_send, out_send = call(
        pack_ffn_kernel, (1,), [None] * 3,
        [
            ((2 * in_size, width), BF16), ((2 * units, width), BF16),
            ((in_size, width), BF16), ((units, width), BF16),
        ],
        prefetch=1, name="pack_ffn", us=3, mib=16, keep=(2, 3), held=range(3),
    )(bits, w_inner, b_inner[None], w_outer)
    x, in_own, out_own, in_send, out_send = fence(x, in_own, out_own, in_send, out_send)
    rows_out = ((rows, width), F32, *row_block(SEQ, width))
    qkv_0, ctx_0, lse_0, csum_0, xsum = call(
        functools.partial(attend_first_kernel, per=per), (micro,),
        [row_block(SEQ, width), None], attn_outs(1) + [((8, width), F32)],
        prefetch=1, name="attend_own", mib=22, held=(0,),
    )(sent_lengths, x, att_own)
    att_y, att_sib, in_send, x, qkv_0, ctx_0, lse_0, csum_0 = fence(
        att_y, att_sib, in_send, x, qkv_0, ctx_0, lse_0, csum_0
    )
    att_x = flip(att_y, XBIT)
    in_y = flip(in_send, YBIT)
    att_y_sib = flip(att_y, CORE)
    qkv_1, ctx_1, lse_1, csum_1 = call(
        functools.partial(attend_next_kernel, per=per), (micro,),
        [row_block(SEQ, width), None], attn_outs(1),
        prefetch=1, name="attend_sibling", mib=22, held=(0, 1),
    )(sent_lengths, x, att_sib)
    att_x, att_y_sib, in_y, x, qkv_1, ctx_1, lse_1, csum_1, in_own, out_own = fence(
        att_x, att_y_sib, in_y, x, qkv_1, ctx_1, lse_1, csum_1, in_own, out_own
    )
    att_x_sib = flip(att_x, CORE)
    in_x = flip(in_y, XBIT)
    out_y = flip(out_send, YBIT)
    in_sib = flip_hbm(in_own, CORE)
    out_sib = flip_hbm(out_own, CORE)
    qkv_b, ctx_b, lse_b, csum_b, att_far, norm1, inv1, low, lsum = call(
        functools.partial(attend_last_kernel, per=per), (micro,),
        [row_block(SEQ, width)] + [None] * 6 + [sent_block(n), sent_block(n), None],
        attn_outs(2) + [
            ((2, att_rows, width), BF16),
            rows_out,
            ((rows, 128), F32, *row_block(SEQ, 128)),
            ((rows, width), BF16, *row_block(SEQ, width)),
            ((8, width), F32),
        ],
        scratch=[pltpu.VMEM((4 * n, width), BF16), pltpu.VMEM((4 * n, SEQ), BF16)],
        prefetch=2, name="attend_far", us=14, mib=36, held=(0, 1, 2, 3, 4, 6),
    )(sent_lengths, bits, x, att_y, att_x, att_y_sib, att_x_sib, att_own, att_sib, ctx_0, ctx_1, vectors)
    low, norm1, inv1, in_x, out_y, in_sib, out_sib, in_y = fence(
        low, norm1, inv1, in_x, out_y, in_sib, out_sib, in_y
    )

    out_x = flip(out_y, XBIT)
    in_y_sib = flip(in_y, CORE)
    in_x_sib = flip(in_x, CORE)
    out_y_sib = flip(out_y, CORE)
    block = 256
    steps = rows // block
    ffn_outs = [
        ((rows, 4 * units), BF16, *row_block(block, 4 * units)),
        ((rows, 4 * units), BF16, *row_block(block, 4 * units)),
        ((8, 4 * units), F32),
    ]
    ffn_scratch = [
        pltpu.VMEM((2, 2 * units, width), BF16),
        pltpu.VMEM((2, 2 * units, width), BF16),
        pltpu.VMEM((2, 8, 2 * units), F32),
    ]
    near_specs = []
    near = []
    for p in range(2):
        near_specs += [piece(in_size, p), piece(units, p)] * 2
        near += [in_own, out_own, in_sib, out_sib]
    hid_near, slope_near, hsum_near, ffn_a = call(
        functools.partial(ffn_near_kernel, units=units), (steps,),
        [row_block(block, width)] + near_specs,
        ffn_outs + [((rows, width), F32, *row_block(block, width))],
        scratch=ffn_scratch, name="ffn_near", mib=34, held=(3, 4, 7, 8),
    )(low, *near)
    out_x, in_x_sib, out_y_sib, in_y_sib, ffn_a, hid_near, slope_near, hsum_near = fence(
        out_x, in_x_sib, out_y_sib, in_y_sib, ffn_a, hid_near, slope_near, hsum_near
    )
    out_x_sib = flip(out_x, CORE)

    far = [in_y, out_y, in_y_sib, out_y_sib, in_x, out_x, in_x_sib, out_x_sib]
    hid_far, slope_far, hsum_far, out_rows, norm2, inv2, pooled = call(
        functools.partial(ffn_far_kernel, units=units, blocks=SEQ // block), (steps,),
        [row_block(block, width)] + [None] * 8
        + [row_block(block, width), row_block(block, width), None],
        ffn_outs + [
            ((rows, width), BF16, *row_block(block, width)),
            ((rows, width), F32, *row_block(block, width)),
            ((rows, 128), F32, *row_block(block, 128)),
            ((8, width), F32),
        ],
        scratch=ffn_scratch, prefetch=1, name="ffn_far", mib=40, held=(1, 2, 3, 4, 5, 6, 7, 8),
    )(sent_lengths, low, *far, ffn_a, norm1, vectors)

    pool = pooled[0:micro]
    unit = pool * lax.rsqrt(jnp.sum(pool * pool, axis=1, keepdims=True) + EPS_UNIT)
    share = 1.0 / (rows * total)
    by_quarter = lambda v: v.reshape(2, 2, units).transpose(1, 0, 2).reshape(2, 2 * units)
    means = share * jnp.concatenate(
        [
            xsum[0:1],
            lsum[0:1],
            jnp.concatenate([csum_0[0:1], csum_1[0:1], csum_b[0:1]], axis=1),
            by_quarter(hsum_near[0]),
            by_quarter(hsum_far[0]),
            jnp.zeros((1, width), F32),
        ]
    )

    def swap_slots(v, mask, pieces):
        if mask == CORE:
            return v.reshape(2, 2, -1)[:, ::-1].reshape(v.shape)
        if mask == YBIT:
            return v.reshape(2, 2, -1)[::-1].reshape(v.shape)
        if mask == XBIT and pieces:
            return v.reshape(4, 2, -1)[:, ::-1].reshape(v.shape)
        return v

    def other_means(v, mask):
        return jnp.concatenate(
            [
                v[0:2],
                swap_slots(v[2].reshape(4, n), mask, False).reshape(1, width),
                swap_slots(v[3:7], mask, True),
                v[7:8],
            ]
        )

    stages, mask = [], 1
    while mask < total:
        pair = mask != XBIT and 2 * mask < total
        stages.append((mask, 2 * mask, 3 * mask) if pair else (mask,))
        mask *= 4 if pair else 2
    bundle = jnp.concatenate([means, unit], axis=0)
    for index, masks in enumerate(stages):
        others = [flip(bundle, m) for m in masks]
        mine = bundle[0:8]
        for m, other in zip(masks, others):
            part = other[0:8]
            for single in (CORE, YBIT, XBIT):
                if m & single:
                    part = other_means(part, single)
            others[masks.index(m)] = (part, other[8:])
        if len(masks) == 3:
            mine = (mine + others[0][0]) + (others[1][0] + others[2][0])
        else:
            mine = mine + others[0][0]
        unit_blocks = [bundle[8:]] + [o[1] for o in others]
        if index < len(stages) - 1:
            bundle = jnp.concatenate([mine] + unit_blocks, axis=0)
    means = mine

    dpre2, dlow, sums2 = call(
        functools.partial(loss_kernel, micro=micro, blocks=len(unit_blocks)), (micro,),
        [None] * (len(unit_blocks) + 2) + [row_block(SEQ, width), row_block(SEQ, 128), None],
        [
            ((rows, width), F32, *row_block(SEQ, width)),
            ((rows, width), BF16, *row_block(SEQ, width)),
            ((8, width), F32),
        ],
        scratch=[pltpu.VMEM((8, width), F32)], prefetch=2, name="loss", mib=28,
    )(sent_lengths, bits, *unit_blocks, pooled, membership.reshape(-1, membership.shape[2]), norm2, inv2, vectors)

    back_rows = SEQ

    def ffn_part(half, p, dlow, extra=None):
        hidden, slope, arrays, specs, base = half
        part = lambda s, *_: (s, p)
        rows_of = back_rows if extra is None else back_rows // 2
        block_of = lambda c: row_block(rows_of, c)
        ins = [block_of(width), block_of(width)] + [((rows_of, 2 * units), part)] * 2
        ins += [specs[1], specs[3], None, None]
        places = ((base, p * units), (base + 1, p * units))
        outs = [((2 * units, width), BF16)] * 2 + [((8, 2 * units), F32)]
        args = [dlow, low, hidden, slope, arrays[1], arrays[3], means, sums2]
        scratch = [pltpu.VMEM((2 * units, width), BF16), pltpu.VMEM((2, 2 * units, width), F32)]
        if extra is not None:
            parts, pieces_in, piece_specs, prev = extra
            ins += [block_of(2 * units)] * 3 + piece_specs
            ins += [block_of(width), block_of(width), block_of(128), None]
            args += [*parts, *pieces_in, prev, norm1, inv1, vectors]
            outs += [
                ((rows, width), F32, *block_of(width)),
                ((rows, width), BF16, *block_of(width)),
                ((8, width), F32),
            ]
            scratch += [pltpu.VMEM((8 * units, width), BF16)]
        else:
            outs += [((rows, 2 * units), BF16, *block_of(2 * units))]
        return call(
            functools.partial(
                ffn_back_kernel if extra is None else ffn_back_last_kernel, units=units, rows=places
            ),
            (rows // rows_of,), ins, outs, scratch=scratch, name="ffn_back",
            us=7 if extra is None else 14, mib=30 if extra is None else 44, keep=(0, 1),
            held=(4, 5) + tuple(range(11, 19)),
        )(*args)

    near_half = lambda p: (
        hid_near, slope_near, near[0:4], [piece(in_size, p), piece(units, p)] * 2, 3
    )
    far_half = lambda p: (hid_far, slope_far, far[4 * p : 4 * p + 4], [None] * 4, 5)

    def add(*values):
        out = values[0].astype(F32)
        for v in values[1:]:
            out = out + v.astype(F32)
        return out.astype(BF16)

    def rest_split(a, mask):
        half = a.shape[0] // 2
        bit = (me // mask) % 2
        if 2 * mask < total:
            bit = (bit + (me // (2 * mask)) % 2) % 2
        keep = lax.dynamic_slice_in_dim(a, bit * half, half, 0)
        send = lax.dynamic_slice_in_dim(a, (1 - bit) * half, half, 0)
        return bit, keep, send

    def rest_finish(bit, part, mask):
        inner = mask * 2
        while inner < total:
            part = add(part, flip(part, inner | mask if inner == 2 * mask else inner))
            inner *= 2
        other = flip(part, mask)
        return jnp.where(
            bit == 0, jnp.concatenate([part, other], 0), jnp.concatenate([other, part], 0)
        )

    def merged(bit, mine, other):
        return jnp.where(
            bit == 0, jnp.concatenate([mine, other], 0), jnp.concatenate([other, mine], 0)
        )

    def inner_flip(a):
        return flip(a, 3 * rest) if 2 * rest < total else jnp.zeros_like(a)

    def inner_rest(a):
        mask = 4 * rest
        while mask < total:
            a = add(a, flip(a, mask))
            mask *= 2
        return a

    full, part = units, units // 2
    top, bottom = slice(0, full), slice(full, 2 * full)

    def halves(a, bit):
        half = a.shape[0] // 2
        kept = lax.dynamic_slice_in_dim(a, bit * half, half, 0)
        return kept, lax.dynamic_slice_in_dim(a, (1 - bit) * half, half, 0)

    def halves_z(a):
        return halves(a, zbit)

    k_f1, s_f1, gb_f1, di_f1 = ffn_part(far_half(1), 1, dlow)
    c_f1 = flip(s_f1, CORE)
    f1a = add(k_f1[top], c_f1[top])
    f1a, c_f1, k_f1, dlow = fence(f1a, c_f1, k_f1, dlow)

    y1a = flip(f1a, YBIT)
    k_f0, s_f0, gb_f0, di_f0 = ffn_part(far_half(0), 0, dlow)
    f1b = add(k_f1[bottom], c_f1[bottom])
    y1a, f1b, k_f0, s_f0, gb_f0, di_f0, dlow = fence(y1a, f1b, k_f0, s_f0, gb_f0, di_f0, dlow)

    y1b = flip(f1b, YBIT)
    c_f0 = flip(s_f0, CORE)
    k_n1, s_n1, gb_n1, di_n1 = ffn_part(near_half(1), 1, dlow)
    y1b, c_f0, k_n1, s_n1, gb_n1, di_n1, dlow = fence(y1b, c_f0, k_n1, s_n1, gb_n1, di_n1, dlow)
    c_n1 = flip(s_n1, CORE)
    f0a = add(k_f0[top], c_f0[top])
    c_n1, f0a, dlow, k_f0, c_f0 = fence(c_n1, f0a, dlow, k_f0, c_f0)
    y0a = flip(f0a, YBIT)
    s1a = add(k_n1[top], c_n1[top], y1a)
    s1b = add(k_n1[bottom], c_n1[bottom], y1b)
    s1a, s1b, dlow = fence(s1a, s1b, dlow)

    x1a = flip(s1a, XBIT)
    x1b = flip(s1b, XBIT)
    pieces_in = [far[4], far[6], far[0], far[2], near[0], near[2], near[0], near[2]]
    piece_specs = [None] * 4 + [piece(in_size, 1)] * 2 + [piece(in_size, 0)] * 2
    k_n0, s_n0, gb_n0, dpre1, dattn, sums1 = ffn_part(
        near_half(0), 0, dlow, ((di_f1, di_f0, di_n1), pieces_in, piece_specs, dpre2)
    )
    f0b = add(k_f0[bottom], c_f0[bottom])
    y0a, x1a, k_n0, s_n0, gb_n0, dpre1, dattn, sums1, f0b = fence(
        y0a, x1a, k_n0, s_n0, gb_n0, dpre1, dattn, sums1, f0b
    )

    def attend_part(w, qkv, ctx, lse, base, place, dattn):
        count = qkv.shape[1] // (3 * n)
        w_spec = None if w.ndim == 2 else ((None, att_rows, width), lambda s, *_: (base, 0, 0))
        return call(
            functools.partial(attend_back_kernel, per=per, base=base, place=place), (micro,),
            [
                row_block(SEQ, width), row_block(SEQ, width), w_spec, sent_block(3 * n * count),
                sent_block(n * count), sent_block(per * count), None, None,
            ],
            [
                ((4 * n, width), BF16), ((8, width), F32),
                ((micro, 3 * n, SEQ), BF16, *sent_block(3 * n)),
            ],
            scratch=[pltpu.VMEM((4 * n, width), F32)],
            prefetch=1, name="attend_back", mib=24, keep=(0,), held=(0,) if w is not att_sib else (0, 2),
        )(sent_lengths, x, dattn, w, qkv, ctx, lse, means, sums1)

    y0b = flip(f0b, YBIT)
    c_n0 = flip(s_n0, CORE)
    g_3, gb_3, dq_3 = attend_part(att_far, qkv_b, ctx_b, lse_b, 1, 3, dattn)
    y0b, x1b, c_n0, g_3, gb_3, dq_3, dattn = fence(y0b, x1b, c_n0, g_3, gb_3, dq_3, dattn)
    keep_a, send_a = halves_z(add(k_n0[top], c_n0[top], y0a, x1a))
    keep_b, send_b = halves_z(add(k_n0[bottom], c_n0[bottom], y0b, x1b))
    send_a, send_b, keep_a, keep_b, g_3, dattn = fence(send_a, send_b, keep_a, keep_b, g_3, dattn)

    z_a = flip(send_a, rest)
    z_b = flip(send_b, rest)
    c_3 = flip(g_3, CORE)
    g_2, gb_2, dq_2 = attend_part(att_far, qkv_b, ctx_b, lse_b, 0, 2, dattn)
    c_3, z_a, z_b, g_2, gb_2, dq_2, dattn = fence(c_3, z_a, z_b, g_2, gb_2, dq_2, dattn)
    af_a = add(g_2[top], c_3[top])
    r_a = add(keep_a, z_a)
    r_b = add(keep_b, z_b)
    af_a, g_2, c_3, r_a, r_b, dattn = fence(af_a, g_2, c_3, r_a, r_b, dattn)

    y_afa = flip(af_a, YBIT)
    i_a = inner_flip(r_a)
    g_1, gb_1, dq_1 = attend_part(att_sib, qkv_1, ctx_1, lse_1, 0, 1, dattn)
    af_b = add(g_2[bottom], c_3[bottom])
    y_afa, i_a, g_1, gb_1, dq_1, dattn, af_b = fence(y_afa, i_a, g_1, gb_1, dq_1, dattn, af_b)
    r_a = inner_rest(add(r_a, i_a))
    r_a, r_b, g_1, dattn, af_b = fence(r_a, r_b, g_1, dattn, af_b)

    y_afb = flip(af_b, YBIT)
    c_1 = flip(g_1, CORE)
    i_b = inner_flip(r_b)
    z_a = flip(r_a, rest)
    g_0, gb_0, dq_0 = attend_part(att_own, qkv_0, ctx_0, lse_0, 0, 0, dattn)
    y_afb, c_1, z_a, i_b, g_0, gb_0, dq_0, dpre1 = fence(
        y_afb, c_1, z_a, i_b, g_0, gb_0, dq_0, dpre1
    )

    t_keep, t_send = halves(add(g_0[top], c_1[top], y_afa), xbit)
    b_keep, b_send = halves(add(g_0[bottom], c_1[bottom], y_afb), xbit)
    r_b = inner_rest(add(r_b, i_b))
    t_send, b_send, t_keep, b_keep, r_b, dpre1 = fence(t_send, b_send, t_keep, b_keep, r_b, dpre1)
    t_x = flip(t_send, XBIT)
    b_x = flip(b_send, XBIT)
    z_b = flip(r_b, rest)
    second = lambda i: ((None, att_rows, width), lambda s, *_: (i, 0, 0))
    (dx,) = call(
        input_grad_kernel, (micro,),
        [row_block(SEQ, width)] + [sent_block(3 * n)] * 4 + [None, None, second(0), second(1)],
        [rows_out], name="input_grad", mib=28, held=(6,),
    )(dpre1, dq_0, dq_1, dq_2, dq_3, att_own, att_sib, att_far, att_far)
    r_in = merged(zbit, r_a, z_a)

    small = jnp.concatenate(
        [sums1, sums2]
        + [v[0:1] for v in (gb_0, gb_1, gb_2, gb_3)]
        + [jnp.pad(v[0:1], ((0, 0), (0, width - 2 * units))) for v in (gb_n0, gb_n1, gb_f0, gb_f1)],
        axis=0,
    )

    def rows_in(v, order):
        return [v[i : i + 1] for i in order]

    def other_small(v, mask):
        if mask == CORE:
            ffn = jnp.concatenate([v[20:24, units : 2 * units], v[20:24, :units]], axis=1)
            return jnp.concatenate([v[:16]] + rows_in(v, (17, 16, 19, 18)) + [ffn], axis=0)
        if mask == YBIT:
            return jnp.concatenate([v[:16]] + rows_in(v, (18, 19, 16, 17, 22, 23, 20, 21)), axis=0)
        if mask == XBIT:
            return jnp.concatenate([v[:20]] + rows_in(v, (21, 20, 23, 22)), axis=0)
        return v

    def small_step(v, mask):
        return v + other_small(flip(v, mask), mask), 2 * mask

    small, step = small_step(small, 1)
    t_x, b_x, z_b, r_in, dx, small = fence(t_x, b_x, z_b, r_in, dx, small)
    t2_keep, t2_send = halves_z(add(t_keep, t_x))
    b2_keep, b2_send = halves_z(add(b_keep, b_x))
    r_out = merged(zbit, r_b, z_b)
    t2_send, b2_send, t2_keep, b2_keep, small, r_in, r_out = fence(
        t2_send, b2_send, t2_keep, b2_keep, small, r_in, r_out
    )
    t2_z = flip(t2_send, rest)
    b2_z = flip(b2_send, rest)
    r_in_x = flip(r_in, XBIT)
    small, step = small_step(small, step)
    t2_z, b2_z, small = fence(t2_z, b2_z, small)
    t2 = add(t2_keep, t2_z)
    b2 = add(b2_keep, b2_z)
    t2, b2, small = fence(t2, b2, small)
    t2_i = inner_flip(t2)
    b2_i = inner_flip(b2)
    r_out_x = flip(r_out, XBIT)
    small, step = small_step(small, step)
    t2_i, b2_i, small, r_in_x = fence(t2_i, b2_i, small, r_in_x)
    t2 = inner_rest(add(t2, t2_i))
    b2 = inner_rest(add(b2, b2_i))
    t2, b2, small = fence(t2, b2, small)
    t2_z = flip(t2, rest)
    b2_x = flip(b2, XBIT)
    small, step = small_step(small, step)
    t2_z, b2_x, small = fence(t2_z, b2_x, small)
    t1 = merged(zbit, t2, t2_z)
    b1 = jnp.concatenate([b2, b2_x], axis=0)
    while step < total:
        small, step = small_step(small, step)
    t1, b1, small, r_out_x = fence(t1, b1, small, r_out_x)
    t1_x = flip(t1, XBIT)
    b1_z = flip(b1, rest)

    shared = small[0:16]
    b_att = small[16, : 3 * n]
    grad_binner = ordered(small[20, :units], small[21, :units])
    hidden_mean = ordered(means[3, :units], means[3, units:])
    g_in = ordered(r_in, r_in_x).astype(F32)
    grad_inner = (g_in + grad_binner[:, None] * means[1][None]).T
    grad_outer = ordered(r_out, r_out_x).astype(F32) + hidden_mean[:, None] * shared[8][None]
    t1_x, b1_z, grad_inner, grad_outer = fence(t1_x, b1_z, grad_inner, grad_outer)
    cut = part // 2
    g_top = ordered(t1, t1_x).astype(F32)
    g_bottom = ordered(
        merged(zbit, b1[:cut], b1_z[:cut]), merged(zbit, b1[cut:], b1_z[cut:])
    ).astype(F32)
    outer = lambda a, b: b_att[a:b, None] * means[0][None]
    grad_wout = g_bottom[n:] + means[2, :n][:, None] * shared[0][None]

    return (
        out_rows.reshape(micro, own, width),
        small[11, 0],
        dx.reshape(micro, own, width),
        (g_top[:n] + outer(0, n)).T,
        b_att[:n],
        (g_top[n:] + outer(n, 2 * n)).T,
        (g_bottom[:n] + outer(2 * n, 3 * n)).T,
        b_att[2 * n :],
        grad_wout,
        shared[0],
        shared[1],
        shared[2],
        grad_inner,
        grad_binner,
        grad_outer,
        shared[8],
        shared[9],
        shared[10],
    )


def solution(mesh):
    rows = P(None, ("dp", "mp"), None)
    cols = P(None, "mp")
    split = P("mp")
    whole = P()
    placed = (rows, P(None, "dp"), whole, cols, split, cols, cols, split, P("mp", None))
    placed += (whole, whole, whole, cols, split, P("mp", None), whole, whole, whole)
    results = (rows, whole, rows, cols, split, cols, cols, split, P("mp", None))
    results += (whole, whole, whole, cols, split, P("mp", None), whole, whole, whole)
    return jax.shard_map(shards, mesh=mesh, in_specs=placed, out_specs=results, check_vma=False)
```

```python
import functools
import math

import jax
import jax.numpy as jnp
from jax import lax
from jax.experimental import pallas as pl
from jax.experimental.pallas import tpu as pltpu
from jax.sharding import PartitionSpec as P

HEAD = 64
SEQ = 512
EPS_NORM = 1e-5
EPS_UNIT = 1e-6
COS_SCALE = 20.0
LOG2E = 1.4426950408889634
NEG = -1e30
F32 = jnp.float32
BF16 = jnp.bfloat16
CORE, YBIT, XBIT = 1, 2, 4
PAD = 16


def dot(a, b, ca, cb, precision=None):
    return lax.dot_general(
        a, b, (((ca,), (cb,)), ((), ())), preferred_element_type=F32, precision=precision
    )


def mm(a, b):
    return dot(a, b, 1, 0)


def mm_nt(a, b):
    return dot(a, b, 1, 1)


def mm_tn(a, b):
    return dot(a, b, 0, 0)


def column(row):
    return jnp.broadcast_to(row, (8, row.shape[1])).T[:, :1]


def call(kernel, grid, ins, outs, scratch=(), prefetch=0, name=None, us=7, mib=44, keep=(), held=()):
    def spec(block, index):
        return pl.BlockSpec(block, index)

    def whole(a, **mode):
        rank = len(a)
        return pl.BlockSpec(tuple(a), lambda *_: (0,) * rank, **mode)

    def run(*args):
        in_specs, placed = [], list(args[:prefetch])
        for i, (item, arg) in enumerate(zip(ins, args[prefetch:])):
            big = arg.size > 1 << 16
            single = {"pipeline_mode": pl.Buffered(1)} if big else {}
            in_specs.append(whole(arg.shape, **single) if item is None else spec(*item))
            placed.append(
                pltpu.with_memory_space_constraint(arg, pltpu.HBM) if big and i not in held else arg
            )
        out_specs = [whole(o[0]) if len(o) == 2 else spec(*o[2:]) for o in outs]
        shapes = []
        for i, o in enumerate(outs):
            if i in keep:
                shapes.append(pltpu.VMEM(o[0], o[1]))
            elif math.prod(o[0]) > 1 << 16:
                shapes.append(pltpu.HBM(o[0], o[1]))
            else:
                shapes.append(jax.ShapeDtypeStruct(o[0], o[1]))
        return pl.pallas_call(
            kernel,
            out_shape=shapes,
            grid_spec=pltpu.PrefetchScalarGridSpec(
                num_scalar_prefetch=prefetch,
                grid=grid,
                in_specs=in_specs,
                out_specs=out_specs,
                scratch_shapes=list(scratch),
            ),
            compiler_params=pltpu.CompilerParams(vmem_limit_bytes=mib << 20),
            cost_estimate=pl.CostEstimate(flops=int(us * 1.1e9), transcendentals=0, bytes_accessed=1000),
            name=name,
        )(*placed)

    return run


def pack_att_kernel(bits_ref, wq, wk, wv, wo, bq, bv, att_ref, send_ref):
    n = wo.shape[0]
    att_ref[0:n, :] = wq[...]
    att_ref[n : 2 * n, :] = wk[...]
    att_ref[2 * n : 3 * n, :] = wv[...]
    att_ref[3 * n : 4 * n, :] = wo[...]
    rows = att_ref.shape[0] - 4 * n
    att_ref[4 * n :, :] = jnp.zeros_like(att_ref[4 * n :, :])
    att_ref[4 * n :, 0:n] = jnp.broadcast_to(bq[...], (rows, n))
    att_ref[4 * n :, 2 * n : 3 * n] = jnp.broadcast_to(bv[...], (rows, n))
    half = att_ref.shape[0] // 2
    send_ref[...] = att_ref[pl.ds(pl.multiple_of(bits_ref[0] * half, 16), half), :]


def pack_ffn_kernel(bits_ref, win, bin_, wout, in_ref, out_ref, in_send, out_send):
    x = bits_ref[0]
    units = win.shape[1] // 2
    size = units + PAD
    for piece in range(2):
        take = pl.multiple_of((x if piece == 0 else 1 - x) * units, 128)
        base = piece * size
        in_ref[base : base + units, :] = win[:, pl.ds(take, units)].T
        in_ref[base + units : base + size, :] = jnp.zeros((PAD, in_ref.shape[1]), BF16)
        in_ref[base + units : base + size, 0:units] = jnp.broadcast_to(
            bin_[:, pl.ds(take, units)], (PAD, units)
        )
        out_ref[piece * units : (piece + 1) * units, :] = wout[pl.ds(take, units), :]
    in_send[...] = in_ref[0:size, :]
    out_send[...] = out_ref[0:units, :]


def key_rows(length, ones):
    row = lax.broadcasted_iota(jnp.int32, (PAD, SEQ), 0)
    pos = lax.broadcasted_iota(jnp.int32, (PAD, SEQ), 1)
    base = jnp.where((row >= 1) & (row <= ones), 1.0, 0.0)
    return jnp.where((row == 0) & (pos >= length), NEG, base).astype(BF16)


def split_rows(first, value):
    row = lax.broadcasted_iota(jnp.int32, (PAD, SEQ), 0)
    high = value.astype(BF16).astype(F32)
    middle = (value - high).astype(BF16).astype(F32)
    lower = value - high - middle
    out = jnp.where(row == 0, first, 0.0)
    for i, part in enumerate((high, middle, lower)):
        out = jnp.where(row == i + 1, part, out)
    return out.astype(BF16)


def stack(*parts):
    return jnp.concatenate(parts, axis=0)


def attention_forward(len_ref, x_ref, packs, qkv_ref, ctx_ref, lse_ref, stat_ref, per, slot):
    length = len_ref[pl.program_id(0)]
    scale = LOG2E / math.sqrt(HEAD)
    n = per * HEAD

    @pl.when(pl.program_id(0) == 0)
    def _():
        stat_ref[...] = jnp.zeros_like(stat_ref)

    keys = key_rows(length, 0)
    ones = jnp.ones((PAD, SEQ), BF16)
    x = x_ref[...]
    for r, w in enumerate(packs):
        bias = column(w[4 * n : 4 * n + 1, 0 : 3 * n].astype(F32))
        qkv_ref[3 * n * r : 3 * n * (r + 1), :] = (mm_nt(w[0 : 3 * n, :], x) + bias).astype(BF16)

    def scores(i):
        a = 3 * n * (i // per) + (i % per) * HEAD
        q = stack(qkv_ref[a : a + HEAD, :], ones)
        k = stack(qkv_ref[n + a : n + a + HEAD, :], keys)
        return mm_tn(k, q)

    heads = per * len(packs)
    following = scores(0)
    for i in range(heads):
        s = following
        if i + 1 < heads:
            following = scores(i + 1)
        top = jnp.max(s, axis=0, keepdims=True)
        e = jnp.exp2(s * scale - top * scale).astype(BF16)
        a = 3 * n * (i // per) + (i % per) * HEAD
        c = mm(stack(qkv_ref[2 * n + a : 2 * n + a + HEAD, :], ones), e)
        total = c[HEAD : HEAD + 1, :]
        ctx_ref[i * HEAD : (i + 1) * HEAD, :] = (c[0:HEAD, :] * (1.0 / total)).astype(BF16)
        lse_ref[i : i + 1, :] = top + jnp.log2(total) * (1.0 / scale)
    sums = mm_nt(jnp.ones((8, SEQ), BF16), ctx_ref[...])
    stat_ref[2:3, slot * n : (slot + len(packs)) * n] += sums[0:1, :]


def attend_first_kernel(len_ref, x_ref, w0, qkv_ref, ctx_ref, lse_ref, stat_ref, *, per):
    attention_forward(len_ref, x_ref, (w0,), qkv_ref, ctx_ref, lse_ref, stat_ref, per, 0)
    stat_ref[0:1, :] += jnp.sum(x_ref[...].astype(F32), axis=0, keepdims=True)


def attend_next_kernel(len_ref, x_ref, w0, qkv_ref, ctx_ref, lse_ref, stat_ref, *, per):
    attention_forward(len_ref, x_ref, (w0,), qkv_ref, ctx_ref, lse_ref, stat_ref, per, 1)


def normalise(v):
    mean = jnp.mean(v, axis=-1, keepdims=True)
    centred = v - mean
    inv = lax.rsqrt(jnp.mean(centred * centred, axis=-1, keepdims=True) + EPS_NORM)
    return centred * inv, inv


def attend_last_kernel(
    len_ref, bits_ref, x_ref, y0, x0, y1, x1, wa, wb, ctxa_ref, ctxb_ref, vec_ref,
    qkv_ref, ctx_ref, lse_ref, stat_ref, pack_ref, norm_ref, inv_ref, low_ref,
    wo_scr, all_scr, *, per
):
    n = per * HEAD

    @pl.when(pl.program_id(0) == 0)
    def _():
        half = y0.shape[0]
        near = pl.multiple_of(bits_ref[0] * half, 16)
        away = pl.multiple_of((1 - bits_ref[0]) * half, 16)
        for r, (a, b) in enumerate(((y0, x0), (y1, x1))):
            pack_ref[r, pl.ds(near, half), :] = a[...]
            pack_ref[r, pl.ds(away, half), :] = b[...]
        for r, w in enumerate((wa, wb, pack_ref.at[0], pack_ref.at[1])):
            wo_scr[r * n : (r + 1) * n, :] = w[3 * n : 4 * n, :]

    packs = (pack_ref.at[0], pack_ref.at[1])
    attention_forward(len_ref, x_ref, packs, qkv_ref, ctx_ref, lse_ref, stat_ref, per, 2)
    all_scr[0:n, :] = ctxa_ref[...]
    all_scr[n : 2 * n, :] = ctxb_ref[...]
    all_scr[2 * n : 4 * n, :] = ctx_ref[...]
    pre = mm_tn(all_scr[...], wo_scr[...]) + vec_ref[0:1, :] + x_ref[...].astype(F32)
    normal, inv = normalise(pre)
    norm_ref[...] = normal
    inv_ref[...] = jnp.broadcast_to(inv, inv_ref.shape)
    first = normal * vec_ref[1:2, :] + vec_ref[2:3, :]
    low_ref[...] = first.astype(BF16)
    stat_ref[1:2, :] += jnp.sum(first, axis=0, keepdims=True)


def gelu_pair(u):
    cdf = 0.5 * lax.erf(u * (1.0 / math.sqrt(2.0))) + 0.5
    density = jnp.exp2(u * u * (-0.5 * LOG2E)) * (1.0 / math.sqrt(2.0 * math.pi))
    return u * cdf, cdf + u * density


def join(ins, outs, wi, wo, bias, units):
    for i in range(2):
        part = slice(i * units, (i + 1) * units)
        wi[part, :] = ins[i][0:units, :]
        wo[part, :] = outs[i][...]
        if bias is not None:
            bias[:, part] = ins[i][units : units + 8, 0:units].astype(F32)


def feed_forward(low, groups, hid_ref, slope_ref, stat_ref, wi, wo, bias, units, slot):
    @pl.when(pl.program_id(0) == 0)
    def _():
        for g, (ins, outs) in enumerate(groups):
            join(ins, outs, wi.at[g], wo.at[g], bias.at[g], units)
        stat_ref[...] = jnp.zeros_like(stat_ref)

    out = None
    for g in range(len(groups)):
        pre = mm_nt(low, wi[g]) + bias[g, 0:1, :]
        hidden, slope = gelu_pair(pre)
        cols = slice(2 * units * g, 2 * units * (g + 1))
        sums = jnp.sum(hidden, axis=0, keepdims=True)
        piece = slice(units * g, units * (g + 1))
        stat_ref[slot : slot + 1, piece] += sums[:, 0:units]
        stat_ref[slot + 1 : slot + 2, piece] += sums[:, units : 2 * units]
        hidden = hidden.astype(BF16)
        hid_ref[:, cols] = hidden
        slope_ref[:, cols] = slope.astype(BF16)
        part = mm(hidden, wo[g])
        out = part if out is None else out + part
    return out


def ffn_near_kernel(
    low_ref, i0, o0, i1, o1, i2, o2, i3, o3, hid_ref, slope_ref, stat_ref, out_ref, wi, wo, bias, *, units
):
    groups = (((i0, i1), (o0, o1)), ((i2, i3), (o2, o3)))
    out_ref[...] = feed_forward(
        low_ref[...], groups, hid_ref, slope_ref, stat_ref, wi, wo, bias, units, 3
    )


def ffn_far_kernel(
    len_ref, low_ref, i0, o0, i1, o1, i2, o2, i3, o3, prev_ref, norm_ref, vec_ref, s0, s1, s2, s3,
    hid_ref, slope_ref, bundle_ref, out_ref, norm2_ref, inv2_ref, pool_ref, stat_ref, wi, wo, bias,
    *, units, blocks, share
):
    step = pl.program_id(0)
    sent, block = step // blocks, step % blocks
    groups = (((i0, i1), (o0, o1)), ((i2, i3), (o2, o3)))
    ffn = feed_forward(low_ref[...], groups, hid_ref, slope_ref, stat_ref, wi, wo, bias, units, 5)
    first = norm_ref[...] * vec_ref[1:2, :] + vec_ref[2:3, :]
    normal, inv = normalise(ffn + prev_ref[...] + vec_ref[3:4, :] + first)
    norm2_ref[...] = normal
    inv2_ref[...] = jnp.broadcast_to(inv, inv2_ref.shape)
    second = normal * vec_ref[4:5, :] + vec_ref[5:6, :]
    out_ref[...] = second.astype(BF16)
    rows = low_ref.shape[0]
    position = block * rows + lax.broadcasted_iota(jnp.int32, (rows, 1), 0)
    part = jnp.sum(jnp.where(position < len_ref[sent], second, 0.0), axis=0, keepdims=True)

    @pl.when(step == 0)
    def _():
        pool_ref[...] = jnp.zeros_like(pool_ref)

    pool_ref[pl.ds(sent, 1), :] += part / len_ref[sent].astype(F32)

    @pl.when(step == pl.num_programs(0) - 1)
    def _():
        bundle_ref[0:8, :] = share * (stat_ref[...] + s0[...] + s1[...] + s2[...] + s3[...])
        pool = pool_ref[...]
        unit = pool * lax.rsqrt(jnp.sum(pool * pool, axis=1, keepdims=True) + EPS_UNIT)
        count = bundle_ref.shape[0] - 8
        bundle_ref[8 : 8 + count, :] = unit[0:count, :]


def loss_kernel(
    len_ref, bits_ref, *refs, micro, blocks, fields
):
    unit_refs = refs[:blocks]
    (pool_ref, member_ref, norm_ref, inv_ref, vec_ref, dpre_ref, dlow_ref, sums_ref,
     grad_scr) = refs[blocks:]
    step = pl.program_id(0)

    @pl.when(step == 0)
    def _():
        high = lax.Precision.HIGHEST
        units = jnp.concatenate([ref[...] for ref in unit_refs], axis=0)
        count = units.shape[0]
        sents = count // micro
        me = bits_ref[1]
        row = lax.broadcasted_iota(jnp.int32, (count, count), 0)
        col = lax.broadcasted_iota(jnp.int32, (count, count), 1)
        source = jnp.where(col // sents == row % micro, col % sents, -1)
        mask = jnp.zeros_like(row)
        for shift, largest, unit in fields:
            field = jnp.bitwise_and(lax.shift_right_logical(row // micro, shift), largest)
            mask = jnp.bitwise_xor(mask, field * unit)
        pick = (source == jnp.bitwise_xor(me, mask)).astype(F32)
        member = dot(pick, member_ref[...].astype(F32), 1, 0)
        same = dot(member, member, 1, 1)
        own = row == col
        apart = own | (row % micro != col % micro)
        positive = jnp.where(apart, 0.0, same)
        logits = COS_SCALE * dot(units, units, 1, 1, high)
        others = jnp.where(apart, NEG, logits)
        top = jnp.max(others, axis=1, keepdims=True)
        raised = jnp.exp(others - top)
        total = jnp.sum(raised, axis=1, keepdims=True)
        chosen = raised * positive
        total_pos = jnp.sum(chosen, axis=1, keepdims=True)
        each = jnp.log(total) - jnp.log(total_pos)
        loss = jnp.sum(each[0:micro], axis=0, keepdims=True)
        dlogits = raised / total - chosen / total_pos
        both = dlogits[0:micro, :] + dlogits.T[0:micro, :]
        dunits = COS_SCALE * dot(both, units, 1, 0, high)
        pooled = pool_ref[0:micro, :]
        rscale = lax.rsqrt(jnp.sum(pooled * pooled, axis=1, keepdims=True) + EPS_UNIT)
        unit = pooled * rscale
        grad_scr[0:micro, :] = rscale * (dunits - unit * jnp.sum(unit * dunits, axis=1, keepdims=True))
        sums_ref[...] = jnp.zeros_like(sums_ref)
        sums_ref[6:7, :] = jnp.broadcast_to(loss, (1, sums_ref.shape[1]))

    length = len_ref[step]
    spread = grad_scr[pl.ds(step, 1), :] * (1.0 / length.astype(F32))
    normal = norm_ref[...]
    g = spread * vec_ref[4:5, :]
    valid = lax.broadcasted_iota(jnp.int32, (SEQ, 1), 0) < length
    along = jnp.mean(g * normal, axis=1, keepdims=True)
    dpre = jnp.where(valid, inv_ref[:, 0:1] * (g - jnp.mean(g) - normal * along), 0.0)
    dpre_ref[...] = dpre
    dlow_ref[...] = dpre.astype(BF16)
    sums_ref[3:4, :] += jnp.sum(dpre, axis=0, keepdims=True)
    sums_ref[4:5, :] += spread * jnp.sum(jnp.where(valid, normal, 0.0), axis=0, keepdims=True)
    sums_ref[5:6, :] += spread * length.astype(F32)


def ffn_back(dlow, low, hid_ref, slope_ref, outs, wo, acc, gb_ref, units, row):
    @pl.when(pl.program_id(0) == 0)
    def _():
        for i in range(2):
            wo[i * units : (i + 1) * units, :] = outs[i][...]
        acc[...] = jnp.zeros_like(acc)
        gb_ref[...] = jnp.zeros_like(gb_ref)

    di = mm_nt(dlow, wo[...]) * slope_ref[...].astype(F32)
    gb_ref[row : row + 1, :] += jnp.sum(di, axis=0, keepdims=True)
    dil = di.astype(BF16)
    acc[1] += mm_tn(hid_ref[...], dlow)
    acc[0] += mm_tn(dil, low)
    return dil


def centre_ffn(keep_ref, send_ref, acc, gb_ref, mean_ref, bsum, units, rows, row):
    for i, (r, g_ref) in enumerate(zip(rows, (keep_ref, send_ref))):
        part = slice(i * units, (i + 1) * units)
        g_ref[0:units, :] = (acc[0, part, :] - column(gb_ref[row : row + 1, part]) * mean_ref[1:2, :]).astype(BF16)
        centre = column(mean_ref[r[0] : r[0] + 1, r[1] : r[1] + units])
        g_ref[units : 2 * units, :] = (acc[1, part, :] - centre * bsum).astype(BF16)


def ffn_back_kernel(*refs, units, rows, row, parts, own, last):
    take = iter(refs)
    more = lambda count: [next(take) for _ in range(count)]
    dlow_ref, low_ref, hid_ref, slope_ref, o0, o1, mean_ref, bsum_ref = more(8)
    part_refs = more(parts)
    pieces = more(2 * (parts + own))
    prev_ref = next(take) if parts + own else None
    norm_ref, inv_ref, vec_ref = more(3) if last else (None,) * 3
    keep_ref, send_ref, gb_ref = more(3)
    di_ref = None if own else next(take)
    dpre_ref, dattn_ref, sums_ref = more(3) if last else (None,) * 3
    sum_ref = next(take) if parts + own and not last else None
    wo, acc = more(2)
    wi = next(take) if parts + own else None

    @pl.when(pl.program_id(0) == 0)
    def _():
        if last:
            sums_ref[...] = jnp.zeros_like(sums_ref)
        for i, ref in enumerate(pieces):
            wi[i * units : (i + 1) * units, :] = ref[0:units, :]

    dil = ffn_back(
        dlow_ref[...], low_ref[...], hid_ref, slope_ref, (o0, o1), wo, acc, gb_ref, units, row
    )
    if di_ref is not None:
        di_ref[...] = dil
    if parts + own:
        dfirst = prev_ref[...]
        for i, part in enumerate([ref[...] for ref in part_refs] + ([dil] if own else [])):
            dfirst = dfirst + mm(part, wi[2 * units * i : 2 * units * (i + 1), :])
        if not last:
            sum_ref[...] = dfirst
    if last:
        normal = norm_ref[...]
        g = dfirst * vec_ref[1:2, :]
        along = jnp.mean(g * normal, axis=1, keepdims=True)
        dpre = inv_ref[:, 0:1] * (g - jnp.mean(g, axis=1, keepdims=True) - normal * along)
        dpre_ref[...] = dpre
        dattn_ref[...] = dpre.astype(BF16)
        sums_ref[0:1, :] += jnp.sum(dpre, axis=0, keepdims=True)
        sums_ref[1:2, :] += jnp.sum(dfirst * normal, axis=0, keepdims=True)
        sums_ref[2:3, :] += jnp.sum(dfirst, axis=0, keepdims=True)

    @pl.when(pl.program_id(0) == pl.num_programs(0) - 1)
    def _():
        centre_ffn(keep_ref, send_ref, acc, gb_ref, mean_ref, bsum_ref[3:4, :], units, rows, row)


def attend_back_kernel(
    len_ref, x_ref, dattn_ref, w_ref, qkv_ref, ctx_ref, lse_ref, mean_ref, bsum_ref,
    g_ref, gb_ref, grad_ref, acc, *, per, base, place
):
    step = pl.program_id(0)
    n = per * HEAD

    @pl.when(step == 0)
    def _():
        acc[...] = jnp.zeros_like(acc)
        gb_ref[...] = jnp.zeros_like(gb_ref)

    inv_root = 1.0 / math.sqrt(HEAD)
    scale = LOG2E * inv_root
    keys = key_rows(len_ref[step], 3)
    row = lax.broadcasted_iota(jnp.int32, (PAD, SEQ), 0)
    ones = jnp.where((row >= 1) & (row <= 3), 1.0, 0.0).astype(BF16)
    x = x_ref[...]
    dattn = dattn_ref[...]
    dctx = mm_nt(w_ref[3 * n : 4 * n, :], dattn).astype(BF16)
    acc[3 * n : 4 * n, :] += mm(ctx_ref[...], dattn)
    for h in range(per):
        c = h * HEAD
        q = qkv_ref[c : c + HEAD, :]
        k = qkv_ref[n + c : n + c + HEAD, :]
        v = qkv_ref[2 * n + c : 2 * n + c + HEAD, :]
        do = dctx[c : c + HEAD, :]
        o = ctx_ref[c : c + HEAD, :]
        lse = lse_ref[base * per + h : base * per + h + 1, :]
        weighted = jnp.sum(o.astype(F32) * do.astype(F32), axis=0, keepdims=True)
        s = mm_tn(stack(k, keys), stack(q, split_rows(1.0, -lse)))
        p = jnp.exp2(s * scale)
        dp = mm_tn(stack(v, ones), stack(do, split_rows(0.0, -weighted)))
        ds = (p * dp).astype(BF16)
        grad_ref[2 * n + c : 2 * n + c + HEAD, :] = mm_nt(do, p.astype(BF16)).astype(BF16)
        grad_ref[n + c : n + c + HEAD, :] = (mm_nt(q, ds) * inv_root).astype(BF16)
        grad_ref[c : c + HEAD, :] = (mm(k, ds) * inv_root).astype(BF16)
    grads = grad_ref[...]
    gb_ref[place : place + 1, 0 : 3 * n] += mm_nt(jnp.ones((8, SEQ), BF16), grads)[0:1, :]
    acc[0 : 3 * n, :] += mm(grads, x)

    @pl.when(step == pl.num_programs(0) - 1)
    def _():
        g_ref[0 : 3 * n, :] = (acc[0 : 3 * n, :] - column(gb_ref[place : place + 1, 0 : 3 * n]) * mean_ref[0:1, :]).astype(BF16)
        centre = column(mean_ref[2:3, place * n : (place + 1) * n])
        g_ref[3 * n : 4 * n, :] = (acc[3 * n : 4 * n, :] - centre * bsum_ref[0:1, :]).astype(BF16)


def input_grad_kernel(prev_ref, g0, g1, g2, g3, w0, w1, w2, w3, out_ref):
    out = prev_ref[...]
    for g, w in ((g0, w0), (g1, w1), (g2, w2), (g3, w3)):
        out = out + mm_tn(g[...], w[0 : g.shape[0], :])
    out_ref[...] = out


def ffn_final_kernel(bits_ref, in0, in1, out0, out1, small_ref, mean_ref, gin_ref, gout_ref):
    units = in0.shape[0]
    for p, (a, b) in enumerate(((in0, out0), (in1, out1))):
        spot = bits_ref[0] if p == 0 else 1 - bits_ref[0]
        spot = pl.multiple_of(spot * units, 128)
        part = slice(p * units, (p + 1) * units)
        grad = a[...].astype(F32) + column(small_ref[12 + p : 13 + p, 0:units]) * mean_ref[1:2, :]
        gin_ref[:, pl.ds(spot, units)] = grad.T
        gout_ref[pl.ds(spot, units), :] = (
            b[...].astype(F32) + column(mean_ref[3:4, part]) * small_ref[3:4, :]
        )


def fence(*values):
    return lax.optimization_barrier(values)


def shards(
    inputs, lengths, membership, w_query, b_query, w_key, w_value, b_value, w_output, b_output,
    gain_first, bias_first, w_inner, b_inner, w_outer, b_outer, gain_second, bias_second,
):
    total = lax.axis_size("dp") * lax.axis_size("mp")
    mp = lax.axis_index("mp")
    dp = lax.axis_index("dp")
    me = dp * lax.axis_size("mp") + mp
    xbit = dp % 2

    def flip(value, mask):
        return lax.ppermute(value, ("dp", "mp"), [(i, i ^ mask) for i in range(total)])

    def flip_hbm(value, mask):
        return flip(pltpu.with_memory_space_constraint(value, pltpu.HBM), mask)

    def ordered(a, b, axis=0):
        return jnp.where(xbit == 0, jnp.concatenate([a, b], axis), jnp.concatenate([b, a], axis))

    micro, own, width = inputs.shape
    rows = micro * own
    n = w_query.shape[1]
    per = n // HEAD
    units = w_inner.shape[1] // 2
    att_rows = 4 * n + 32
    in_size = units + PAD

    rest = 2 * XBIT
    zbit = (me // rest) % 2
    if 2 * rest < total:
        zbit = (zbit + (me // (2 * rest)) % 2) % 2
    bits = jnp.stack([xbit, me, zbit]).astype(jnp.int32)
    sent_lengths = lax.dynamic_slice_in_dim(lengths, mp, 1, 1).reshape(-1)
    x = inputs.reshape(rows, width)
    vectors = jnp.stack(
        [b_output, gain_first, bias_first, b_outer, gain_second, bias_second, b_outer, b_outer]
    ).astype(F32)

    row_block = lambda r, c: ((r, c), lambda s, *_: (s, 0))
    sent_block = lambda a: ((None, a, SEQ), lambda s, *_: (s, 0, 0))
    piece = lambda r, p: ((r, width), lambda s, *_: (p, 0))

    att_own, att_send = call(
        pack_att_kernel, (1,), [None] * 6,
        [((att_rows, width), BF16), ((att_rows // 2, width), BF16)],
        prefetch=1, name="pack_att", us=2, mib=14, keep=(1,),
    )(bits, w_query.T, w_key.T, w_value.T, w_output, b_query[None], b_value[None])
    att_own, att_send, x, w_inner = fence(att_own, att_send, x, w_inner)

    def attn_outs(count):
        return [
            ((micro, 3 * n * count, SEQ), BF16, *sent_block(3 * n * count)),
            ((micro, n * count, SEQ), BF16, *sent_block(n * count)),
            ((micro, per * count, SEQ), F32, *sent_block(per * count)),
            ((8, width), F32),
        ]

    att_y = flip(att_send, YBIT)
    att_sib = flip_hbm(att_own, CORE)
    in_own, out_own, in_send, out_send = call(
        pack_ffn_kernel, (1,), [None] * 3,
        [
            ((2 * in_size, width), BF16), ((2 * units, width), BF16),
            ((in_size, width), BF16), ((units, width), BF16),
        ],
        prefetch=1, name="pack_ffn", us=3, mib=16, keep=(2, 3),
    )(bits, w_inner, b_inner[None], w_outer)
    att_sib, x, in_own, out_own, in_send, out_send = fence(
        att_sib, x, in_own, out_own, in_send, out_send
    )
    rows_out = ((rows, width), F32, *row_block(SEQ, width))
    qkv_0, ctx_0, lse_0, stat_0 = call(
        functools.partial(attend_first_kernel, per=per), (micro,),
        [row_block(SEQ, width), None], attn_outs(1),
        prefetch=1, name="attend_own", mib=60, held=(0,),
    )(sent_lengths, x, att_own)
    att_y, x, in_send, qkv_0, ctx_0, lse_0, stat_0 = fence(
        att_y, x, in_send, qkv_0, ctx_0, lse_0, stat_0
    )
    att_x = flip(att_y, XBIT)
    in_y = flip(in_send, YBIT)
    att_y_sib = flip(att_y, CORE)
    qkv_1, ctx_1, lse_1, stat_1 = call(
        functools.partial(attend_next_kernel, per=per), (micro,),
        [row_block(SEQ, width), None], attn_outs(1),
        prefetch=1, name="attend_sibling", mib=60, held=(0, 1),
    )(sent_lengths, x, att_sib)
    att_x, att_y_sib, in_y, x, qkv_1, ctx_1, lse_1, stat_1, in_own, out_own = fence(
        att_x, att_y_sib, in_y, x, qkv_1, ctx_1, lse_1, stat_1, in_own, out_own
    )
    att_x_sib = flip(att_x, CORE)
    in_x = flip(in_y, XBIT)
    out_y = flip(out_send, YBIT)
    in_sib = flip_hbm(in_own, CORE)
    out_sib = flip_hbm(out_own, CORE)
    qkv_b, ctx_b, lse_b, stat_2, att_far, norm1, inv1, low = call(
        functools.partial(attend_last_kernel, per=per), (micro,),
        [row_block(SEQ, width)] + [None] * 6 + [sent_block(n), sent_block(n), None],
        attn_outs(2) + [
            ((2, att_rows, width), BF16),
            rows_out,
            ((rows, 128), F32, *row_block(SEQ, 128)),
            ((rows, width), BF16, *row_block(SEQ, width)),
        ],
        scratch=[pltpu.VMEM((4 * n, width), BF16), pltpu.VMEM((4 * n, SEQ), BF16)],
        prefetch=2, name="attend_far", us=14, mib=60, held=(0, 1, 2, 3, 4, 6),
    )(
        sent_lengths, bits, x, att_y, att_x, att_y_sib, att_x_sib, att_own, att_sib,
        ctx_0, ctx_1, vectors,
    )
    low, norm1, inv1, in_x, out_y, in_sib, out_sib, in_y = fence(
        low, norm1, inv1, in_x, out_y, in_sib, out_sib, in_y
    )

    out_x = flip(out_y, XBIT)
    in_y_sib = flip(in_y, CORE)
    in_x_sib = flip(in_x, CORE)
    out_y_sib = flip(out_y, CORE)
    block = 256
    steps = rows // block
    ffn_outs = [
        ((rows, 4 * units), BF16, *row_block(block, 4 * units)),
        ((rows, 4 * units), BF16, *row_block(block, 4 * units)),
    ]
    ffn_scratch = [
        pltpu.VMEM((2, 2 * units, width), BF16),
        pltpu.VMEM((2, 2 * units, width), BF16),
        pltpu.VMEM((2, 8, 2 * units), F32),
    ]
    near_specs = []
    near = []
    for p in range(2):
        near_specs += [piece(in_size, p), piece(units, p)] * 2
        near += [in_own, out_own, in_sib, out_sib]
    hid_near, slope_near, stat_3, ffn_a = call(
        functools.partial(ffn_near_kernel, units=units), (steps,),
        [row_block(block, width)] + near_specs,
        ffn_outs + [((8, width), F32), ((rows, width), F32, *row_block(block, width))],
        scratch=ffn_scratch, name="ffn_near", mib=60, held=(3, 4, 7, 8),
    )(low, *near)
    out_x, in_x_sib, out_y_sib, in_y_sib, ffn_a, hid_near, slope_near, stat_3 = fence(
        out_x, in_x_sib, out_y_sib, in_y_sib, ffn_a, hid_near, slope_near, stat_3
    )
    out_x_sib = flip(out_x, CORE)

    far = [in_y, out_y, in_y_sib, out_y_sib, in_x, out_x, in_x_sib, out_x_sib]
    hid_far, slope_far, bundle, out_rows, norm2, inv2, pooled = call(
        functools.partial(
            ffn_far_kernel, units=units, blocks=SEQ // block, share=1.0 / (rows * total)
        ), (steps,),
        [row_block(block, width)] + [None] * 8
        + [row_block(block, width), row_block(block, width)] + [None] * 5,
        ffn_outs + [
            ((8 + micro, width), F32),
            ((rows, width), BF16, *row_block(block, width)),
            ((rows, width), F32, *row_block(block, width)),
            ((rows, 128), F32, *row_block(block, 128)),
            ((8, width), F32),
        ],
        scratch=[pltpu.VMEM((8, width), F32)] + ffn_scratch, prefetch=1, name="ffn_far", mib=60, held=(1, 2, 3, 4, 5, 6, 7, 8),
    )(sent_lengths, low, *far, ffn_a, norm1, vectors, stat_0, stat_1, stat_2, stat_3)

    def swap_slots(v, mask, pieces):
        if mask == CORE:
            return v.reshape(2, 2, -1)[:, ::-1].reshape(v.shape)
        if mask == YBIT:
            return v.reshape(2, 2, -1)[::-1].reshape(v.shape)
        if mask == XBIT and pieces:
            return v.reshape(4, 2, -1)[:, ::-1].reshape(v.shape)
        return v

    def other_means(v, mask):
        return jnp.concatenate(
            [
                v[0:2],
                swap_slots(v[2].reshape(4, n), mask, False).reshape(1, width),
                swap_slots(v[3:7], mask, True),
                v[7:8],
            ]
        )

    def groups_of(first, last):
        found, mask = [], first
        while mask < last:
            found.append((mask, 2 * mask, 3 * mask) if 2 * mask < last else (mask,))
            mask *= 4
        return found

    mp_stages, x_stages, z_stages = groups_of(1, XBIT), [(XBIT,)], [(rest,)]
    if 2 * rest < total:
        z_stages += [(3 * rest,)] + groups_of(4 * rest, total)

    def sum_step(v, masks, reorder):
        parts = [v]
        for m in masks:
            part = flip(v, m)
            for single in (CORE, YBIT, XBIT):
                if m & single:
                    part = reorder(part, single)
            parts.append(part)
        while len(parts) > 1:
            parts = [parts[i] + parts[i + 1] for i in range(0, len(parts), 2)]
        return parts[0]

    stages = z_stages + mp_stages + x_stages
    fields, shift = [], 0
    for index, masks in enumerate(stages):
        others = [flip(bundle, m) for m in masks]
        parts = [bundle[0:8]]
        for m, other in zip(masks, others):
            part = other[0:8]
            for single in (CORE, YBIT, XBIT):
                if m & single:
                    part = other_means(part, single)
            parts.append(part)
        while len(parts) > 1:
            parts = [parts[i] + parts[i + 1] for i in range(0, len(parts), 2)]
        mine = parts[0]
        unit_blocks = [bundle[8:]] + [o[8:] for o in others]
        fields.append((shift, len(masks), masks[0]))
        shift += (len(masks) + 1) // 2
        if index < len(stages) - 1:
            bundle = jnp.concatenate([mine] + unit_blocks, axis=0)
    means = mine

    dpre2, dlow, sums2 = call(
        functools.partial(loss_kernel, micro=micro, blocks=len(unit_blocks), fields=fields), (micro,),
        [None] * (len(unit_blocks) + 2) + [row_block(SEQ, width), row_block(SEQ, 128), None],
        [
            ((rows, width), F32, *row_block(SEQ, width)),
            ((rows, width), BF16, *row_block(SEQ, width)),
            ((8, width), F32),
        ],
        scratch=[pltpu.VMEM((8, width), F32)], prefetch=2, name="loss", mib=28,
    )(sent_lengths, bits, *unit_blocks, pooled, membership.reshape(-1, membership.shape[2]), norm2, inv2, vectors)

    back_rows = SEQ

    def ffn_part(half, p, dlow, row, parts=(), pieces=(), own=False, prev=None, last=False):
        hidden, slope, arrays, specs, base = half
        part = lambda s, *_: (s, p)
        block_of = lambda c: row_block(back_rows, c)
        ins = [block_of(width), block_of(width)] + [((back_rows, 2 * units), part)] * 2
        ins += [specs[1], specs[3], None, None] + [block_of(2 * units)] * len(parts)
        args = [dlow, low, hidden, slope, arrays[1], arrays[3], means, sums2, *parts]
        free = [4, 5] + list(range(len(args), len(args) + len(pieces)))
        ins += [spec for _, spec in pieces]
        args += [a for a, _ in pieces]
        places = ((base, p * units), (base + 1, p * units))
        outs = [((2 * units, width), BF16)] * 2 + [((8, 2 * units), F32)]
        scratch = [pltpu.VMEM((2 * units, width), BF16), pltpu.VMEM((2, 2 * units, width), F32)]
        rows_f32 = ((rows, width), F32, *block_of(width))
        if not own:
            outs += [((rows, 2 * units), BF16, *block_of(2 * units))]
        if pieces:
            ins += [block_of(width)]
            args += [prev]
            scratch += [pltpu.VMEM((len(pieces) * units, width), BF16)]
        if last:
            ins += [block_of(width), block_of(128), None]
            args += [norm1, inv1, vectors]
            outs += [rows_f32, ((rows, width), BF16, *block_of(width)), ((8, width), F32)]
        elif pieces:
            outs += [rows_f32]
        return call(
            functools.partial(
                ffn_back_kernel, units=units, rows=places, row=row, parts=len(parts), own=own, last=last
            ),
            (rows // back_rows,), ins, outs, scratch=scratch, name="ffn_back",
            us=8 + 2 * len(pieces), mib=44, keep=(0, 1), held=free,
        )(*args)

    near_half = lambda p: (
        hid_near, slope_near, near[0:4], [piece(in_size, p), piece(units, p)] * 2, 3
    )
    far_half = lambda p: (hid_far, slope_far, far[4 * p : 4 * p + 4], [None] * 4, 5)

    def add(*values):
        out = values[0].astype(F32)
        for v in values[1:]:
            out = out + v.astype(F32)
        return out.astype(BF16)

    def rest_split(a, mask):
        half = a.shape[0] // 2
        bit = (me // mask) % 2
        if 2 * mask < total:
            bit = (bit + (me // (2 * mask)) % 2) % 2
        keep = lax.dynamic_slice_in_dim(a, bit * half, half, 0)
        send = lax.dynamic_slice_in_dim(a, (1 - bit) * half, half, 0)
        return bit, keep, send

    def rest_finish(bit, part, mask):
        inner = mask * 2
        while inner < total:
            part = add(part, flip(part, inner | mask if inner == 2 * mask else inner))
            inner *= 2
        other = flip(part, mask)
        return jnp.where(
            bit == 0, jnp.concatenate([part, other], 0), jnp.concatenate([other, part], 0)
        )

    def merged(bit, mine, other):
        return jnp.where(
            bit == 0, jnp.concatenate([mine, other], 0), jnp.concatenate([other, mine], 0)
        )

    def inner_flip(a):
        return flip(a, 3 * rest) if 2 * rest < total else jnp.zeros_like(a)

    def inner_rest(a):
        mask = 4 * rest
        while mask < total:
            a = add(a, flip(a, mask))
            mask *= 2
        return a

    full, part = units, units // 2
    top, bottom = slice(0, full), slice(full, 2 * full)

    def halves(a, bit):
        half = a.shape[0] // 2
        kept = lax.dynamic_slice_in_dim(a, bit * half, half, 0)
        return kept, lax.dynamic_slice_in_dim(a, (1 - bit) * half, half, 0)

    def halves_z(a):
        return halves(a, zbit)

    far_in = lambda p: [(far[4 * p], None), (far[4 * p + 2], None)]
    near_in = lambda p: [(near[0], piece(in_size, p)), (near[2], piece(in_size, p))]
    k_f1, s_f1, gb_f1, di_f1 = ffn_part(far_half(1), 1, dlow, 7)
    c_f1 = flip(s_f1, CORE)
    f1a = add(k_f1[top], c_f1[top])
    f1a, c_f1, k_f1, dlow = fence(f1a, c_f1, k_f1, dlow)

    y1a = flip(f1a, YBIT)
    k_f0, s_f0, gb_f0, di_f0, acc = ffn_part(
        far_half(0), 0, dlow, 6, (di_f1,), far_in(1), prev=dpre2
    )
    f1b = add(k_f1[bottom], c_f1[bottom])
    y1a, f1b, k_f0, s_f0, gb_f0, di_f0, acc, dlow = fence(
        y1a, f1b, k_f0, s_f0, gb_f0, di_f0, acc, dlow
    )

    y1b = flip(f1b, YBIT)
    c_f0 = flip(s_f0, CORE)
    k_n1, s_n1, gb_n1, acc = ffn_part(
        near_half(1), 1, dlow, 5, (di_f0,), far_in(0) + near_in(1), own=True, prev=acc
    )
    y1b, c_f0, k_n1, s_n1, gb_n1, acc, dlow = fence(y1b, c_f0, k_n1, s_n1, gb_n1, acc, dlow)
    c_n1 = flip(s_n1, CORE)
    f0a = add(k_f0[top], c_f0[top])
    c_n1, f0a, dlow, k_f0, c_f0 = fence(c_n1, f0a, dlow, k_f0, c_f0)
    y0a = flip(f0a, YBIT)
    s1a = add(k_n1[top], c_n1[top], y1a)
    s1b = add(k_n1[bottom], c_n1[bottom], y1b)
    s1a, s1b, dlow = fence(s1a, s1b, dlow)

    x1a = flip(s1a, XBIT)
    x1b = flip(s1b, XBIT)
    k_n0, s_n0, gb_n0, dpre1, dattn, sums1 = ffn_part(
        near_half(0), 0, dlow, 4, (), near_in(0), own=True, prev=acc, last=True
    )
    f0b = add(k_f0[bottom], c_f0[bottom])
    y0a, x1a, k_n0, s_n0, gb_n0, dpre1, dattn, sums1, f0b = fence(
        y0a, x1a, k_n0, s_n0, gb_n0, dpre1, dattn, sums1, f0b
    )
    c_n0 = flip(s_n0, CORE)
    keep_a, send_a = halves_z(add(k_n0[top], c_n0[top], y0a, x1a))
    keep_a, send_a, c_n0, dattn, f0b = fence(keep_a, send_a, c_n0, dattn, f0b)

    def attend_part(w, qkv, ctx, lse, base, place, dattn):
        w_spec = None if w.ndim == 2 else ((None, att_rows, width), lambda s, *_: (base, 0, 0))
        quarter_block = lambda a: ((None, a, SEQ), lambda s, *_: (s, base, 0))
        return call(
            functools.partial(attend_back_kernel, per=per, base=base, place=place), (micro,),
            [
                row_block(SEQ, width), row_block(SEQ, width), w_spec, quarter_block(3 * n),
                quarter_block(n), sent_block(lse.shape[1]), None, None,
            ],
            [
                ((4 * n, width), BF16), ((8, width), F32),
                ((micro, 3 * n, SEQ), BF16, *sent_block(3 * n)),
            ],
            scratch=[pltpu.VMEM((4 * n, width), F32)],
            prefetch=1, name="attend_back", mib=24, keep=(0,),
            held=() if w is not att_sib else (2,),
        )(sent_lengths, x, dattn, w, qkv, ctx, lse, means, sums1)

    y0b = flip(f0b, YBIT)
    z_a = flip(send_a, rest)
    g_3, gb_3, dq_3 = attend_part(att_far, qkv_b, ctx_b, lse_b, 1, 3, dattn)
    y0b, x1b, z_a, g_3, gb_3, dq_3, dattn = fence(y0b, x1b, z_a, g_3, gb_3, dq_3, dattn)
    keep_b, send_b = halves_z(add(k_n0[bottom], c_n0[bottom], y0b, x1b))
    r_a = add(keep_a, z_a)
    r_a, send_b, keep_b, g_3, dattn = fence(r_a, send_b, keep_b, g_3, dattn)

    i_a = inner_flip(r_a)
    z_b = flip(send_b, rest)
    c_3 = flip(g_3, CORE)
    g_2, gb_2, dq_2 = attend_part(att_far, qkv_b, ctx_b, lse_b, 0, 2, dattn)
    c_3, i_a, z_b, g_2, gb_2, dq_2, dattn = fence(c_3, i_a, z_b, g_2, gb_2, dq_2, dattn)
    af_a = add(g_2[top], c_3[top])
    r_a = inner_rest(add(r_a, i_a))
    r_b = add(keep_b, z_b)
    af_a, g_2, c_3, r_a, r_b, dattn = fence(af_a, g_2, c_3, r_a, r_b, dattn)

    y_afa = flip(af_a, YBIT)
    z_a = flip(r_a, rest)
    i_b = inner_flip(r_b)
    g_1, gb_1, dq_1 = attend_part(att_sib, qkv_1, ctx_1, lse_1, 0, 1, dattn)
    af_b = add(g_2[bottom], c_3[bottom])
    y_afa, i_b, z_a, g_1, gb_1, dq_1, dattn, af_b = fence(
        y_afa, i_b, z_a, g_1, gb_1, dq_1, dattn, af_b
    )
    r_in = merged(zbit, r_a, z_a)
    r_b = inner_rest(add(r_b, i_b))
    r_in, r_b, g_1, dattn, af_b = fence(r_in, r_b, g_1, dattn, af_b)

    y_afb = flip(af_b, YBIT)
    c_1 = flip(g_1, CORE)
    r_in_x = flip(r_in, XBIT)
    z_b = flip(r_b, rest)
    g_0, gb_0, dq_0 = attend_part(att_own, qkv_0, ctx_0, lse_0, 0, 0, dattn)
    y_afb, c_1, r_in_x, z_b, g_0, gb_0, dq_0, dpre1 = fence(
        y_afb, c_1, r_in_x, z_b, g_0, gb_0, dq_0, dpre1
    )

    small = jnp.concatenate(
        [sums1 + sums2, gb_0 + gb_1 + gb_2 + gb_3 + gb_n0 + gb_n1 + gb_f0 + gb_f1], axis=0
    )

    def rows_in(v, order):
        return [v[i : i + 1] for i in order]

    def other_small(v, mask):
        if mask == CORE:
            ffn = jnp.concatenate([v[12:16, units : 2 * units], v[12:16, :units]], axis=1)
            return jnp.concatenate([v[:8]] + rows_in(v, (9, 8, 11, 10)) + [ffn], axis=0)
        if mask == YBIT:
            return jnp.concatenate([v[:8]] + rows_in(v, (10, 11, 8, 9, 14, 15, 12, 13)), axis=0)
        return jnp.concatenate([v[:12]] + rows_in(v, (13, 12, 15, 14)), axis=0)

    def small_step(v, mask):
        if mask >= total:
            return v
        return sum_step(v, (3 * rest if mask == 2 * rest else mask,), other_small)

    small = small_step(small, CORE)

    t_keep, t_send = halves(add(g_0[top], c_1[top], y_afa), xbit)
    b_keep, b_send = halves_z(add(g_0[bottom], c_1[bottom], y_afb))
    r_out = merged(zbit, r_b, z_b)
    t_send, b_send, t_keep, b_keep, r_out, dpre1, small = fence(
        t_send, b_send, t_keep, b_keep, r_out, dpre1, small
    )
    t_x = flip(t_send, XBIT)
    b_z = flip(b_send, rest)
    r_out_x = flip(r_out, XBIT)
    second = lambda i: ((None, att_rows, width), lambda s, *_: (i, 0, 0))
    (dx,) = call(
        input_grad_kernel, (2 * micro,),
        [row_block(SEQ // 2, width)]
        + [((None, 3 * n, SEQ // 2), lambda s, *_: (s // 2, 0, s % 2))] * 4
        + [None, None, second(0), second(1)],
        [((rows, width), F32, *row_block(SEQ // 2, width))], name="input_grad", mib=28, held=(6,),
    )(dpre1, dq_0, dq_1, dq_2, dq_3, att_own, att_sib, att_far, att_far)

    small = small_step(small, YBIT)
    t_x, b_z, dx, small = fence(t_x, b_z, dx, small)
    t2_keep, t2_send = halves_z(add(t_keep, t_x))
    b2_keep, b2_send = halves(add(b_keep, b_z), xbit)
    t2_send, b2_send, t2_keep, b2_keep, small = fence(t2_send, b2_send, t2_keep, b2_keep, small)
    t2_z = flip(t2_send, rest)
    b2_x = flip(b2_send, XBIT)
    small = small_step(small, XBIT)
    t2_z, b2_x, small, r_out_x = fence(t2_z, b2_x, small, r_out_x)
    t2 = add(t2_keep, t2_z)
    b2 = add(b2_keep, b2_x)
    t2, b2, small = fence(t2, b2, small)
    t2_i = inner_flip(t2)
    b2_i = inner_flip(b2)
    small = small_step(small, rest)
    t2_i, b2_i, small = fence(t2_i, b2_i, small)
    t2 = inner_rest(add(t2, t2_i))
    b2 = inner_rest(add(b2, b2_i))
    t2, b2, small = fence(t2, b2, small)
    t2_z = flip(t2, rest)
    b2_x = flip(b2, XBIT)
    small = small_step(small, 2 * rest)
    t2_z, b2_x, small = fence(t2_z, b2_x, small)
    t1 = merged(zbit, t2, t2_z)
    b1 = merged(xbit, b2, b2_x)
    t1, b1, small = fence(t1, b1, small)
    t1_x = flip(t1, XBIT)
    b1_z = flip(b1, rest)
    mask = 4 * rest
    while mask < total:
        small = small_step(small, mask)
        mask *= 2

    shared = small[0:8]
    b_att = small[8, : 3 * n]
    grad_binner = ordered(small[12, :units], small[13, :units])
    grad_inner, grad_outer = call(
        ffn_final_kernel, (1,), [None] * 6, [((width, 2 * units), F32), ((2 * units, width), F32)],
        prefetch=1, name="ffn_final", mib=20, held=range(4),
    )(bits, r_in, r_in_x, r_out, r_out_x, small, means)
    t1_x, b1_z, grad_inner, grad_outer = fence(t1_x, b1_z, grad_inner, grad_outer)
    g_top = ordered(t1, t1_x).astype(F32)
    g_bottom = merged(zbit, b1, b1_z).astype(F32)
    outer = lambda a, b: b_att[a:b, None] * means[0][None]
    grad_wout = g_bottom[n:] + means[2, :n][:, None] * shared[0][None]

    return (
        out_rows.reshape(micro, own, width),
        small[6, 0],
        dx.reshape(micro, own, width),
        (g_top[:n] + outer(0, n)).T,
        b_att[:n],
        (g_top[n:] + outer(n, 2 * n)).T,
        (g_bottom[:n] + outer(2 * n, 3 * n)).T,
        b_att[2 * n :],
        grad_wout,
        shared[0],
        shared[1],
        shared[2],
        grad_inner,
        grad_binner,
        grad_outer,
        shared[3],
        shared[4],
        shared[5],
    )


def solution(mesh):
    rows = P(None, ("dp", "mp"), None)
    cols = P(None, "mp")
    split = P("mp")
    whole = P()
    placed = (rows, P(None, "dp"), whole, cols, split, cols, cols, split, P("mp", None))
    placed += (whole, whole, whole, cols, split, P("mp", None), whole, whole, whole)
    results = (rows, whole, rows, cols, split, cols, cols, split, P("mp", None))
    results += (whole, whole, whole, cols, split, P("mp", None), whole, whole, whole)
    return jax.shard_map(shards, mesh=mesh, in_specs=placed, out_specs=results, check_vma=False)
```

```python
import functools
import math

import jax
import jax.numpy as jnp
from jax import lax
from jax.experimental import pallas as pl
from jax.experimental.pallas import tpu as pltpu
from jax.sharding import PartitionSpec as P

HEAD = 64
SEQ = 512
EPS_NORM = 1e-5
EPS_UNIT = 1e-6
COS_SCALE = 20.0
LOG2E = 1.4426950408889634
NEG = -1e30
F32 = jnp.float32
BF16 = jnp.bfloat16
CORE, YBIT, XBIT = 1, 2, 4
PAD = 16


def dot(a, b, ca, cb, precision=None):
    return lax.dot_general(
        a, b, (((ca,), (cb,)), ((), ())), preferred_element_type=F32, precision=precision
    )


def mm(a, b):
    return dot(a, b, 1, 0)


def mm_nt(a, b):
    return dot(a, b, 1, 1)


def mm_tn(a, b):
    return dot(a, b, 0, 0)


def column(row):
    return jnp.broadcast_to(row, (8, row.shape[1])).T[:, :1]


def call(kernel, grid, ins, outs, scratch=(), prefetch=0, name=None, us=7, mib=44, keep=(), held=()):
    def spec(block, index):
        return pl.BlockSpec(block, index)

    def whole(a, **mode):
        rank = len(a)
        return pl.BlockSpec(tuple(a), lambda *_: (0,) * rank, **mode)

    def run(*args):
        in_specs, placed = [], list(args[:prefetch])
        for i, (item, arg) in enumerate(zip(ins, args[prefetch:])):
            big = arg.size > 1 << 16
            single = {"pipeline_mode": pl.Buffered(1)} if big else {}
            in_specs.append(whole(arg.shape, **single) if item is None else spec(*item))
            placed.append(
                pltpu.with_memory_space_constraint(arg, pltpu.HBM) if big and i not in held else arg
            )
        out_specs = [whole(o[0]) if len(o) == 2 else spec(*o[2:]) for o in outs]
        shapes = []
        for i, o in enumerate(outs):
            if i in keep:
                shapes.append(pltpu.VMEM(o[0], o[1]))
            elif math.prod(o[0]) > 1 << 16:
                shapes.append(pltpu.HBM(o[0], o[1]))
            else:
                shapes.append(jax.ShapeDtypeStruct(o[0], o[1]))
        return pl.pallas_call(
            kernel,
            out_shape=shapes,
            grid_spec=pltpu.PrefetchScalarGridSpec(
                num_scalar_prefetch=prefetch,
                grid=grid,
                in_specs=in_specs,
                out_specs=out_specs,
                scratch_shapes=list(scratch),
            ),
            compiler_params=pltpu.CompilerParams(vmem_limit_bytes=mib << 20),
            cost_estimate=pl.CostEstimate(flops=int(us * 1.1e9), transcendentals=0, bytes_accessed=1000),
            name=name,
        )(*placed)

    return run


def pack_att_kernel(bits_ref, wq, wk, wv, wo, bqv, att_ref, send_ref):
    n = wo.shape[0]
    att_ref[0:n, :] = wq[...]
    att_ref[n : 2 * n, :] = wk[...]
    att_ref[2 * n : 3 * n, :] = wv[...]
    att_ref[3 * n : 4 * n, :] = wo[...]
    rows = att_ref.shape[0] - 4 * n
    att_ref[4 * n :, :] = jnp.zeros_like(att_ref[4 * n :, :])
    att_ref[4 * n :, 0 : 3 * n] = jnp.broadcast_to(bqv[...], (rows, 3 * n))
    size = send_ref.shape[0]
    send_ref[...] = att_ref[pl.ds(pl.multiple_of(bits_ref[3] * size, 16), size), :]


def pack_ffn_kernel(bits_ref, win, bin_, wout, in_ref, out_ref, in_send, out_send):
    x = bits_ref[0]
    units = win.shape[1] // 2
    size = units + PAD
    for piece in range(2):
        take = pl.multiple_of((x if piece == 0 else 1 - x) * units, 128)
        base = piece * size
        in_ref[base : base + units, :] = win[:, pl.ds(take, units)].T
        in_ref[base + units : base + size, :] = jnp.zeros((PAD, in_ref.shape[1]), BF16)
        in_ref[base + units : base + size, 0:units] = jnp.broadcast_to(
            bin_[:, pl.ds(take, units)], (PAD, units)
        )
        out_ref[piece * units : (piece + 1) * units, :] = wout[pl.ds(take, units), :]
    in_send[...] = in_ref[0:size, :]
    out_send[...] = out_ref[0:units, :]


def key_rows(length, ones):
    row = lax.broadcasted_iota(jnp.int32, (PAD, SEQ), 0)
    pos = lax.broadcasted_iota(jnp.int32, (PAD, SEQ), 1)
    base = jnp.where((row >= 1) & (row <= ones), 1.0, 0.0)
    return jnp.where((row == 0) & (pos >= length), NEG, base).astype(BF16)


def split_rows(first, value):
    row = lax.broadcasted_iota(jnp.int32, (PAD, SEQ), 0)
    high = value.astype(BF16).astype(F32)
    middle = (value - high).astype(BF16).astype(F32)
    lower = value - high - middle
    out = jnp.where(row == 0, first, 0.0)
    for i, part in enumerate((high, middle, lower)):
        out = jnp.where(row == i + 1, part, out)
    return out.astype(BF16)


def stack(*parts):
    return jnp.concatenate(parts, axis=0)


def attention_forward(len_ref, x_ref, packs, qkv_ref, ctx_ref, lse_ref, stat_ref, per, slot):
    length = len_ref[pl.program_id(0)]
    scale = LOG2E / math.sqrt(HEAD)
    n = per * HEAD

    @pl.when(pl.program_id(0) == 0)
    def _():
        stat_ref[...] = jnp.zeros_like(stat_ref)

    keys = key_rows(length, 0)
    ones = jnp.ones((PAD, SEQ), BF16)
    x = x_ref[...]
    for r, w in enumerate(packs):
        bias = column(w[4 * n : 4 * n + 1, 0 : 3 * n].astype(F32))
        qkv_ref[3 * n * r : 3 * n * (r + 1), :] = (mm_nt(w[0 : 3 * n, :], x) + bias).astype(BF16)

    def scores(i):
        a = 3 * n * (i // per) + (i % per) * HEAD
        q = stack(qkv_ref[a : a + HEAD, :], ones)
        k = stack(qkv_ref[n + a : n + a + HEAD, :], keys)
        return mm_tn(k, q)

    heads = per * len(packs)
    following = scores(0)
    for i in range(heads):
        s = following
        if i + 1 < heads:
            following = scores(i + 1)
        top = jnp.max(s, axis=0, keepdims=True)
        e = jnp.exp2(s * scale - top * scale).astype(BF16)
        a = 3 * n * (i // per) + (i % per) * HEAD
        c = mm(stack(qkv_ref[2 * n + a : 2 * n + a + HEAD, :], ones), e)
        total = c[HEAD : HEAD + 1, :]
        ctx_ref[i * HEAD : (i + 1) * HEAD, :] = (c[0:HEAD, :] * (1.0 / total)).astype(BF16)
        lse_ref[i : i + 1, :] = top + jnp.log2(total) * (1.0 / scale)
    sums = mm_nt(jnp.ones((8, SEQ), BF16), ctx_ref[...])
    stat_ref[2:3, slot * n : (slot + len(packs)) * n] += sums[0:1, :]


def attend_first_kernel(len_ref, x_ref, w0, qkv_ref, ctx_ref, lse_ref, stat_ref, *, per):
    attention_forward(len_ref, x_ref, (w0,), qkv_ref, ctx_ref, lse_ref, stat_ref, per, 0)
    stat_ref[0:1, :] += jnp.sum(x_ref[...].astype(F32), axis=0, keepdims=True)


def attend_next_kernel(len_ref, x_ref, w0, qkv_ref, ctx_ref, lse_ref, stat_ref, *, per):
    attention_forward(len_ref, x_ref, (w0,), qkv_ref, ctx_ref, lse_ref, stat_ref, per, 1)


def normalise(v):
    mean = jnp.mean(v, axis=-1, keepdims=True)
    centred = v - mean
    inv = lax.rsqrt(jnp.mean(centred * centred, axis=-1, keepdims=True) + EPS_NORM)
    return centred * inv, inv


def attend_last_kernel(
    len_ref, bits_ref, x_ref, p0, p1, p2, p3, q0, q1, q2, q3, wa, wb, ctxa_ref, ctxb_ref, vec_ref,
    qkv_ref, ctx_ref, lse_ref, stat_ref, pack_ref, norm_ref, inv_ref, low_ref,
    wo_scr, all_scr, *, per
):
    n = per * HEAD

    @pl.when(pl.program_id(0) == 0)
    def _():
        size = p0.shape[0]
        for r, group in enumerate(((p0, p1, p2, p3), (q0, q1, q2, q3))):
            for k, ref in enumerate(group):
                start = pl.multiple_of(jnp.bitwise_xor(bits_ref[3], k) * size, 16)
                pack_ref[r, pl.ds(start, size), :] = ref[...]
        for r, w in enumerate((wa, wb, pack_ref.at[0], pack_ref.at[1])):
            wo_scr[r * n : (r + 1) * n, :] = w[3 * n : 4 * n, :]

    packs = (pack_ref.at[0], pack_ref.at[1])
    attention_forward(len_ref, x_ref, packs, qkv_ref, ctx_ref, lse_ref, stat_ref, per, 2)
    all_scr[0:n, :] = ctxa_ref[...]
    all_scr[n : 2 * n, :] = ctxb_ref[...]
    all_scr[2 * n : 4 * n, :] = ctx_ref[...]
    pre = mm_tn(all_scr[...], wo_scr[...]) + vec_ref[0:1, :] + x_ref[...].astype(F32)
    normal, inv = normalise(pre)
    norm_ref[...] = normal
    inv_ref[...] = jnp.broadcast_to(inv, inv_ref.shape)
    first = normal * vec_ref[1:2, :] + vec_ref[2:3, :]
    low_ref[...] = first.astype(BF16)
    stat_ref[1:2, :] += jnp.sum(first, axis=0, keepdims=True)


def gelu_pair(u):
    cdf = 0.5 * lax.erf(u * (1.0 / math.sqrt(2.0))) + 0.5
    density = jnp.exp2(u * u * (-0.5 * LOG2E)) * (1.0 / math.sqrt(2.0 * math.pi))
    return u * cdf, cdf + u * density


def join(ins, outs, wi, wo, bias, units):
    for i in range(2):
        part = slice(i * units, (i + 1) * units)
        wi[part, :] = ins[i][0:units, :]
        wo[part, :] = outs[i][...]
        if bias is not None:
            bias[:, part] = ins[i][units : units + 8, 0:units].astype(F32)


def feed_forward(low, groups, hid_ref, slope_ref, stat_ref, wi, wo, bias, units, slot):
    @pl.when(pl.program_id(0) == 0)
    def _():
        for g, (ins, outs) in enumerate(groups):
            join(ins, outs, wi.at[g], wo.at[g], bias.at[g], units)
        stat_ref[...] = jnp.zeros_like(stat_ref)

    out = None
    for g in range(len(groups)):
        pre = mm_nt(low, wi[g]) + bias[g, 0:1, :]
        hidden, slope = gelu_pair(pre)
        cols = slice(2 * units * g, 2 * units * (g + 1))
        sums = jnp.sum(hidden, axis=0, keepdims=True)
        piece = slice(units * g, units * (g + 1))
        stat_ref[slot : slot + 1, piece] += sums[:, 0:units]
        stat_ref[slot + 1 : slot + 2, piece] += sums[:, units : 2 * units]
        hidden = hidden.astype(BF16)
        hid_ref[:, cols] = hidden
        slope_ref[:, cols] = slope.astype(BF16)
        part = mm(hidden, wo[g])
        out = part if out is None else out + part
    return out


def ffn_near_kernel(
    low_ref, i0, o0, i1, o1, i2, o2, i3, o3, hid_ref, slope_ref, stat_ref, out_ref, wi, wo, bias, *, units
):
    groups = (((i0, i1), (o0, o1)), ((i2, i3), (o2, o3)))
    out_ref[...] = feed_forward(
        low_ref[...], groups, hid_ref, slope_ref, stat_ref, wi, wo, bias, units, 3
    )


def ffn_far_kernel(
    len_ref, low_ref, i0, o0, i1, o1, i2, o2, i3, o3, prev_ref, norm_ref, vec_ref, s0, s1, s2, s3,
    hid_ref, slope_ref, bundle_ref, out_ref, norm2_ref, inv2_ref, pool_ref, stat_ref, wi, wo, bias,
    *, units, blocks, share
):
    step = pl.program_id(0)
    sent, block = step // blocks, step % blocks
    groups = (((i0, i1), (o0, o1)), ((i2, i3), (o2, o3)))
    ffn = feed_forward(low_ref[...], groups, hid_ref, slope_ref, stat_ref, wi, wo, bias, units, 5)
    first = norm_ref[...] * vec_ref[1:2, :] + vec_ref[2:3, :]
    normal, inv = normalise(ffn + prev_ref[...] + vec_ref[3:4, :] + first)
    norm2_ref[...] = normal.astype(BF16)
    inv2_ref[...] = jnp.broadcast_to(inv, inv2_ref.shape)
    second = normal * vec_ref[4:5, :] + vec_ref[5:6, :]
    out_ref[...] = second.astype(BF16)
    rows = low_ref.shape[0]
    position = block * rows + lax.broadcasted_iota(jnp.int32, (rows, 1), 0)
    part = jnp.sum(jnp.where(position < len_ref[sent], second, 0.0), axis=0, keepdims=True)

    @pl.when(step == 0)
    def _():
        pool_ref[...] = jnp.zeros_like(pool_ref)

    pool_ref[pl.ds(sent, 1), :] += part / len_ref[sent].astype(F32)

    @pl.when(step == pl.num_programs(0) - 1)
    def _():
        bundle_ref[0:8, :] = share * (stat_ref[...] + s0[...] + s1[...] + s2[...] + s3[...])
        pool = pool_ref[...]
        unit = pool * lax.rsqrt(jnp.sum(pool * pool, axis=1, keepdims=True) + EPS_UNIT)
        count = bundle_ref.shape[0] - 8
        bundle_ref[8 : 8 + count, :] = unit[0:count, :]


def loss_kernel(
    len_ref, bits_ref, *refs, micro, blocks, fields
):
    unit_refs = refs[:blocks]
    (pool_ref, member_ref, norm_ref, inv_ref, vec_ref, dlow_ref, sums_ref, grad_scr) = refs[blocks:]
    step = pl.program_id(0)

    @pl.when(step == 0)
    def _():
        high = lax.Precision.HIGHEST
        units = jnp.concatenate([ref[...] for ref in unit_refs], axis=0)
        count = units.shape[0]
        sents = count // micro
        me = bits_ref[1]
        row = lax.broadcasted_iota(jnp.int32, (count, count), 0)
        col = lax.broadcasted_iota(jnp.int32, (count, count), 1)
        source = jnp.where(col // sents == row % micro, col % sents, -1)
        mask = jnp.zeros_like(row)
        for shift, largest, unit in fields:
            field = jnp.bitwise_and(lax.shift_right_logical(row // micro, shift), largest)
            mask = jnp.bitwise_xor(mask, field * unit)
        pick = (source == jnp.bitwise_xor(me, mask)).astype(F32)
        member = dot(pick, member_ref[...].astype(F32), 1, 0)
        same = dot(member, member, 1, 1)
        own = row == col
        apart = own | (row % micro != col % micro)
        positive = jnp.where(apart, 0.0, same)
        logits = COS_SCALE * dot(units, units, 1, 1, high)
        others = jnp.where(apart, NEG, logits)
        top = jnp.max(others, axis=1, keepdims=True)
        raised = jnp.exp(others - top)
        total = jnp.sum(raised, axis=1, keepdims=True)
        chosen = raised * positive
        total_pos = jnp.sum(chosen, axis=1, keepdims=True)
        each = jnp.log(total) - jnp.log(total_pos)
        loss = jnp.sum(each[0:micro], axis=0, keepdims=True)
        dlogits = raised / total - chosen / total_pos
        both = dlogits[0:micro, :] + dlogits.T[0:micro, :]
        dunits = COS_SCALE * dot(both, units, 1, 0, high)
        pooled = pool_ref[0:micro, :]
        rscale = lax.rsqrt(jnp.sum(pooled * pooled, axis=1, keepdims=True) + EPS_UNIT)
        unit = pooled * rscale
        grad_scr[0:micro, :] = rscale * (dunits - unit * jnp.sum(unit * dunits, axis=1, keepdims=True))
        sums_ref[...] = jnp.zeros_like(sums_ref)
        sums_ref[6:7, :] = jnp.broadcast_to(loss, (1, sums_ref.shape[1]))

    length = len_ref[step]
    spread = grad_scr[pl.ds(step, 1), :] * (1.0 / length.astype(F32))
    normal = norm_ref[...].astype(F32)
    g = spread * vec_ref[4:5, :]
    valid = lax.broadcasted_iota(jnp.int32, (SEQ, 1), 0) < length
    along = jnp.mean(g * normal, axis=1, keepdims=True)
    dpre = jnp.where(valid, inv_ref[:, 0:1] * (g - jnp.mean(g) - normal * along), 0.0)
    dlow_ref[...] = dpre.astype(BF16)
    sums_ref[3:4, :] += jnp.sum(dpre, axis=0, keepdims=True)
    sums_ref[4:5, :] += spread * jnp.sum(jnp.where(valid, normal, 0.0), axis=0, keepdims=True)
    sums_ref[5:6, :] += spread * length.astype(F32)


def ffn_back(dlow, low, hid_ref, slope_ref, outs, wo, acc, gb_ref, units, row):
    @pl.when(pl.program_id(0) == 0)
    def _():
        for i in range(2):
            wo[i * units : (i + 1) * units, :] = outs[i][...]
        acc[...] = jnp.zeros_like(acc)
        gb_ref[...] = jnp.zeros_like(gb_ref)

    di = mm_nt(dlow, wo[...]) * slope_ref[...].astype(F32)
    gb_ref[row : row + 1, :] += jnp.sum(di, axis=0, keepdims=True)
    dil = di.astype(BF16)
    acc[1] += mm_tn(hid_ref[...], dlow)
    acc[0] += mm_tn(dil, low)
    return dil


def centre_ffn(keep_ref, send_ref, acc, gb_ref, mean_ref, bsum, units, rows, row):
    for i, (r, g_ref) in enumerate(zip(rows, (keep_ref, send_ref))):
        part = slice(i * units, (i + 1) * units)
        g_ref[0:units, :] = (acc[0, part, :] - column(gb_ref[row : row + 1, part]) * mean_ref[1:2, :]).astype(BF16)
        centre = column(mean_ref[r[0] : r[0] + 1, r[1] : r[1] + units])
        g_ref[units : 2 * units, :] = (acc[1, part, :] - centre * bsum).astype(BF16)


def ffn_back_kernel(*refs, units, rows, row, parts, own, last):
    take = iter(refs)
    more = lambda count: [next(take) for _ in range(count)]
    dlow_ref, low_ref, hid_ref, slope_ref, o0, o1, mean_ref, bsum_ref = more(8)
    part_refs = more(parts)
    pieces = more(2 * (parts + own))
    prev_ref = next(take) if own else None
    norm_ref, inv_ref, vec_ref = more(3) if last else (None,) * 3
    keep_ref, send_ref, gb_ref = more(3)
    di_ref = None if own else next(take)
    dattn_ref, sums_ref = more(2) if last else (None,) * 2
    sum_ref = next(take) if parts + own and not last else None
    wo, acc = more(2)
    wi = next(take) if parts + own else None

    @pl.when(pl.program_id(0) == 0)
    def _():
        if last:
            sums_ref[...] = jnp.zeros_like(sums_ref)
        for i, ref in enumerate(pieces):
            wi[i * units : (i + 1) * units, :] = ref[0:units, :]

    dil = ffn_back(
        dlow_ref[...], low_ref[...], hid_ref, slope_ref, (o0, o1), wo, acc, gb_ref, units, row
    )
    if di_ref is not None:
        di_ref[...] = dil
    if parts + own:
        dfirst = prev_ref[...] if own else dlow_ref[...].astype(F32)
        for i, part in enumerate([ref[...] for ref in part_refs] + ([dil] if own else [])):
            dfirst = dfirst + mm(part, wi[2 * units * i : 2 * units * (i + 1), :])
        if not last:
            sum_ref[...] = dfirst
    if last:
        normal = norm_ref[...]
        g = dfirst * vec_ref[1:2, :]
        along = jnp.mean(g * normal, axis=1, keepdims=True)
        dpre = inv_ref[:, 0:1] * (g - jnp.mean(g, axis=1, keepdims=True) - normal * along)
        dattn_ref[...] = dpre.astype(BF16)
        sums_ref[0:1, :] += jnp.sum(dpre, axis=0, keepdims=True)
        sums_ref[1:2, :] += jnp.sum(dfirst * normal, axis=0, keepdims=True)
        sums_ref[2:3, :] += jnp.sum(dfirst, axis=0, keepdims=True)

    @pl.when(pl.program_id(0) == pl.num_programs(0) - 1)
    def _():
        centre_ffn(keep_ref, send_ref, acc, gb_ref, mean_ref, bsum_ref[3:4, :], units, rows, row)


def attend_back_kernel(
    len_ref, x_ref, dattn_ref, w_ref, qkv_ref, ctx_ref, lse_ref, mean_ref, bsum_ref,
    g_ref, gb_ref, grad_ref, acc, *, per, base, place
):
    step = pl.program_id(0)
    n = per * HEAD

    @pl.when(step == 0)
    def _():
        acc[...] = jnp.zeros_like(acc)
        gb_ref[...] = jnp.zeros_like(gb_ref)

    inv_root = 1.0 / math.sqrt(HEAD)
    scale = LOG2E * inv_root
    keys = key_rows(len_ref[step], 3)
    row = lax.broadcasted_iota(jnp.int32, (PAD, SEQ), 0)
    ones = jnp.where((row >= 1) & (row <= 3), 1.0, 0.0).astype(BF16)
    x = x_ref[...]
    dattn = dattn_ref[...]
    dctx = mm_nt(w_ref[3 * n : 4 * n, :], dattn).astype(BF16)
    acc[3 * n : 4 * n, :] += mm(ctx_ref[...], dattn)
    for h in range(per):
        c = h * HEAD
        q = qkv_ref[c : c + HEAD, :]
        k = qkv_ref[n + c : n + c + HEAD, :]
        v = qkv_ref[2 * n + c : 2 * n + c + HEAD, :]
        do = dctx[c : c + HEAD, :]
        o = ctx_ref[c : c + HEAD, :]
        lse = lse_ref[base * per + h : base * per + h + 1, :]
        weighted = jnp.sum(o.astype(F32) * do.astype(F32), axis=0, keepdims=True)
        s = mm_tn(stack(k, keys), stack(q, split_rows(1.0, -lse)))
        p = jnp.exp2(s * scale)
        dp = mm_tn(stack(v, ones), stack(do, split_rows(0.0, -weighted)))
        ds = (p * dp).astype(BF16)
        grad_ref[2 * n + c : 2 * n + c + HEAD, :] = mm_nt(do, p.astype(BF16)).astype(BF16)
        grad_ref[n + c : n + c + HEAD, :] = (mm_nt(q, ds) * inv_root).astype(BF16)
        grad_ref[c : c + HEAD, :] = (mm(k, ds) * inv_root).astype(BF16)
    grads = grad_ref[...]
    gb_ref[place : place + 1, 0 : 3 * n] += mm_nt(jnp.ones((8, SEQ), BF16), grads)[0:1, :]
    acc[0 : 3 * n, :] += mm(grads, x)

    @pl.when(step == pl.num_programs(0) - 1)
    def _():
        g_ref[0 : 3 * n, :] = (acc[0 : 3 * n, :] - column(gb_ref[place : place + 1, 0 : 3 * n]) * mean_ref[0:1, :]).astype(BF16)
        centre = column(mean_ref[2:3, place * n : (place + 1) * n])
        g_ref[3 * n : 4 * n, :] = (acc[3 * n : 4 * n, :] - centre * bsum_ref[0:1, :]).astype(BF16)


def input_grad_kernel(prev_ref, g0, g1, g2, g3, w0, w1, w2, w3, out_ref):
    out = prev_ref[...].astype(F32)
    for g, w in ((g0, w0), (g1, w1), (g2, w2), (g3, w3)):
        out = out + mm_tn(g[...], w[0 : g.shape[0], :])
    out_ref[...] = out


def ffn_final_kernel(bits_ref, in0, in1, out0, out1, small_ref, mean_ref, gin_ref, gout_ref):
    units = in0.shape[0]
    for p, (a, b) in enumerate(((in0, out0), (in1, out1))):
        spot = bits_ref[0] if p == 0 else 1 - bits_ref[0]
        spot = pl.multiple_of(spot * units, 128)
        part = slice(p * units, (p + 1) * units)
        grad = a[...].astype(F32) + column(small_ref[12 + p : 13 + p, 0:units]) * mean_ref[1:2, :]
        gin_ref[:, pl.ds(spot, units)] = grad.T
        gout_ref[pl.ds(spot, units), :] = (
            b[...].astype(F32) + column(mean_ref[3:4, part]) * small_ref[3:4, :]
        )


def fence(*values):
    return lax.optimization_barrier(values)


def shards(
    inputs, lengths, membership, w_query, b_query, w_key, w_value, b_value, w_output, b_output,
    gain_first, bias_first, w_inner, b_inner, w_outer, b_outer, gain_second, bias_second,
):
    total = lax.axis_size("dp") * lax.axis_size("mp")
    mp = lax.axis_index("mp")
    dp = lax.axis_index("dp")
    me = dp * lax.axis_size("mp") + mp
    xbit = dp % 2

    def flip(value, mask):
        return lax.ppermute(value, ("dp", "mp"), [(i, i ^ mask) for i in range(total)])

    def flip_hbm(value, mask):
        return flip(pltpu.with_memory_space_constraint(value, pltpu.HBM), mask)

    def ordered(a, b, axis=0):
        return jnp.where(xbit == 0, jnp.concatenate([a, b], axis), jnp.concatenate([b, a], axis))

    micro, own, width = inputs.shape
    rows = micro * own
    n = w_query.shape[1]
    per = n // HEAD
    units = w_inner.shape[1] // 2
    att_rows = 4 * n + 64
    att_piece = att_rows // 4
    in_size = units + PAD

    rest = 2 * XBIT
    zbit = (me // rest) % 2
    if 2 * rest < total:
        zbit = (zbit + (me // (2 * rest)) % 2) % 2
    bits = jnp.stack([xbit, me, zbit, 2 * xbit + (me // rest) % 2]).astype(jnp.int32)
    sent_lengths = lax.dynamic_slice_in_dim(lengths, mp, 1, 1).reshape(-1)
    x = inputs.reshape(rows, width)
    vectors = jnp.stack(
        [b_output, gain_first, bias_first, b_outer, gain_second, bias_second, b_outer, b_outer]
    ).astype(F32)

    row_block = lambda r, c: ((r, c), lambda s, *_: (s, 0))
    sent_block = lambda a: ((None, a, SEQ), lambda s, *_: (s, 0, 0))
    piece = lambda r, p: ((r, width), lambda s, *_: (p, 0))

    att_own, att_send = call(
        pack_att_kernel, (1,), [None] * 5,
        [((att_rows, width), BF16), ((att_piece, width), BF16)],
        prefetch=1, name="pack_att", us=2, mib=14, keep=(1,),
    )(bits, w_query.T, w_key.T, w_value.T, w_output,
      jnp.concatenate([b_query, jnp.zeros_like(b_query), b_value])[None])
    att_own, att_send, x, w_inner = fence(att_own, att_send, x, w_inner)

    def attn_outs(count):
        return [
            ((micro, 3 * n * count, SEQ), BF16, *sent_block(3 * n * count)),
            ((micro, n * count, SEQ), BF16, *sent_block(n * count)),
            ((micro, per * count, SEQ), F32, *sent_block(per * count)),
            ((8, width), F32),
        ]

    att_0 = flip(att_send, YBIT)
    att_sib = flip_hbm(att_own, CORE)
    in_own, out_own, in_send, out_send = call(
        pack_ffn_kernel, (1,), [None] * 3,
        [
            ((2 * in_size, width), BF16), ((2 * units, width), BF16),
            ((in_size, width), BF16), ((units, width), BF16),
        ],
        prefetch=1, name="pack_ffn", us=3, mib=16, keep=(2, 3),
    )(bits, w_inner, b_inner[None], w_outer)
    att_0, att_sib, x, in_own, out_own, in_send, out_send = fence(
        att_0, att_sib, x, in_own, out_own, in_send, out_send
    )
    att_2 = flip(att_0, XBIT)
    att_1 = flip(att_0, rest)
    in_y = flip(in_send, YBIT)
    sib_0 = flip(att_0, CORE)
    rows_out = ((rows, width), F32, *row_block(SEQ, width))
    qkv_0, ctx_0, lse_0, stat_0 = call(
        functools.partial(attend_first_kernel, per=per), (micro,),
        [row_block(SEQ, width), None], attn_outs(1),
        prefetch=1, name="attend_own", mib=60, held=(0,),
    )(sent_lengths, x, att_own)
    att_1, att_2, sib_0, x, qkv_0, ctx_0, lse_0, stat_0 = fence(
        att_1, att_2, sib_0, x, qkv_0, ctx_0, lse_0, stat_0
    )
    att_3 = flip(att_1, XBIT)
    sib_1 = flip(att_1, CORE)
    sib_2 = flip(att_2, CORE)
    qkv_1, ctx_1, lse_1, stat_1 = call(
        functools.partial(attend_next_kernel, per=per), (micro,),
        [row_block(SEQ, width), None], attn_outs(1),
        prefetch=1, name="attend_sibling", mib=60, held=(0, 1),
    )(sent_lengths, x, att_sib)
    att_3, sib_1, sib_2, in_y, x, qkv_1, ctx_1, lse_1, stat_1, in_own, out_own = fence(
        att_3, sib_1, sib_2, in_y, x, qkv_1, ctx_1, lse_1, stat_1, in_own, out_own
    )
    sib_3 = flip(att_3, CORE)
    in_x = flip(in_y, XBIT)
    out_y = flip(out_send, YBIT)
    in_sib = flip_hbm(in_own, CORE)
    out_sib = flip_hbm(out_own, CORE)
    qkv_b, ctx_b, lse_b, stat_2, att_far, norm1, inv1, low = call(
        functools.partial(attend_last_kernel, per=per), (micro,),
        [row_block(SEQ, width)] + [None] * 10 + [sent_block(n), sent_block(n), None],
        attn_outs(2) + [
            ((2, att_rows, width), BF16),
            rows_out,
            ((rows, 128), F32, *row_block(SEQ, 128)),
            ((rows, width), BF16, *row_block(SEQ, width)),
        ],
        scratch=[pltpu.VMEM((4 * n, width), BF16), pltpu.VMEM((4 * n, SEQ), BF16)],
        prefetch=2, name="attend_far", us=14, mib=60, held=tuple(range(9)) + (10,),
    )(
        sent_lengths, bits, x, att_0, att_1, att_2, att_3, sib_0, sib_1, sib_2, sib_3, att_own, att_sib,
        ctx_0, ctx_1, vectors,
    )
    low, norm1, inv1, in_x, out_y, in_sib, out_sib, in_y = fence(
        low, norm1, inv1, in_x, out_y, in_sib, out_sib, in_y
    )

    out_x = flip(out_y, XBIT)
    in_y_sib = flip(in_y, CORE)
    in_x_sib = flip(in_x, CORE)
    out_y_sib = flip(out_y, CORE)
    block = 256
    steps = rows // block
    ffn_outs = [
        ((rows, 4 * units), BF16, *row_block(block, 4 * units)),
        ((rows, 4 * units), BF16, *row_block(block, 4 * units)),
    ]
    ffn_scratch = [
        pltpu.VMEM((2, 2 * units, width), BF16),
        pltpu.VMEM((2, 2 * units, width), BF16),
        pltpu.VMEM((2, 8, 2 * units), F32),
    ]
    near_specs = []
    near = []
    for p in range(2):
        near_specs += [piece(in_size, p), piece(units, p)] * 2
        near += [in_own, out_own, in_sib, out_sib]
    hid_near, slope_near, stat_3, ffn_a = call(
        functools.partial(ffn_near_kernel, units=units), (steps,),
        [row_block(block, width)] + near_specs,
        ffn_outs + [((8, width), F32), ((rows, width), F32, *row_block(block, width))],
        scratch=ffn_scratch, name="ffn_near", mib=60, held=(3, 4, 7, 8),
    )(low, *near)
    out_x, in_x_sib, out_y_sib, in_y_sib, ffn_a, hid_near, slope_near, stat_3 = fence(
        out_x, in_x_sib, out_y_sib, in_y_sib, ffn_a, hid_near, slope_near, stat_3
    )
    out_x_sib = flip(out_x, CORE)

    far = [in_y, out_y, in_y_sib, out_y_sib, in_x, out_x, in_x_sib, out_x_sib]
    hid_far, slope_far, bundle, out_rows, norm2, inv2, pooled = call(
        functools.partial(
            ffn_far_kernel, units=units, blocks=SEQ // block, share=1.0 / (rows * total)
        ), (steps,),
        [row_block(block, width)] + [None] * 8
        + [row_block(block, width), row_block(block, width)] + [None] * 5,
        ffn_outs + [
            ((8 + micro, width), F32),
            ((rows, width), BF16, *row_block(block, width)),
            ((rows, width), BF16, *row_block(block, width)),
            ((rows, 128), F32, *row_block(block, 128)),
            ((8, width), F32),
        ],
        scratch=[pltpu.VMEM((8, width), F32)] + ffn_scratch, prefetch=1, name="ffn_far", mib=60, held=(1, 2, 3, 4, 5, 6, 7, 8),
    )(sent_lengths, low, *far, ffn_a, norm1, vectors, stat_0, stat_1, stat_2, stat_3)

    def rows_in(v, order):
        return [v[i : i + 1] for i in order]

    def other_means(v, mask):
        if mask == XBIT:
            rows = jnp.concatenate([v[3:7, units : 2 * units], v[3:7, :units]], axis=1)
            return jnp.concatenate([v[0:3], rows, v[7:8]], axis=0)
        order = (1, 0, 3, 2) if mask == CORE else (2, 3, 0, 1)
        slots = jnp.concatenate([v[2:3, i * n : (i + 1) * n] for i in order], axis=1)
        return jnp.concatenate([v[0:2], slots] + rows_in(v, [3 + i for i in order]) + [v[7:8]], axis=0)

    def groups_of(first, last):
        found, mask = [], first
        while mask < last:
            found.append((mask, 2 * mask, 3 * mask) if 2 * mask < last else (mask,))
            mask *= 4
        return found

    mp_stages, x_stages, z_stages = groups_of(1, XBIT), [(XBIT,)], [(rest,)]
    if 2 * rest < total:
        z_stages += [(2 * rest,)] + groups_of(4 * rest, total)

    def sum_step(v, masks, reorder):
        parts = [v]
        for m in masks:
            part = flip(v, m)
            for single in (CORE, YBIT, XBIT):
                if m & single:
                    part = reorder(part, single)
            parts.append(part)
        while len(parts) > 1:
            parts = [parts[i] + parts[i + 1] for i in range(0, len(parts), 2)]
        return parts[0]

    stages = z_stages + mp_stages + x_stages
    fields, shift = [], 0
    for index, masks in enumerate(stages):
        others = [flip(bundle, m) for m in masks]
        parts = [bundle[0:8]]
        for m, other in zip(masks, others):
            part = other[0:8]
            for single in (CORE, YBIT, XBIT):
                if m & single:
                    part = other_means(part, single)
            parts.append(part)
        while len(parts) > 1:
            parts = [parts[i] + parts[i + 1] for i in range(0, len(parts), 2)]
        mine = parts[0]
        unit_blocks = [bundle[8:]] + [o[8:] for o in others]
        fields.append((shift, len(masks), masks[0]))
        shift += (len(masks) + 1) // 2
        if index < len(stages) - 1:
            bundle = jnp.concatenate([mine] + unit_blocks, axis=0)
    means = mine

    dlow, sums2 = call(
        functools.partial(loss_kernel, micro=micro, blocks=len(unit_blocks), fields=fields), (micro,),
        [None] * (len(unit_blocks) + 2) + [row_block(SEQ, width), row_block(SEQ, 128), None],
        [
            ((rows, width), BF16, *row_block(SEQ, width)),
            ((8, width), F32),
        ],
        scratch=[pltpu.VMEM((8, width), F32)], prefetch=2, name="loss", mib=28,
    )(sent_lengths, bits, *unit_blocks, pooled, membership.reshape(-1, membership.shape[2]), norm2, inv2, vectors)

    back_rows = SEQ

    def ffn_part(half, p, dlow, row, parts=(), pieces=(), own=False, prev=None, last=False):
        hidden, slope, arrays, specs, base = half
        part = lambda s, *_: (s, p)
        block_of = lambda c: row_block(back_rows, c)
        ins = [block_of(width), block_of(width)] + [((back_rows, 2 * units), part)] * 2
        ins += [specs[1], specs[3], None, None] + [block_of(2 * units)] * len(parts)
        args = [dlow, low, hidden, slope, arrays[1], arrays[3], means, sums2, *parts]
        free = [4, 5] + list(range(len(args), len(args) + len(pieces)))
        ins += [spec for _, spec in pieces]
        args += [a for a, _ in pieces]
        places = ((base, p * units), (base + 1, p * units))
        outs = [((2 * units, width), BF16)] * 2 + [((8, 2 * units), F32)]
        scratch = [pltpu.VMEM((2 * units, width), BF16), pltpu.VMEM((2, 2 * units, width), F32)]
        rows_f32 = ((rows, width), F32, *block_of(width))
        if not own:
            outs += [((rows, 2 * units), BF16, *block_of(2 * units))]
        if own:
            ins += [block_of(width)]
            args += [prev]
        if pieces:
            scratch += [pltpu.VMEM((len(pieces) * units, width), BF16)]
        if last:
            ins += [block_of(width), block_of(128), None]
            args += [norm1, inv1, vectors]
            outs += [((rows, width), BF16, *block_of(width)), ((8, width), F32)]
        elif pieces:
            outs += [rows_f32]
        return call(
            functools.partial(
                ffn_back_kernel, units=units, rows=places, row=row, parts=len(parts), own=own, last=last
            ),
            (rows // back_rows,), ins, outs, scratch=scratch, name="ffn_back",
            us=8 + 2 * len(pieces), mib=44, keep=(0, 1), held=free,
        )(*args)

    near_half = lambda p: (
        hid_near, slope_near, near[0:4], [piece(in_size, p), piece(units, p)] * 2, 3
    )
    far_half = lambda p: (hid_far, slope_far, far[4 * p : 4 * p + 4], [None] * 4, 5)

    def add(*values):
        out = values[0].astype(F32)
        for v in values[1:]:
            out = out + v.astype(F32)
        return out.astype(BF16)

    def rest_split(a, mask):
        half = a.shape[0] // 2
        bit = (me // mask) % 2
        if 2 * mask < total:
            bit = (bit + (me // (2 * mask)) % 2) % 2
        keep = lax.dynamic_slice_in_dim(a, bit * half, half, 0)
        send = lax.dynamic_slice_in_dim(a, (1 - bit) * half, half, 0)
        return bit, keep, send

    def rest_finish(bit, part, mask):
        inner = mask * 2
        while inner < total:
            part = add(part, flip(part, inner | mask if inner == 2 * mask else inner))
            inner *= 2
        other = flip(part, mask)
        return jnp.where(
            bit == 0, jnp.concatenate([part, other], 0), jnp.concatenate([other, part], 0)
        )

    def merged(bit, mine, other):
        return jnp.where(
            bit == 0, jnp.concatenate([mine, other], 0), jnp.concatenate([other, mine], 0)
        )

    def inner_flip(a):
        return flip(a, 3 * rest) if 2 * rest < total else jnp.zeros_like(a)

    def inner_rest(a):
        mask = 4 * rest
        while mask < total:
            a = add(a, flip(a, mask))
            mask *= 2
        return a

    full, part = units, units // 2
    top, bottom = slice(0, full), slice(full, 2 * full)

    def halves(a, bit):
        half = a.shape[0] // 2
        kept = lax.dynamic_slice_in_dim(a, bit * half, half, 0)
        return kept, lax.dynamic_slice_in_dim(a, (1 - bit) * half, half, 0)

    def halves_z(a):
        return halves(a, zbit)

    far_in = lambda p: [(far[4 * p], None), (far[4 * p + 2], None)]
    near_in = lambda p: [(near[0], piece(in_size, p)), (near[2], piece(in_size, p))]
    k_f1, s_f1, gb_f1, di_f1 = ffn_part(far_half(1), 1, dlow, 7)
    c_f1 = flip(s_f1, CORE)
    f1a = add(k_f1[top], c_f1[top])
    f1a, c_f1, k_f1, dlow = fence(f1a, c_f1, k_f1, dlow)

    y1a = flip(f1a, YBIT)
    k_f0, s_f0, gb_f0, di_f0, acc = ffn_part(
        far_half(0), 0, dlow, 6, (di_f1,), far_in(1)
    )
    f1b = add(k_f1[bottom], c_f1[bottom])
    y1a, f1b, k_f0, s_f0, gb_f0, di_f0, acc, dlow = fence(
        y1a, f1b, k_f0, s_f0, gb_f0, di_f0, acc, dlow
    )

    y1b = flip(f1b, YBIT)
    c_f0 = flip(s_f0, CORE)
    k_n1, s_n1, gb_n1, acc = ffn_part(
        near_half(1), 1, dlow, 5, (di_f0,), far_in(0) + near_in(1), own=True, prev=acc
    )
    y1b, c_f0, k_n1, s_n1, gb_n1, acc, dlow = fence(y1b, c_f0, k_n1, s_n1, gb_n1, acc, dlow)
    c_n1 = flip(s_n1, CORE)
    f0a = add(k_f0[top], c_f0[top])
    c_n1, f0a, dlow, k_f0, c_f0 = fence(c_n1, f0a, dlow, k_f0, c_f0)
    y0a = flip(f0a, YBIT)
    s1a = add(k_n1[top], c_n1[top], y1a)
    s1b = add(k_n1[bottom], c_n1[bottom], y1b)
    s1a, s1b, dlow = fence(s1a, s1b, dlow)

    x1a = flip(s1a, XBIT)
    x1b = flip(s1b, XBIT)
    k_n0, s_n0, gb_n0, dattn, sums1 = ffn_part(
        near_half(0), 0, dlow, 4, (), near_in(0), own=True, prev=acc, last=True
    )
    f0b = add(k_f0[bottom], c_f0[bottom])
    y0a, x1a, k_n0, s_n0, gb_n0, dattn, sums1, f0b = fence(
        y0a, x1a, k_n0, s_n0, gb_n0, dattn, sums1, f0b
    )
    def other_sums(v, mask):
        if mask == CORE:
            ffn = jnp.concatenate([v[8:16, units : 2 * units], v[8:16, :units]], axis=1)
            return jnp.concatenate([v[:8], ffn] + rows_in(v, (17, 16, 19, 18)) + [v[20:24]], axis=0)
        if mask == YBIT:
            order = (14, 15, 12, 13)
            return jnp.concatenate([v[:12]] + rows_in(v, order + (18, 19, 16, 17)) + [v[20:24]], axis=0)
        return jnp.concatenate([v[:12]] + rows_in(v, (13, 12, 15, 14)) + [v[16:24]], axis=0)

    def sums_step(v, mask):
        return sum_step(v, (mask,), other_sums) if mask < total else v

    c_n0 = flip(s_n0, CORE)
    keep_a, send_a = halves_z(add(k_n0[top], c_n0[top], y0a, x1a))
    keep_a, send_a, c_n0, dattn, f0b = fence(keep_a, send_a, c_n0, dattn, f0b)

    def attend_part(w, qkv, ctx, lse, base, place, dattn):
        w_spec = None if w.ndim == 2 else ((None, att_rows, width), lambda s, *_: (base, 0, 0))
        quarter_block = lambda a: ((None, a, SEQ), lambda s, *_: (s, base, 0))
        return call(
            functools.partial(attend_back_kernel, per=per, base=base, place=place), (micro,),
            [
                row_block(SEQ, width), row_block(SEQ, width), w_spec, quarter_block(3 * n),
                quarter_block(n), sent_block(lse.shape[1]), None, None,
            ],
            [
                ((4 * n, width), BF16), ((8, width), F32),
                ((micro, 3 * n, SEQ), BF16, *sent_block(3 * n)),
            ],
            scratch=[pltpu.VMEM((4 * n, width), F32)],
            prefetch=1, name="attend_back", mib=24, keep=(0,),
            held=() if w is not att_sib else (2,),
        )(sent_lengths, x, dattn, w, qkv, ctx, lse, means, sums1)

    y0b = flip(f0b, YBIT)
    z_a = flip(send_a, rest)
    g_3, gb_3, dq_3 = attend_part(att_far, qkv_b, ctx_b, lse_b, 1, 3, dattn)
    y0b, x1b, z_a, g_3, gb_3, dq_3, dattn = fence(
        y0b, x1b, z_a, g_3, gb_3, dq_3, dattn
    )
    keep_b, send_b = halves_z(add(k_n0[bottom], c_n0[bottom], y0b, x1b))
    r_a = add(keep_a, z_a)
    r_a, send_b, keep_b, g_3, dattn = fence(r_a, send_b, keep_b, g_3, dattn)

    i_a = inner_flip(r_a)
    z_b = flip(send_b, rest)
    c_3 = flip(g_3, CORE)
    g_2, gb_2, dq_2 = attend_part(att_far, qkv_b, ctx_b, lse_b, 0, 2, dattn)
    c_3, i_a, z_b, g_2, gb_2, dq_2, dattn = fence(
        c_3, i_a, z_b, g_2, gb_2, dq_2, dattn
    )
    af_a = add(g_2[top], c_3[top])
    r_a = inner_rest(add(r_a, i_a))
    r_b = add(keep_b, z_b)
    af_a, g_2, c_3, r_a, r_b, dattn = fence(af_a, g_2, c_3, r_a, r_b, dattn)

    y_afa = flip(af_a, YBIT)
    z_a = flip(r_a, rest)
    i_b = inner_flip(r_b)
    g_1, gb_1, dq_1 = attend_part(att_sib, qkv_1, ctx_1, lse_1, 0, 1, dattn)
    af_b = add(g_2[bottom], c_3[bottom])
    y_afa, i_b, z_a, g_1, gb_1, dq_1, dattn, af_b = fence(
        y_afa, i_b, z_a, g_1, gb_1, dq_1, dattn, af_b
    )
    r_in = merged(zbit, r_a, z_a)
    r_b = inner_rest(add(r_b, i_b))
    r_in, r_b, g_1, dattn, af_b = fence(r_in, r_b, g_1, dattn, af_b)

    y_afb = flip(af_b, YBIT)
    c_1 = flip(g_1, CORE)
    r_in_x = flip(r_in, XBIT)
    z_b = flip(r_b, rest)
    g_0, gb_0, dq_0 = attend_part(att_own, qkv_0, ctx_0, lse_0, 0, 0, dattn)
    y_afb, c_1, r_in_x, z_b, g_0, gb_0, dq_0, dattn = fence(
        y_afb, c_1, r_in_x, z_b, g_0, gb_0, dq_0, dattn
    )
    sums = jnp.concatenate(
        [sums1 + sums2, gb_n0 + gb_n1 + gb_f0 + gb_f1, gb_0 + gb_1 + gb_2 + gb_3], axis=0
    )
    sums = sums_step(sums, CORE)

    t_keep, t_send = halves(add(g_0[top], c_1[top], y_afa), xbit)
    b_keep, b_send = halves_z(add(g_0[bottom], c_1[bottom], y_afb))
    r_out = merged(zbit, r_b, z_b)
    t_send, b_send, t_keep, b_keep, r_out, dattn, sums = fence(
        t_send, b_send, t_keep, b_keep, r_out, dattn, sums
    )
    t_x = flip(t_send, XBIT)
    b_z = flip(b_send, rest)
    sums = sums_step(sums, YBIT)
    second = lambda i: ((None, att_rows, width), lambda s, *_: (i, 0, 0))
    (dx,) = call(
        input_grad_kernel, (2 * micro,),
        [row_block(SEQ // 2, width)]
        + [((None, 3 * n, SEQ // 2), lambda s, *_: (s // 2, 0, s % 2))] * 4
        + [None, None, second(0), second(1)],
        [((rows, width), F32, *row_block(SEQ // 2, width))], name="input_grad", mib=28, held=(6,),
    )(dattn, dq_0, dq_1, dq_2, dq_3, att_own, att_sib, att_far, att_far)

    t_x, b_z, dx, sums, r_out = fence(t_x, b_z, dx, sums, r_out)
    t2_keep, t2_send = halves_z(add(t_keep, t_x))
    b2_keep, b2_send = halves(add(b_keep, b_z), xbit)
    t2_send, b2_send, t2_keep, b2_keep, sums = fence(t2_send, b2_send, t2_keep, b2_keep, sums)
    t2_z = flip(t2_send, rest)
    b2_x = flip(b2_send, XBIT)
    sums = sums_step(sums, rest)
    t2_z, b2_x, sums, r_out = fence(t2_z, b2_x, sums, r_out)
    r_out_x = flip(r_out, XBIT)
    t2 = add(t2_keep, t2_z)
    b2 = add(b2_keep, b2_x)
    t2, b2, sums = fence(t2, b2, sums)
    t2_i = inner_flip(t2)
    b2_i = inner_flip(b2)
    sums = sums_step(sums, XBIT)
    t2_i, b2_i, sums, r_out_x = fence(t2_i, b2_i, sums, r_out_x)
    t2 = inner_rest(add(t2, t2_i))
    b2 = inner_rest(add(b2, b2_i))
    t2, b2, sums = fence(t2, b2, sums)
    t2_z = flip(t2, rest)
    b2_x = flip(b2, XBIT)
    sums = sums_step(sums, 2 * rest)
    mask = 4 * rest
    while mask < total:
        sums = sums_step(sums, mask)
        mask *= 2
    t2_z, b2_x, sums = fence(t2_z, b2_x, sums)
    t1 = merged(zbit, t2, t2_z)
    b1 = merged(xbit, b2, b2_x)
    t1, b1, sums = fence(t1, b1, sums)
    t1_x = flip(t1, XBIT)
    b1_z = flip(b1, rest)
    grad_inner, grad_outer = call(
        ffn_final_kernel, (1,), [None] * 6, [((width, 2 * units), F32), ((2 * units, width), F32)],
        prefetch=1, name="ffn_final", mib=20, held=range(4),
    )(bits, r_in, r_in_x, r_out, r_out_x, sums, means)
    t1_x, b1_z, grad_inner, grad_outer = fence(t1_x, b1_z, grad_inner, grad_outer)

    shared = sums[0:8]
    b_att = sums[16, : 3 * n]
    grad_binner = ordered(sums[12, :units], sums[13, :units])
    g_top = ordered(t1, t1_x).astype(F32)
    g_bottom = merged(zbit, b1, b1_z).astype(F32)
    outer = lambda a, b: b_att[a:b, None] * means[0][None]
    grad_wout = g_bottom[n:] + means[2, :n][:, None] * shared[0][None]

    return (
        out_rows.reshape(micro, own, width),
        sums[6, 0],
        dx.reshape(micro, own, width),
        (g_top[:n] + outer(0, n)).T,
        b_att[:n],
        (g_top[n:] + outer(n, 2 * n)).T,
        (g_bottom[:n] + outer(2 * n, 3 * n)).T,
        b_att[2 * n :],
        grad_wout,
        shared[0],
        shared[1],
        shared[2],
        grad_inner,
        grad_binner,
        grad_outer,
        shared[3],
        shared[4],
        shared[5],
    )


def solution(mesh):
    rows = P(None, ("dp", "mp"), None)
    cols = P(None, "mp")
    split = P("mp")
    whole = P()
    placed = (rows, P(None, "dp"), whole, cols, split, cols, cols, split, P("mp", None))
    placed += (whole, whole, whole, cols, split, P("mp", None), whole, whole, whole)
    results = (rows, whole, rows, cols, split, cols, cols, split, P("mp", None))
    results += (whole, whole, whole, cols, split, P("mp", None), whole, whole, whole)
    return jax.shard_map(shards, mesh=mesh, in_specs=placed, out_specs=results, check_vma=False)
```

```python
import functools
import math

import jax
import jax.numpy as jnp
from jax import lax
from jax.experimental import pallas as pl
from jax.experimental.pallas import tpu as pltpu
from jax.sharding import PartitionSpec as P

HEAD = 64
SEQ = 512
EPS_NORM = 1e-5
EPS_UNIT = 1e-6
COS_SCALE = 20.0
LOG2E = 1.4426950408889634
NEG = -1e30
F32 = jnp.float32
BF16 = jnp.bfloat16
CORE, YBIT, XBIT = 1, 2, 4
PAD = 16


def dot(a, b, ca, cb, precision=None):
    return lax.dot_general(
        a, b, (((ca,), (cb,)), ((), ())), preferred_element_type=F32, precision=precision
    )


def mm(a, b):
    return dot(a, b, 1, 0)


def mm_nt(a, b):
    return dot(a, b, 1, 1)


def mm_tn(a, b):
    return dot(a, b, 0, 0)


def column(row):
    return jnp.broadcast_to(row, (8, row.shape[1])).T[:, :1]


def call(kernel, grid, ins, outs, scratch=(), prefetch=0, name=None, us=7, mib=44, keep=(), held=()):
    def spec(block, index):
        return pl.BlockSpec(block, index)

    def whole(a, **mode):
        rank = len(a)
        return pl.BlockSpec(tuple(a), lambda *_: (0,) * rank, **mode)

    def run(*args):
        in_specs, placed = [], list(args[:prefetch])
        for i, (item, arg) in enumerate(zip(ins, args[prefetch:])):
            big = arg.size > 1 << 16
            single = {"pipeline_mode": pl.Buffered(1)} if big else {}
            in_specs.append(whole(arg.shape, **single) if item is None else spec(*item))
            placed.append(
                pltpu.with_memory_space_constraint(arg, pltpu.HBM) if big and i not in held else arg
            )
        out_specs = [whole(o[0]) if len(o) == 2 else spec(*o[2:]) for o in outs]
        shapes = []
        for i, o in enumerate(outs):
            if i in keep:
                shapes.append(pltpu.VMEM(o[0], o[1]))
            elif math.prod(o[0]) > 1 << 16:
                shapes.append(pltpu.HBM(o[0], o[1]))
            else:
                shapes.append(jax.ShapeDtypeStruct(o[0], o[1]))
        return pl.pallas_call(
            kernel,
            out_shape=shapes,
            grid_spec=pltpu.PrefetchScalarGridSpec(
                num_scalar_prefetch=prefetch,
                grid=grid,
                in_specs=in_specs,
                out_specs=out_specs,
                scratch_shapes=list(scratch),
            ),
            compiler_params=pltpu.CompilerParams(vmem_limit_bytes=mib << 20),
            cost_estimate=pl.CostEstimate(flops=int(us * 1.1e9), transcendentals=0, bytes_accessed=1000),
            name=name,
        )(*placed)

    return run


def pack_att_kernel(bits_ref, wq, wk, wv, wo, bqv, att_ref, send_ref):
    n = wo.shape[0]
    att_ref[0:n, :] = wq[...]
    att_ref[n : 2 * n, :] = wk[...]
    att_ref[2 * n : 3 * n, :] = wv[...]
    att_ref[3 * n : 4 * n, :] = wo[...]
    rows = att_ref.shape[0] - 4 * n
    att_ref[4 * n :, :] = jnp.zeros_like(att_ref[4 * n :, :])
    att_ref[4 * n :, 0 : 3 * n] = jnp.broadcast_to(bqv[...], (rows, 3 * n))
    size = send_ref.shape[0]
    send_ref[...] = att_ref[pl.ds(pl.multiple_of(bits_ref[3] * size, 16), size), :]


def pack_ffn_kernel(bits_ref, win, bin_, wout, in_ref, out_ref, in_send, out_send):
    x = bits_ref[0]
    units = win.shape[1] // 2
    size = units + PAD
    for piece in range(2):
        take = pl.multiple_of((x if piece == 0 else 1 - x) * units, 128)
        base = piece * size
        in_ref[base : base + units, :] = win[:, pl.ds(take, units)].T
        in_ref[base + units : base + size, :] = jnp.zeros((PAD, in_ref.shape[1]), BF16)
        in_ref[base + units : base + size, 0:units] = jnp.broadcast_to(
            bin_[:, pl.ds(take, units)], (PAD, units)
        )
        out_ref[piece * units : (piece + 1) * units, :] = wout[pl.ds(take, units), :]
    in_send[...] = in_ref[0:size, :]
    out_send[...] = out_ref[0:units, :]


def key_rows(length, ones):
    row = lax.broadcasted_iota(jnp.int32, (PAD, SEQ), 0)
    pos = lax.broadcasted_iota(jnp.int32, (PAD, SEQ), 1)
    base = jnp.where((row >= 1) & (row <= ones), 1.0, 0.0)
    return jnp.where((row == 0) & (pos >= length), NEG, base).astype(BF16)


def split_rows(first, value):
    row = lax.broadcasted_iota(jnp.int32, (PAD, SEQ), 0)
    high = value.astype(BF16).astype(F32)
    middle = (value - high).astype(BF16).astype(F32)
    lower = value - high - middle
    out = jnp.where(row == 0, first, 0.0)
    for i, part in enumerate((high, middle, lower)):
        out = jnp.where(row == i + 1, part, out)
    return out.astype(BF16)


def stack(*parts):
    return jnp.concatenate(parts, axis=0)


def attention_forward(len_ref, x_ref, packs, qkv_ref, ctx_ref, lse_ref, stat_ref, per, slot):
    length = len_ref[pl.program_id(0)]
    scale = LOG2E / math.sqrt(HEAD)
    n = per * HEAD

    @pl.when(pl.program_id(0) == 0)
    def _():
        stat_ref[...] = jnp.zeros_like(stat_ref)

    keys = key_rows(length, 0)
    ones = jnp.ones((PAD, SEQ), BF16)
    x = x_ref[...]
    for r, w in enumerate(packs):
        bias = column(w[4 * n : 4 * n + 1, 0 : 3 * n].astype(F32))
        qkv_ref[3 * n * r : 3 * n * (r + 1), :] = (mm_nt(w[0 : 3 * n, :], x) + bias).astype(BF16)

    def scores(i):
        a = 3 * n * (i // per) + (i % per) * HEAD
        q = stack(qkv_ref[a : a + HEAD, :], ones)
        k = stack(qkv_ref[n + a : n + a + HEAD, :], keys)
        return mm_tn(k, q)

    heads = per * len(packs)
    following = scores(0)
    for i in range(heads):
        s = following
        if i + 1 < heads:
            following = scores(i + 1)
        top = jnp.max(s, axis=0, keepdims=True)
        e = jnp.exp2(s * scale - top * scale).astype(BF16)
        a = 3 * n * (i // per) + (i % per) * HEAD
        c = mm(stack(qkv_ref[2 * n + a : 2 * n + a + HEAD, :], ones), e)
        total = c[HEAD : HEAD + 1, :]
        ctx_ref[i * HEAD : (i + 1) * HEAD, :] = (c[0:HEAD, :] * (1.0 / total)).astype(BF16)
        lse_ref[i : i + 1, :] = top + jnp.log2(total) * (1.0 / scale)
    sums = mm_nt(jnp.ones((8, SEQ), BF16), ctx_ref[...])
    stat_ref[2:3, slot * n : (slot + len(packs)) * n] += sums[0:1, :]


def attend_first_kernel(len_ref, x_ref, w0, qkv_ref, ctx_ref, lse_ref, stat_ref, *, per):
    attention_forward(len_ref, x_ref, (w0,), qkv_ref, ctx_ref, lse_ref, stat_ref, per, 0)
    stat_ref[0:1, :] += jnp.sum(x_ref[...].astype(F32), axis=0, keepdims=True)


def attend_next_kernel(len_ref, x_ref, w0, qkv_ref, ctx_ref, lse_ref, stat_ref, *, per):
    attention_forward(len_ref, x_ref, (w0,), qkv_ref, ctx_ref, lse_ref, stat_ref, per, 1)


def normalise(v):
    mean = jnp.mean(v, axis=-1, keepdims=True)
    centred = v - mean
    inv = lax.rsqrt(jnp.mean(centred * centred, axis=-1, keepdims=True) + EPS_NORM)
    return centred * inv, inv


def attend_last_kernel(
    len_ref, bits_ref, x_ref, p0, p1, p2, p3, q0, q1, q2, q3, wa, wb, ctxa_ref, ctxb_ref, vec_ref,
    qkv_ref, ctx_ref, lse_ref, stat_ref, pack_ref, norm_ref, inv_ref, low_ref,
    wo_scr, all_scr, *, per
):
    n = per * HEAD

    @pl.when(pl.program_id(0) == 0)
    def _():
        size = p0.shape[0]
        for r, group in enumerate(((p0, p1, p2, p3), (q0, q1, q2, q3))):
            for k, ref in enumerate(group):
                start = pl.multiple_of(jnp.bitwise_xor(bits_ref[3], k) * size, 16)
                pack_ref[r, pl.ds(start, size), :] = ref[...]
        for r, w in enumerate((wa, wb, pack_ref.at[0], pack_ref.at[1])):
            wo_scr[r * n : (r + 1) * n, :] = w[3 * n : 4 * n, :]

    packs = (pack_ref.at[0], pack_ref.at[1])
    attention_forward(len_ref, x_ref, packs, qkv_ref, ctx_ref, lse_ref, stat_ref, per, 2)
    all_scr[0:n, :] = ctxa_ref[...]
    all_scr[n : 2 * n, :] = ctxb_ref[...]
    all_scr[2 * n : 4 * n, :] = ctx_ref[...]
    pre = mm_tn(all_scr[...], wo_scr[...]) + vec_ref[0:1, :] + x_ref[...].astype(F32)
    normal, inv = normalise(pre)
    norm_ref[...] = normal
    inv_ref[...] = jnp.broadcast_to(inv, inv_ref.shape)
    first = normal * vec_ref[1:2, :] + vec_ref[2:3, :]
    low_ref[...] = first.astype(BF16)
    stat_ref[1:2, :] += jnp.sum(first, axis=0, keepdims=True)


def gelu_pair(u):
    cdf = 0.5 * lax.erf(u * (1.0 / math.sqrt(2.0))) + 0.5
    density = jnp.exp2(u * u * (-0.5 * LOG2E)) * (1.0 / math.sqrt(2.0 * math.pi))
    return u * cdf, cdf + u * density


def join(ins, outs, wi, wo, bias, units):
    for i in range(2):
        part = slice(i * units, (i + 1) * units)
        wi[part, :] = ins[i][0:units, :]
        wo[part, :] = outs[i][...]
        if bias is not None:
            bias[:, part] = ins[i][units : units + 8, 0:units].astype(F32)


def feed_forward(low, groups, hid_ref, slope_ref, stat_ref, wi, wo, bias, units, slot):
    @pl.when(pl.program_id(0) == 0)
    def _():
        for g, (ins, outs) in enumerate(groups):
            join(ins, outs, wi.at[g], wo.at[g], bias.at[g], units)
        stat_ref[...] = jnp.zeros_like(stat_ref)

    out = None
    for g in range(len(groups)):
        pre = mm_nt(low, wi[g]) + bias[g, 0:1, :]
        hidden, slope = gelu_pair(pre)
        cols = slice(2 * units * g, 2 * units * (g + 1))
        sums = jnp.sum(hidden, axis=0, keepdims=True)
        piece = slice(units * g, units * (g + 1))
        stat_ref[slot : slot + 1, piece] += sums[:, 0:units]
        stat_ref[slot + 1 : slot + 2, piece] += sums[:, units : 2 * units]
        hidden = hidden.astype(BF16)
        hid_ref[:, cols] = hidden
        slope_ref[:, cols] = slope.astype(BF16)
        part = mm(hidden, wo[g])
        out = part if out is None else out + part
    return out


def ffn_near_kernel(
    low_ref, i0, o0, i1, o1, i2, o2, i3, o3, hid_ref, slope_ref, stat_ref, out_ref, wi, wo, bias, *, units
):
    groups = (((i0, i1), (o0, o1)), ((i2, i3), (o2, o3)))
    out_ref[...] = feed_forward(
        low_ref[...], groups, hid_ref, slope_ref, stat_ref, wi, wo, bias, units, 3
    )


def ffn_far_kernel(
    len_ref, low_ref, i0, o0, i1, o1, i2, o2, i3, o3, prev_ref, norm_ref, vec_ref, s0, s1, s2, s3,
    hid_ref, slope_ref, bundle_ref, out_ref, norm2_ref, inv2_ref, pool_ref, stat_ref, wi, wo, bias,
    *, units, blocks, share
):
    step = pl.program_id(0)
    sent, block = step // blocks, step % blocks
    groups = (((i0, i1), (o0, o1)), ((i2, i3), (o2, o3)))
    ffn = feed_forward(low_ref[...], groups, hid_ref, slope_ref, stat_ref, wi, wo, bias, units, 5)
    first = norm_ref[...] * vec_ref[1:2, :] + vec_ref[2:3, :]
    normal, inv = normalise(ffn + prev_ref[...] + vec_ref[3:4, :] + first)
    norm2_ref[...] = normal.astype(BF16)
    inv2_ref[...] = jnp.broadcast_to(inv, inv2_ref.shape)
    second = normal * vec_ref[4:5, :] + vec_ref[5:6, :]
    out_ref[...] = second.astype(BF16)
    rows = low_ref.shape[0]
    position = block * rows + lax.broadcasted_iota(jnp.int32, (rows, 1), 0)
    part = jnp.sum(jnp.where(position < len_ref[sent], second, 0.0), axis=0, keepdims=True)

    @pl.when(step == 0)
    def _():
        pool_ref[...] = jnp.zeros_like(pool_ref)

    pool_ref[pl.ds(sent, 1), :] += part / len_ref[sent].astype(F32)

    @pl.when(step == pl.num_programs(0) - 1)
    def _():
        bundle_ref[0:8, :] = share * (stat_ref[...] + s0[...] + s1[...] + s2[...] + s3[...])
        pool = pool_ref[...]
        unit = pool * lax.rsqrt(jnp.sum(pool * pool, axis=1, keepdims=True) + EPS_UNIT)
        count = bundle_ref.shape[0] - 8
        bundle_ref[8 : 8 + count, :] = unit[0:count, :]


def loss_kernel(
    len_ref, bits_ref, *refs, micro, blocks, fields
):
    unit_refs = refs[:blocks]
    (pool_ref, member_ref, norm_ref, inv_ref, vec_ref, dlow_ref, sums_ref, grad_scr) = refs[blocks:]
    step = pl.program_id(0)

    @pl.when(step == 0)
    def _():
        high = lax.Precision.HIGHEST
        units = jnp.concatenate([ref[...] for ref in unit_refs], axis=0)
        count = units.shape[0]
        sents = count // micro
        me = bits_ref[1]
        row = lax.broadcasted_iota(jnp.int32, (count, count), 0)
        col = lax.broadcasted_iota(jnp.int32, (count, count), 1)
        source = jnp.where(col // sents == row % micro, col % sents, -1)
        mask = jnp.zeros_like(row)
        for shift, largest, unit in fields:
            field = jnp.bitwise_and(lax.shift_right_logical(row // micro, shift), largest)
            mask = jnp.bitwise_xor(mask, field * unit)
        pick = (source == jnp.bitwise_xor(me, mask)).astype(F32)
        member = dot(pick, member_ref[...].astype(F32), 1, 0)
        same = dot(member, member, 1, 1)
        own = row == col
        apart = own | (row % micro != col % micro)
        positive = jnp.where(apart, 0.0, same)
        logits = COS_SCALE * dot(units, units, 1, 1, high)
        others = jnp.where(apart, NEG, logits)
        top = jnp.max(others, axis=1, keepdims=True)
        raised = jnp.exp(others - top)
        total = jnp.sum(raised, axis=1, keepdims=True)
        chosen = raised * positive
        total_pos = jnp.sum(chosen, axis=1, keepdims=True)
        each = jnp.log(total) - jnp.log(total_pos)
        loss = jnp.sum(each[0:micro], axis=0, keepdims=True)
        dlogits = raised / total - chosen / total_pos
        both = dlogits[0:micro, :] + dlogits.T[0:micro, :]
        dunits = COS_SCALE * dot(both, units, 1, 0, high)
        pooled = pool_ref[0:micro, :]
        rscale = lax.rsqrt(jnp.sum(pooled * pooled, axis=1, keepdims=True) + EPS_UNIT)
        unit = pooled * rscale
        grad_scr[0:micro, :] = rscale * (dunits - unit * jnp.sum(unit * dunits, axis=1, keepdims=True))
        sums_ref[...] = jnp.zeros_like(sums_ref)
        sums_ref[6:7, :] = jnp.broadcast_to(loss, (1, sums_ref.shape[1]))

    length = len_ref[step]
    spread = grad_scr[pl.ds(step, 1), :] * (1.0 / length.astype(F32))
    normal = norm_ref[...].astype(F32)
    g = spread * vec_ref[4:5, :]
    valid = lax.broadcasted_iota(jnp.int32, (SEQ, 1), 0) < length
    along = jnp.mean(g * normal, axis=1, keepdims=True)
    dpre = jnp.where(valid, inv_ref[:, 0:1] * (g - jnp.mean(g) - normal * along), 0.0)
    dlow_ref[...] = dpre.astype(BF16)
    sums_ref[3:4, :] += jnp.sum(dpre, axis=0, keepdims=True)
    sums_ref[4:5, :] += spread * jnp.sum(jnp.where(valid, normal, 0.0), axis=0, keepdims=True)
    sums_ref[5:6, :] += spread * length.astype(F32)


def ffn_back(dlow, low, hid_ref, slope_ref, outs, wo, acc, gb_ref, units, row):
    @pl.when(pl.program_id(0) == 0)
    def _():
        for i in range(2):
            wo[i * units : (i + 1) * units, :] = outs[i][...]
        acc[...] = jnp.zeros_like(acc)
        gb_ref[...] = jnp.zeros_like(gb_ref)

    di = mm_nt(dlow, wo[...]) * slope_ref[...].astype(F32)
    gb_ref[row : row + 1, :] += jnp.sum(di, axis=0, keepdims=True)
    dil = di.astype(BF16)
    acc[1] += mm_tn(hid_ref[...], dlow)
    acc[0] += mm_tn(dil, low)
    return dil


def centre_ffn(keep_ref, send_ref, acc, gb_ref, mean_ref, bsum, units, rows, row):
    for i, (r, g_ref) in enumerate(zip(rows, (keep_ref, send_ref))):
        part = slice(i * units, (i + 1) * units)
        g_ref[0:units, :] = (acc[0, part, :] - column(gb_ref[row : row + 1, part]) * mean_ref[1:2, :]).astype(BF16)
        centre = column(mean_ref[r[0] : r[0] + 1, r[1] : r[1] + units])
        g_ref[units : 2 * units, :] = (acc[1, part, :] - centre * bsum).astype(BF16)


def ffn_back_kernel(*refs, units, rows, row, parts, own, last):
    take = iter(refs)
    more = lambda count: [next(take) for _ in range(count)]
    dlow_ref, low_ref, hid_ref, slope_ref, o0, o1, mean_ref, bsum_ref = more(8)
    part_refs = more(parts)
    pieces = more(2 * (parts + own))
    prev_ref = next(take) if own else None
    norm_ref, inv_ref, vec_ref = more(3) if last else (None,) * 3
    keep_ref, send_ref, gb_ref = more(3)
    di_ref = None if own else next(take)
    dattn_ref, sums_ref = more(2) if last else (None,) * 2
    sum_ref = next(take) if parts + own and not last else None
    wo, acc = more(2)
    wi = next(take) if parts + own else None

    @pl.when(pl.program_id(0) == 0)
    def _():
        if last:
            sums_ref[...] = jnp.zeros_like(sums_ref)
        for i, ref in enumerate(pieces):
            wi[i * units : (i + 1) * units, :] = ref[0:units, :]

    dil = ffn_back(
        dlow_ref[...], low_ref[...], hid_ref, slope_ref, (o0, o1), wo, acc, gb_ref, units, row
    )
    if di_ref is not None:
        di_ref[...] = dil
    if parts + own:
        dfirst = prev_ref[...] if own else dlow_ref[...].astype(F32)
        for i, part in enumerate([ref[...] for ref in part_refs] + ([dil] if own else [])):
            dfirst = dfirst + mm(part, wi[2 * units * i : 2 * units * (i + 1), :])
        if not last:
            sum_ref[...] = dfirst
    if last:
        normal = norm_ref[...]
        g = dfirst * vec_ref[1:2, :]
        along = jnp.mean(g * normal, axis=1, keepdims=True)
        dpre = inv_ref[:, 0:1] * (g - jnp.mean(g, axis=1, keepdims=True) - normal * along)
        dattn_ref[...] = dpre.astype(BF16)
        sums_ref[0:1, :] += jnp.sum(dpre, axis=0, keepdims=True)
        sums_ref[1:2, :] += jnp.sum(dfirst * normal, axis=0, keepdims=True)
        sums_ref[2:3, :] += jnp.sum(dfirst, axis=0, keepdims=True)

    @pl.when(pl.program_id(0) == pl.num_programs(0) - 1)
    def _():
        centre_ffn(keep_ref, send_ref, acc, gb_ref, mean_ref, bsum_ref[3:4, :], units, rows, row)


def attend_back_kernel(
    len_ref, x_ref, dattn_ref, w_ref, qkv_ref, ctx_ref, lse_ref, mean_ref, bsum_ref,
    g_ref, gb_ref, grad_ref, acc, dctx_scr, *, per, base, place
):
    step = pl.program_id(0)
    n = per * HEAD

    @pl.when(step == 0)
    def _():
        acc[...] = jnp.zeros_like(acc)
        gb_ref[...] = jnp.zeros_like(gb_ref)

    inv_root = 1.0 / math.sqrt(HEAD)
    scale = LOG2E * inv_root
    keys = key_rows(len_ref[step], 3)
    row = lax.broadcasted_iota(jnp.int32, (PAD, SEQ), 0)
    ones = jnp.where((row >= 1) & (row <= 3), 1.0, 0.0).astype(BF16)
    x = x_ref[...]
    dattn = dattn_ref[...]
    dctx_scr[...] = mm_nt(w_ref[3 * n : 4 * n, :], dattn).astype(BF16)
    acc[3 * n : 4 * n, :] += mm(ctx_ref[...], dattn)
    def head(h, carry):
        c = pl.multiple_of(h * HEAD, HEAD)
        rows_of = lambda ref, first: ref[pl.ds(pl.multiple_of(first + c, HEAD), HEAD), :]
        q, k, v = (rows_of(qkv_ref, i * n) for i in range(3))
        do = rows_of(dctx_scr, 0)
        o = rows_of(ctx_ref, 0)
        lse = lse_ref[pl.ds(base * per + h, 1), :]
        weighted = jnp.sum(o.astype(F32) * do.astype(F32), axis=0, keepdims=True)
        s = mm_tn(stack(k, keys), stack(q, split_rows(1.0, -lse)))
        p = jnp.exp2(s * scale)
        dp = mm_tn(stack(v, ones), stack(do, split_rows(0.0, -weighted)))
        ds = (p * dp).astype(BF16)
        grad_ref[pl.ds(pl.multiple_of(2 * n + c, HEAD), HEAD), :] = mm_nt(do, p.astype(BF16)).astype(BF16)
        grad_ref[pl.ds(pl.multiple_of(n + c, HEAD), HEAD), :] = (mm_nt(q, ds) * inv_root).astype(BF16)
        grad_ref[pl.ds(c, HEAD), :] = (mm(k, ds) * inv_root).astype(BF16)
        return carry

    lax.fori_loop(0, per, head, 0)
    grads = grad_ref[...]
    gb_ref[place : place + 1, 0 : 3 * n] += mm_nt(jnp.ones((8, SEQ), BF16), grads)[0:1, :]
    acc[0 : 3 * n, :] += mm(grads, x)

    @pl.when(step == pl.num_programs(0) - 1)
    def _():
        g_ref[0 : 3 * n, :] = (acc[0 : 3 * n, :] - column(gb_ref[place : place + 1, 0 : 3 * n]) * mean_ref[0:1, :]).astype(BF16)
        centre = column(mean_ref[2:3, place * n : (place + 1) * n])
        g_ref[3 * n : 4 * n, :] = (acc[3 * n : 4 * n, :] - centre * bsum_ref[0:1, :]).astype(BF16)


def input_grad_kernel(prev_ref, g0, g1, g2, g3, w0, w1, w2, w3, out_ref):
    out = prev_ref[...].astype(F32)
    for g, w in ((g0, w0), (g1, w1), (g2, w2), (g3, w3)):
        out = out + mm_tn(g[...], w[0 : g.shape[0], :])
    out_ref[...] = out


def ffn_final_kernel(bits_ref, in0, in1, out0, out1, small_ref, mean_ref, gin_ref, gout_ref):
    units = in0.shape[0]
    for p, (a, b) in enumerate(((in0, out0), (in1, out1))):
        spot = bits_ref[0] if p == 0 else 1 - bits_ref[0]
        spot = pl.multiple_of(spot * units, 128)
        part = slice(p * units, (p + 1) * units)
        grad = a[...].astype(F32) + column(small_ref[12 + p : 13 + p, 0:units]) * mean_ref[1:2, :]
        gin_ref[:, pl.ds(spot, units)] = grad.T
        gout_ref[pl.ds(spot, units), :] = (
            b[...].astype(F32) + column(mean_ref[3:4, part]) * small_ref[3:4, :]
        )


def fence(*values):
    return lax.optimization_barrier(values)


def shards(
    inputs, lengths, membership, w_query, b_query, w_key, w_value, b_value, w_output, b_output,
    gain_first, bias_first, w_inner, b_inner, w_outer, b_outer, gain_second, bias_second,
):
    total = lax.axis_size("dp") * lax.axis_size("mp")
    mp = lax.axis_index("mp")
    dp = lax.axis_index("dp")
    me = dp * lax.axis_size("mp") + mp
    xbit = dp % 2

    def flip(value, mask):
        return lax.ppermute(value, ("dp", "mp"), [(i, i ^ mask) for i in range(total)])

    def flip_hbm(value, mask):
        return flip(pltpu.with_memory_space_constraint(value, pltpu.HBM), mask)

    def ordered(a, b, axis=0):
        return jnp.where(xbit == 0, jnp.concatenate([a, b], axis), jnp.concatenate([b, a], axis))

    micro, own, width = inputs.shape
    rows = micro * own
    n = w_query.shape[1]
    per = n // HEAD
    units = w_inner.shape[1] // 2
    att_rows = 4 * n + 64
    att_piece = att_rows // 4
    in_size = units + PAD

    rest = 2 * XBIT
    zbit = (me // rest) % 2
    if 2 * rest < total:
        zbit = (zbit + (me // (2 * rest)) % 2) % 2
    bits = jnp.stack([xbit, me, zbit, 2 * xbit + (me // rest) % 2]).astype(jnp.int32)
    sent_lengths = lax.dynamic_slice_in_dim(lengths, mp, 1, 1).reshape(-1)
    x = inputs.reshape(rows, width)
    vectors = jnp.stack(
        [b_output, gain_first, bias_first, b_outer, gain_second, bias_second, b_outer, b_outer]
    ).astype(F32)

    row_block = lambda r, c: ((r, c), lambda s, *_: (s, 0))
    sent_block = lambda a: ((None, a, SEQ), lambda s, *_: (s, 0, 0))
    piece = lambda r, p: ((r, width), lambda s, *_: (p, 0))

    att_own, att_send = call(
        pack_att_kernel, (1,), [None] * 5,
        [((att_rows, width), BF16), ((att_piece, width), BF16)],
        prefetch=1, name="pack_att", us=2, mib=14, keep=(1,),
    )(bits, w_query.T, w_key.T, w_value.T, w_output,
      jnp.concatenate([b_query, jnp.zeros_like(b_query), b_value])[None])
    att_own, att_send, x, w_inner = fence(att_own, att_send, x, w_inner)

    def attn_outs(count):
        return [
            ((micro, 3 * n * count, SEQ), BF16, *sent_block(3 * n * count)),
            ((micro, n * count, SEQ), BF16, *sent_block(n * count)),
            ((micro, per * count, SEQ), F32, *sent_block(per * count)),
            ((8, width), F32),
        ]

    att_0 = flip(att_send, YBIT)
    att_sib = flip_hbm(att_own, CORE)
    in_own, out_own, in_send, out_send = call(
        pack_ffn_kernel, (1,), [None] * 3,
        [
            ((2 * in_size, width), BF16), ((2 * units, width), BF16),
            ((in_size, width), BF16), ((units, width), BF16),
        ],
        prefetch=1, name="pack_ffn", us=3, mib=16, keep=(2, 3),
    )(bits, w_inner, b_inner[None], w_outer)
    att_0, att_sib, x, in_own, out_own, in_send, out_send = fence(
        att_0, att_sib, x, in_own, out_own, in_send, out_send
    )
    att_2 = flip(att_0, XBIT)
    att_1 = flip(att_0, rest)
    in_y = flip(in_send, YBIT)
    sib_0 = flip(att_0, CORE)
    rows_out = ((rows, width), F32, *row_block(SEQ, width))
    qkv_0, ctx_0, lse_0, stat_0 = call(
        functools.partial(attend_first_kernel, per=per), (micro,),
        [row_block(SEQ, width), None], attn_outs(1),
        prefetch=1, name="attend_own", mib=60, held=(0,),
    )(sent_lengths, x, att_own)
    att_1, att_2, sib_0, x, qkv_0, ctx_0, lse_0, stat_0 = fence(
        att_1, att_2, sib_0, x, qkv_0, ctx_0, lse_0, stat_0
    )
    att_3 = flip(att_1, XBIT)
    sib_1 = flip(att_1, CORE)
    sib_2 = flip(att_2, CORE)
    qkv_1, ctx_1, lse_1, stat_1 = call(
        functools.partial(attend_next_kernel, per=per), (micro,),
        [row_block(SEQ, width), None], attn_outs(1),
        prefetch=1, name="attend_sibling", mib=60, held=(0, 1),
    )(sent_lengths, x, att_sib)
    att_3, sib_1, sib_2, in_y, x, qkv_1, ctx_1, lse_1, stat_1, in_own, out_own = fence(
        att_3, sib_1, sib_2, in_y, x, qkv_1, ctx_1, lse_1, stat_1, in_own, out_own
    )
    sib_3 = flip(att_3, CORE)
    in_x = flip(in_y, XBIT)
    out_y = flip(out_send, YBIT)
    in_sib = flip_hbm(in_own, CORE)
    out_sib = flip_hbm(out_own, CORE)
    qkv_b, ctx_b, lse_b, stat_2, att_far, norm1, inv1, low = call(
        functools.partial(attend_last_kernel, per=per), (micro,),
        [row_block(SEQ, width)] + [None] * 10 + [sent_block(n), sent_block(n), None],
        attn_outs(2) + [
            ((2, att_rows, width), BF16),
            rows_out,
            ((rows, 128), F32, *row_block(SEQ, 128)),
            ((rows, width), BF16, *row_block(SEQ, width)),
        ],
        scratch=[pltpu.VMEM((4 * n, width), BF16), pltpu.VMEM((4 * n, SEQ), BF16)],
        prefetch=2, name="attend_far", us=14, mib=60, held=tuple(range(9)) + (10,),
    )(
        sent_lengths, bits, x, att_0, att_1, att_2, att_3, sib_0, sib_1, sib_2, sib_3, att_own, att_sib,
        ctx_0, ctx_1, vectors,
    )
    low, norm1, inv1, in_x, out_y, in_sib, out_sib, in_y = fence(
        low, norm1, inv1, in_x, out_y, in_sib, out_sib, in_y
    )

    out_x = flip(out_y, XBIT)
    in_y_sib = flip(in_y, CORE)
    in_x_sib = flip(in_x, CORE)
    out_y_sib = flip(out_y, CORE)
    block = 256
    steps = rows // block
    ffn_outs = [
        ((rows, 4 * units), BF16, *row_block(block, 4 * units)),
        ((rows, 4 * units), BF16, *row_block(block, 4 * units)),
    ]
    ffn_scratch = [
        pltpu.VMEM((2, 2 * units, width), BF16),
        pltpu.VMEM((2, 2 * units, width), BF16),
        pltpu.VMEM((2, 8, 2 * units), F32),
    ]
    near_specs = []
    near = []
    for p in range(2):
        near_specs += [piece(in_size, p), piece(units, p)] * 2
        near += [in_own, out_own, in_sib, out_sib]
    hid_near, slope_near, stat_3, ffn_a = call(
        functools.partial(ffn_near_kernel, units=units), (steps,),
        [row_block(block, width)] + near_specs,
        ffn_outs + [((8, width), F32), ((rows, width), F32, *row_block(block, width))],
        scratch=ffn_scratch, name="ffn_near", mib=60, held=(3, 4, 7, 8),
    )(low, *near)
    out_x, in_x_sib, out_y_sib, in_y_sib, ffn_a, hid_near, slope_near, stat_3 = fence(
        out_x, in_x_sib, out_y_sib, in_y_sib, ffn_a, hid_near, slope_near, stat_3
    )
    out_x_sib = flip(out_x, CORE)

    far = [in_y, out_y, in_y_sib, out_y_sib, in_x, out_x, in_x_sib, out_x_sib]
    hid_far, slope_far, bundle, out_rows, norm2, inv2, pooled = call(
        functools.partial(
            ffn_far_kernel, units=units, blocks=SEQ // block, share=1.0 / (rows * total)
        ), (steps,),
        [row_block(block, width)] + [None] * 8
        + [row_block(block, width), row_block(block, width)] + [None] * 5,
        ffn_outs + [
            ((8 + micro, width), F32),
            ((rows, width), BF16, *row_block(block, width)),
            ((rows, width), BF16, *row_block(block, width)),
            ((rows, 128), F32, *row_block(block, 128)),
            ((8, width), F32),
        ],
        scratch=[pltpu.VMEM((8, width), F32)] + ffn_scratch, prefetch=1, name="ffn_far", mib=60, held=(1, 2, 3, 4, 5, 6, 7, 8),
    )(sent_lengths, low, *far, ffn_a, norm1, vectors, stat_0, stat_1, stat_2, stat_3)

    def rows_in(v, order):
        return [v[i : i + 1] for i in order]

    def other_means(v, mask):
        if mask == XBIT:
            rows = jnp.concatenate([v[3:7, units : 2 * units], v[3:7, :units]], axis=1)
            return jnp.concatenate([v[0:3], rows, v[7:8]], axis=0)
        order = (1, 0, 3, 2) if mask == CORE else (2, 3, 0, 1)
        slots = jnp.concatenate([v[2:3, i * n : (i + 1) * n] for i in order], axis=1)
        return jnp.concatenate([v[0:2], slots] + rows_in(v, [3 + i for i in order]) + [v[7:8]], axis=0)

    def groups_of(first, last):
        found, mask = [], first
        while mask < last:
            found.append((mask, 2 * mask, 3 * mask) if 2 * mask < last else (mask,))
            mask *= 4
        return found

    mp_stages, x_stages, z_stages = groups_of(1, XBIT), [(XBIT,)], [(rest,)]
    if 2 * rest < total:
        z_stages += [(2 * rest,)] + groups_of(4 * rest, total)

    def sum_step(v, masks, reorder):
        parts = [v]
        for m in masks:
            part = flip(v, m)
            for single in (CORE, YBIT, XBIT):
                if m & single:
                    part = reorder(part, single)
            parts.append(part)
        while len(parts) > 1:
            parts = [parts[i] + parts[i + 1] for i in range(0, len(parts), 2)]
        return parts[0]

    stages = z_stages + mp_stages + x_stages
    fields, shift = [], 0
    for index, masks in enumerate(stages):
        others = [flip(bundle, m) for m in masks]
        parts = [bundle[0:8]]
        for m, other in zip(masks, others):
            part = other[0:8]
            for single in (CORE, YBIT, XBIT):
                if m & single:
                    part = other_means(part, single)
            parts.append(part)
        while len(parts) > 1:
            parts = [parts[i] + parts[i + 1] for i in range(0, len(parts), 2)]
        mine = parts[0]
        unit_blocks = [bundle[8:]] + [o[8:] for o in others]
        fields.append((shift, len(masks), masks[0]))
        shift += (len(masks) + 1) // 2
        if index < len(stages) - 1:
            bundle = jnp.concatenate([mine] + unit_blocks, axis=0)
    means = mine

    dlow, sums2 = call(
        functools.partial(loss_kernel, micro=micro, blocks=len(unit_blocks), fields=fields), (micro,),
        [None] * (len(unit_blocks) + 2) + [row_block(SEQ, width), row_block(SEQ, 128), None],
        [
            ((rows, width), BF16, *row_block(SEQ, width)),
            ((8, width), F32),
        ],
        scratch=[pltpu.VMEM((8, width), F32)], prefetch=2, name="loss", mib=28,
    )(sent_lengths, bits, *unit_blocks, pooled, membership.reshape(-1, membership.shape[2]), norm2, inv2, vectors)

    back_rows = SEQ // 2

    def ffn_part(half, p, dlow, row, parts=(), pieces=(), own=False, prev=None, last=False):
        hidden, slope, arrays, specs, base = half
        part = lambda s, *_: (s, p)
        block_of = lambda c: row_block(back_rows, c)
        ins = [block_of(width), block_of(width)] + [((back_rows, 2 * units), part)] * 2
        ins += [specs[1], specs[3], None, None] + [block_of(2 * units)] * len(parts)
        args = [dlow, low, hidden, slope, arrays[1], arrays[3], means, sums2, *parts]
        free = [4, 5] + list(range(len(args), len(args) + len(pieces)))
        ins += [spec for _, spec in pieces]
        args += [a for a, _ in pieces]
        places = ((base, p * units), (base + 1, p * units))
        outs = [((2 * units, width), BF16)] * 2 + [((8, 2 * units), F32)]
        scratch = [pltpu.VMEM((2 * units, width), BF16), pltpu.VMEM((2, 2 * units, width), F32)]
        rows_f32 = ((rows, width), F32, *block_of(width))
        if not own:
            outs += [((rows, 2 * units), BF16, *block_of(2 * units))]
        if own:
            ins += [block_of(width)]
            args += [prev]
        if pieces:
            scratch += [pltpu.VMEM((len(pieces) * units, width), BF16)]
        if last:
            ins += [block_of(width), block_of(128), None]
            args += [norm1, inv1, vectors]
            outs += [((rows, width), BF16, *block_of(width)), ((8, width), F32)]
        elif pieces:
            outs += [rows_f32]
        return call(
            functools.partial(
                ffn_back_kernel, units=units, rows=places, row=row, parts=len(parts), own=own, last=last
            ),
            (rows // back_rows,), ins, outs, scratch=scratch, name="ffn_back",
            us=8 + 2 * len(pieces), mib=44, keep=(0, 1), held=free,
        )(*args)

    near_half = lambda p: (
        hid_near, slope_near, near[0:4], [piece(in_size, p), piece(units, p)] * 2, 3
    )
    far_half = lambda p: (hid_far, slope_far, far[4 * p : 4 * p + 4], [None] * 4, 5)

    def add(*values):
        out = values[0].astype(F32)
        for v in values[1:]:
            out = out + v.astype(F32)
        return out.astype(BF16)

    def rest_split(a, mask):
        half = a.shape[0] // 2
        bit = (me // mask) % 2
        if 2 * mask < total:
            bit = (bit + (me // (2 * mask)) % 2) % 2
        keep = lax.dynamic_slice_in_dim(a, bit * half, half, 0)
        send = lax.dynamic_slice_in_dim(a, (1 - bit) * half, half, 0)
        return bit, keep, send

    def rest_finish(bit, part, mask):
        inner = mask * 2
        while inner < total:
            part = add(part, flip(part, inner | mask if inner == 2 * mask else inner))
            inner *= 2
        other = flip(part, mask)
        return jnp.where(
            bit == 0, jnp.concatenate([part, other], 0), jnp.concatenate([other, part], 0)
        )

    def merged(bit, mine, other):
        return jnp.where(
            bit == 0, jnp.concatenate([mine, other], 0), jnp.concatenate([other, mine], 0)
        )

    def inner_flip(a):
        return flip(a, 3 * rest) if 2 * rest < total else jnp.zeros_like(a)

    def inner_rest(a):
        mask = 4 * rest
        while mask < total:
            a = add(a, flip(a, mask))
            mask *= 2
        return a

    full, part = units, units // 2
    top, bottom = slice(0, full), slice(full, 2 * full)

    def halves(a, bit):
        half = a.shape[0] // 2
        kept = lax.dynamic_slice_in_dim(a, bit * half, half, 0)
        return kept, lax.dynamic_slice_in_dim(a, (1 - bit) * half, half, 0)

    def halves_z(a):
        return halves(a, zbit)

    far_in = lambda p: [(far[4 * p], None), (far[4 * p + 2], None)]
    near_in = lambda p: [(near[0], piece(in_size, p)), (near[2], piece(in_size, p))]
    k_f1, s_f1, gb_f1, di_f1 = ffn_part(far_half(1), 1, dlow, 7)
    c_f1 = flip(s_f1, CORE)
    f1a = add(k_f1[top], c_f1[top])
    f1a, c_f1, k_f1, dlow = fence(f1a, c_f1, k_f1, dlow)

    y1a = flip(f1a, YBIT)
    k_f0, s_f0, gb_f0, di_f0, acc = ffn_part(
        far_half(0), 0, dlow, 6, (di_f1,), far_in(1)
    )
    f1b = add(k_f1[bottom], c_f1[bottom])
    y1a, f1b, k_f0, s_f0, gb_f0, di_f0, acc, dlow = fence(
        y1a, f1b, k_f0, s_f0, gb_f0, di_f0, acc, dlow
    )

    y1b = flip(f1b, YBIT)
    c_f0 = flip(s_f0, CORE)
    k_n1, s_n1, gb_n1, acc = ffn_part(
        near_half(1), 1, dlow, 5, (di_f0,), far_in(0) + near_in(1), own=True, prev=acc
    )
    y1b, c_f0, k_n1, s_n1, gb_n1, acc, dlow = fence(y1b, c_f0, k_n1, s_n1, gb_n1, acc, dlow)
    c_n1 = flip(s_n1, CORE)
    f0a = add(k_f0[top], c_f0[top])
    c_n1, f0a, dlow, k_f0, c_f0 = fence(c_n1, f0a, dlow, k_f0, c_f0)
    y0a = flip(f0a, YBIT)
    s1a = add(k_n1[top], c_n1[top], y1a)
    s1b = add(k_n1[bottom], c_n1[bottom], y1b)
    s1a, s1b, dlow = fence(s1a, s1b, dlow)

    x1a = flip(s1a, XBIT)
    x1b = flip(s1b, XBIT)
    k_n0, s_n0, gb_n0, dattn, sums1 = ffn_part(
        near_half(0), 0, dlow, 4, (), near_in(0), own=True, prev=acc, last=True
    )
    f0b = add(k_f0[bottom], c_f0[bottom])
    y0a, x1a, k_n0, s_n0, gb_n0, dattn, sums1, f0b = fence(
        y0a, x1a, k_n0, s_n0, gb_n0, dattn, sums1, f0b
    )
    def other_sums(v, mask):
        if mask == CORE:
            ffn = jnp.concatenate([v[8:16, units : 2 * units], v[8:16, :units]], axis=1)
            return jnp.concatenate([v[:8], ffn] + rows_in(v, (17, 16, 19, 18)) + [v[20:24]], axis=0)
        if mask == YBIT:
            order = (14, 15, 12, 13)
            return jnp.concatenate([v[:12]] + rows_in(v, order + (18, 19, 16, 17)) + [v[20:24]], axis=0)
        return jnp.concatenate([v[:12]] + rows_in(v, (13, 12, 15, 14)) + [v[16:24]], axis=0)

    def sums_step(v, mask):
        return sum_step(v, (mask,), other_sums) if mask < total else v

    c_n0 = flip(s_n0, CORE)
    keep_a, send_a = halves_z(add(k_n0[top], c_n0[top], y0a, x1a))
    keep_a, send_a, c_n0, dattn, f0b = fence(keep_a, send_a, c_n0, dattn, f0b)

    def attend_part(w, qkv, ctx, lse, base, place, dattn):
        w_spec = None if w.ndim == 2 else ((None, att_rows, width), lambda s, *_: (base, 0, 0))
        quarter_block = lambda a: ((None, a, SEQ), lambda s, *_: (s, base, 0))
        return call(
            functools.partial(attend_back_kernel, per=per, base=base, place=place), (micro,),
            [
                row_block(SEQ, width), row_block(SEQ, width), w_spec, quarter_block(3 * n),
                quarter_block(n), sent_block(lse.shape[1]), None, None,
            ],
            [
                ((4 * n, width), BF16), ((8, width), F32),
                ((micro, 3 * n, SEQ), BF16, *sent_block(3 * n)),
            ],
            scratch=[pltpu.VMEM((4 * n, width), F32), pltpu.VMEM((n, SEQ), BF16)],
            prefetch=1, name="attend_back", mib=24, keep=(0,),
            held=() if w is not att_sib else (2,),
        )(sent_lengths, x, dattn, w, qkv, ctx, lse, means, sums1)

    y0b = flip(f0b, YBIT)
    z_a = flip(send_a, rest)
    g_3, gb_3, dq_3 = attend_part(att_far, qkv_b, ctx_b, lse_b, 1, 3, dattn)
    y0b, x1b, z_a, g_3, gb_3, dq_3, dattn = fence(
        y0b, x1b, z_a, g_3, gb_3, dq_3, dattn
    )
    keep_b, send_b = halves_z(add(k_n0[bottom], c_n0[bottom], y0b, x1b))
    r_a = add(keep_a, z_a)
    r_a, send_b, keep_b, g_3, dattn = fence(r_a, send_b, keep_b, g_3, dattn)

    i_a = inner_flip(r_a)
    z_b = flip(send_b, rest)
    c_3 = flip(g_3, CORE)
    g_2, gb_2, dq_2 = attend_part(att_far, qkv_b, ctx_b, lse_b, 0, 2, dattn)
    c_3, i_a, z_b, g_2, gb_2, dq_2, dattn = fence(
        c_3, i_a, z_b, g_2, gb_2, dq_2, dattn
    )
    af_a = add(g_2[top], c_3[top])
    r_a = inner_rest(add(r_a, i_a))
    r_b = add(keep_b, z_b)
    af_a, g_2, c_3, r_a, r_b, dattn = fence(af_a, g_2, c_3, r_a, r_b, dattn)

    y_afa = flip(af_a, YBIT)
    z_a = flip(r_a, rest)
    i_b = inner_flip(r_b)
    g_1, gb_1, dq_1 = attend_part(att_sib, qkv_1, ctx_1, lse_1, 0, 1, dattn)
    af_b = add(g_2[bottom], c_3[bottom])
    y_afa, i_b, z_a, g_1, gb_1, dq_1, dattn, af_b = fence(
        y_afa, i_b, z_a, g_1, gb_1, dq_1, dattn, af_b
    )
    r_in = merged(zbit, r_a, z_a)
    r_b = inner_rest(add(r_b, i_b))
    r_in, r_b, g_1, dattn, af_b = fence(r_in, r_b, g_1, dattn, af_b)

    y_afb = flip(af_b, YBIT)
    c_1 = flip(g_1, CORE)
    r_in_x = flip(r_in, XBIT)
    z_b = flip(r_b, rest)
    g_0, gb_0, dq_0 = attend_part(att_own, qkv_0, ctx_0, lse_0, 0, 0, dattn)
    y_afb, c_1, r_in_x, z_b, g_0, gb_0, dq_0, dattn = fence(
        y_afb, c_1, r_in_x, z_b, g_0, gb_0, dq_0, dattn
    )
    sums = jnp.concatenate(
        [sums1 + sums2, gb_n0 + gb_n1 + gb_f0 + gb_f1, gb_0 + gb_1 + gb_2 + gb_3], axis=0
    )
    sums = sums_step(sums, CORE)

    t_keep, t_send = halves(add(g_0[top], c_1[top], y_afa), xbit)
    b_keep, b_send = halves_z(add(g_0[bottom], c_1[bottom], y_afb))
    r_out = merged(zbit, r_b, z_b)
    t_send, b_send, t_keep, b_keep, r_out, dattn, sums = fence(
        t_send, b_send, t_keep, b_keep, r_out, dattn, sums
    )
    t_x = flip(t_send, XBIT)
    b_z = flip(b_send, rest)
    sums = sums_step(sums, YBIT)
    second = lambda i: ((None, att_rows, width), lambda s, *_: (i, 0, 0))
    (dx,) = call(
        input_grad_kernel, (2 * micro,),
        [row_block(SEQ // 2, width)]
        + [((None, 3 * n, SEQ // 2), lambda s, *_: (s // 2, 0, s % 2))] * 4
        + [None, None, second(0), second(1)],
        [((rows, width), F32, *row_block(SEQ // 2, width))], name="input_grad", mib=28, held=(6,),
    )(dattn, dq_0, dq_1, dq_2, dq_3, att_own, att_sib, att_far, att_far)

    t_x, b_z, dx, sums, r_out = fence(t_x, b_z, dx, sums, r_out)
    t2_keep, t2_send = halves_z(add(t_keep, t_x))
    b2_keep, b2_send = halves(add(b_keep, b_z), xbit)
    t2_send, b2_send, t2_keep, b2_keep, sums = fence(t2_send, b2_send, t2_keep, b2_keep, sums)
    t2_z = flip(t2_send, rest)
    b2_x = flip(b2_send, XBIT)
    sums = sums_step(sums, rest)
    t2_z, b2_x, sums, r_out = fence(t2_z, b2_x, sums, r_out)
    r_out_x = flip(r_out, XBIT)
    t2 = add(t2_keep, t2_z)
    b2 = add(b2_keep, b2_x)
    t2, b2, sums = fence(t2, b2, sums)
    t2_i = inner_flip(t2)
    b2_i = inner_flip(b2)
    sums = sums_step(sums, XBIT)
    t2_i, b2_i, sums, r_out_x = fence(t2_i, b2_i, sums, r_out_x)
    t2 = inner_rest(add(t2, t2_i))
    b2 = inner_rest(add(b2, b2_i))
    t2, b2, sums = fence(t2, b2, sums)
    t2_z = flip(t2, rest)
    b2_x = flip(b2, XBIT)
    sums = sums_step(sums, 2 * rest)
    mask = 4 * rest
    while mask < total:
        sums = sums_step(sums, mask)
        mask *= 2
    t2_z, b2_x, sums = fence(t2_z, b2_x, sums)
    t1 = merged(zbit, t2, t2_z)
    b1 = merged(xbit, b2, b2_x)
    t1, b1, sums = fence(t1, b1, sums)
    t1_x = flip(t1, XBIT)
    b1_z = flip(b1, rest)
    grad_inner, grad_outer = call(
        ffn_final_kernel, (1,), [None] * 6, [((width, 2 * units), F32), ((2 * units, width), F32)],
        prefetch=1, name="ffn_final", mib=20, held=range(4),
    )(bits, r_in, r_in_x, r_out, r_out_x, sums, means)
    t1_x, b1_z, grad_inner, grad_outer = fence(t1_x, b1_z, grad_inner, grad_outer)

    shared = sums[0:8]
    b_att = sums[16, : 3 * n]
    grad_binner = ordered(sums[12, :units], sums[13, :units])
    g_top = ordered(t1, t1_x).astype(F32)
    g_bottom = merged(zbit, b1, b1_z).astype(F32)
    outer = lambda a, b: b_att[a:b, None] * means[0][None]
    grad_wout = g_bottom[n:] + means[2, :n][:, None] * shared[0][None]

    return (
        out_rows.reshape(micro, own, width),
        sums[6, 0],
        dx.reshape(micro, own, width),
        (g_top[:n] + outer(0, n)).T,
        b_att[:n],
        (g_top[n:] + outer(n, 2 * n)).T,
        (g_bottom[:n] + outer(2 * n, 3 * n)).T,
        b_att[2 * n :],
        grad_wout,
        shared[0],
        shared[1],
        shared[2],
        grad_inner,
        grad_binner,
        grad_outer,
        shared[3],
        shared[4],
        shared[5],
    )


def solution(mesh):
    rows = P(None, ("dp", "mp"), None)
    cols = P(None, "mp")
    split = P("mp")
    whole = P()
    placed = (rows, P(None, "dp"), whole, cols, split, cols, cols, split, P("mp", None))
    placed += (whole, whole, whole, cols, split, P("mp", None), whole, whole, whole)
    results = (rows, whole, rows, cols, split, cols, cols, split, P("mp", None))
    results += (whole, whole, whole, cols, split, P("mp", None), whole, whole, whole)
    return jax.shard_map(shards, mesh=mesh, in_specs=placed, out_specs=results, check_vma=False)
```

```python
import functools
import math

import jax
import jax.numpy as jnp
from jax import lax
from jax.experimental import pallas as pl
from jax.experimental.pallas import tpu as pltpu
from jax.sharding import PartitionSpec as P

HEAD = 64
SEQ = 512
EPS_NORM = 1e-5
EPS_UNIT = 1e-6
COS_SCALE = 20.0
LOG2E = 1.4426950408889634
NEG = -1e30
F32 = jnp.float32
BF16 = jnp.bfloat16
CORE, YBIT, XBIT = 1, 2, 4
PAD = 16


def dot(a, b, ca, cb, precision=None):
    return lax.dot_general(
        a, b, (((ca,), (cb,)), ((), ())), preferred_element_type=F32, precision=precision
    )


def mm(a, b):
    return dot(a, b, 1, 0)


def mm_nt(a, b):
    return dot(a, b, 1, 1)


def mm_tn(a, b):
    return dot(a, b, 0, 0)


def column(row):
    return jnp.broadcast_to(row, (8, row.shape[1])).T[:, :1]


def call(kernel, grid, ins, outs, scratch=(), prefetch=0, name=None, us=7, mib=44, keep=(), held=()):
    def spec(block, index):
        return pl.BlockSpec(block, index)

    def whole(a, **mode):
        rank = len(a)
        return pl.BlockSpec(tuple(a), lambda *_: (0,) * rank, **mode)

    def run(*args):
        in_specs, placed = [], list(args[:prefetch])
        for i, (item, arg) in enumerate(zip(ins, args[prefetch:])):
            big = arg.size > 1 << 16
            single = {"pipeline_mode": pl.Buffered(1)} if big else {}
            in_specs.append(whole(arg.shape, **single) if item is None else spec(*item))
            placed.append(
                pltpu.with_memory_space_constraint(arg, pltpu.HBM) if big and i not in held else arg
            )
        out_specs = [whole(o[0]) if len(o) == 2 else spec(*o[2:]) for o in outs]
        shapes = []
        for i, o in enumerate(outs):
            if i in keep:
                shapes.append(pltpu.VMEM(o[0], o[1]))
            elif math.prod(o[0]) > 1 << 16:
                shapes.append(pltpu.HBM(o[0], o[1]))
            else:
                shapes.append(jax.ShapeDtypeStruct(o[0], o[1]))
        return pl.pallas_call(
            kernel,
            out_shape=shapes,
            grid_spec=pltpu.PrefetchScalarGridSpec(
                num_scalar_prefetch=prefetch,
                grid=grid,
                in_specs=in_specs,
                out_specs=out_specs,
                scratch_shapes=list(scratch),
            ),
            compiler_params=pltpu.CompilerParams(vmem_limit_bytes=mib << 20),
            cost_estimate=pl.CostEstimate(flops=int(us * 1.1e9), transcendentals=0, bytes_accessed=1000),
            name=name,
        )(*placed)

    return run


def pack_att_kernel(bits_ref, wq, wk, wv, wo, bqv, att_ref, send_ref):
    n = wo.shape[0]
    att_ref[0:n, :] = wq[...]
    att_ref[n : 2 * n, :] = wk[...]
    att_ref[2 * n : 3 * n, :] = wv[...]
    att_ref[3 * n : 4 * n, :] = wo[...]
    rows = att_ref.shape[0] - 4 * n
    att_ref[4 * n :, :] = jnp.zeros_like(att_ref[4 * n :, :])
    att_ref[4 * n :, 0 : 3 * n] = jnp.broadcast_to(bqv[...], (rows, 3 * n))
    size = send_ref.shape[0]
    send_ref[...] = att_ref[pl.ds(pl.multiple_of(bits_ref[3] * size, 16), size), :]


def pack_ffn_kernel(bits_ref, win, bin_, wout, in_ref, out_ref, in_send, out_send):
    x = bits_ref[0]
    units = win.shape[1] // 2
    size = units + PAD
    for piece in range(2):
        take = pl.multiple_of((x if piece == 0 else 1 - x) * units, 128)
        base = piece * size
        in_ref[base : base + units, :] = win[:, pl.ds(take, units)].T
        in_ref[base + units : base + size, :] = jnp.zeros((PAD, in_ref.shape[1]), BF16)
        in_ref[base + units : base + size, 0:units] = jnp.broadcast_to(
            bin_[:, pl.ds(take, units)], (PAD, units)
        )
        out_ref[piece * units : (piece + 1) * units, :] = wout[pl.ds(take, units), :]
    in_send[...] = in_ref[0:size, :]
    out_send[...] = out_ref[0:units, :]


def key_rows(length, ones):
    row = lax.broadcasted_iota(jnp.int32, (PAD, SEQ), 0)
    pos = lax.broadcasted_iota(jnp.int32, (PAD, SEQ), 1)
    base = jnp.where((row >= 1) & (row <= ones), 1.0, 0.0)
    return jnp.where((row == 0) & (pos >= length), NEG, base).astype(BF16)


def split_rows(first, value):
    row = lax.broadcasted_iota(jnp.int32, (PAD, SEQ), 0)
    high = value.astype(BF16).astype(F32)
    middle = (value - high).astype(BF16).astype(F32)
    lower = value - high - middle
    out = jnp.where(row == 0, first, 0.0)
    for i, part in enumerate((high, middle, lower)):
        out = jnp.where(row == i + 1, part, out)
    return out.astype(BF16)


def stack(*parts):
    return jnp.concatenate(parts, axis=0)


def attention_forward(len_ref, x_ref, packs, qkv_ref, ctx_ref, lse_ref, stat_ref, per, slot):
    length = len_ref[pl.program_id(0)]
    scale = LOG2E / math.sqrt(HEAD)
    n = per * HEAD

    @pl.when(pl.program_id(0) == 0)
    def _():
        stat_ref[...] = jnp.zeros_like(stat_ref)

    keys = key_rows(length, 0)
    ones = jnp.ones((PAD, SEQ), BF16)
    x = x_ref[...]
    for r, w in enumerate(packs):
        bias = column(w[4 * n : 4 * n + 1, 0 : 3 * n].astype(F32))
        qkv_ref[3 * n * r : 3 * n * (r + 1), :] = (mm_nt(w[0 : 3 * n, :], x) + bias).astype(BF16)

    def scores(i):
        a = 3 * n * (i // per) + (i % per) * HEAD
        q = stack(qkv_ref[a : a + HEAD, :], ones)
        k = stack(qkv_ref[n + a : n + a + HEAD, :], keys)
        return mm_tn(k, q)

    heads = per * len(packs)
    following = scores(0)
    for i in range(heads):
        s = following
        if i + 1 < heads:
            following = scores(i + 1)
        top = jnp.max(s, axis=0, keepdims=True)
        e = jnp.exp2(s * scale - top * scale).astype(BF16)
        a = 3 * n * (i // per) + (i % per) * HEAD
        c = mm(stack(qkv_ref[2 * n + a : 2 * n + a + HEAD, :], ones), e)
        total = c[HEAD : HEAD + 1, :]
        ctx_ref[i * HEAD : (i + 1) * HEAD, :] = (c[0:HEAD, :] * (1.0 / total)).astype(BF16)
        lse_ref[i : i + 1, :] = top + jnp.log2(total) * (1.0 / scale)
    sums = mm_nt(jnp.ones((8, SEQ), BF16), ctx_ref[...])
    stat_ref[2:3, slot * n : (slot + len(packs)) * n] += sums[0:1, :]


def attend_first_kernel(len_ref, x_ref, w0, qkv_ref, ctx_ref, lse_ref, stat_ref, *, per):
    attention_forward(len_ref, x_ref, (w0,), qkv_ref, ctx_ref, lse_ref, stat_ref, per, 0)
    stat_ref[0:1, :] += jnp.sum(x_ref[...].astype(F32), axis=0, keepdims=True)


def attend_next_kernel(len_ref, x_ref, w0, qkv_ref, ctx_ref, lse_ref, stat_ref, *, per):
    attention_forward(len_ref, x_ref, (w0,), qkv_ref, ctx_ref, lse_ref, stat_ref, per, 1)


def normalise(v):
    mean = jnp.mean(v, axis=-1, keepdims=True)
    centred = v - mean
    inv = lax.rsqrt(jnp.mean(centred * centred, axis=-1, keepdims=True) + EPS_NORM)
    return centred * inv, inv


def attend_last_kernel(
    len_ref, bits_ref, x_ref, p0, p1, p2, p3, q0, q1, q2, q3, wa, wb, ctxa_ref, ctxb_ref, vec_ref,
    qkv_ref, ctx_ref, lse_ref, stat_ref, pack_ref, norm_ref, inv_ref, low_ref,
    wo_scr, all_scr, *, per
):
    n = per * HEAD

    @pl.when(pl.program_id(0) == 0)
    def _():
        size = p0.shape[0]
        for r, group in enumerate(((p0, p1, p2, p3), (q0, q1, q2, q3))):
            for k, ref in enumerate(group):
                start = pl.multiple_of(jnp.bitwise_xor(bits_ref[3], k) * size, 16)
                pack_ref[r, pl.ds(start, size), :] = ref[...]
        for r, w in enumerate((wa, wb, pack_ref.at[0], pack_ref.at[1])):
            wo_scr[r * n : (r + 1) * n, :] = w[3 * n : 4 * n, :]

    packs = (pack_ref.at[0], pack_ref.at[1])
    attention_forward(len_ref, x_ref, packs, qkv_ref, ctx_ref, lse_ref, stat_ref, per, 2)
    all_scr[0:n, :] = ctxa_ref[...]
    all_scr[n : 2 * n, :] = ctxb_ref[...]
    all_scr[2 * n : 4 * n, :] = ctx_ref[...]
    pre = mm_tn(all_scr[...], wo_scr[...]) + vec_ref[0:1, :] + x_ref[...].astype(F32)
    normal, inv = normalise(pre)
    norm_ref[...] = normal
    inv_ref[...] = jnp.broadcast_to(inv, inv_ref.shape)
    first = normal * vec_ref[1:2, :] + vec_ref[2:3, :]
    low_ref[...] = first.astype(BF16)
    stat_ref[1:2, :] += jnp.sum(first, axis=0, keepdims=True)


def gelu_pair(u):
    cdf = 0.5 * lax.erf(u * (1.0 / math.sqrt(2.0))) + 0.5
    density = jnp.exp2(u * u * (-0.5 * LOG2E)) * (1.0 / math.sqrt(2.0 * math.pi))
    return u * cdf, cdf + u * density


def join(ins, outs, wi, wo, bias, units):
    for i in range(2):
        part = slice(i * units, (i + 1) * units)
        wi[part, :] = ins[i][0:units, :]
        wo[part, :] = outs[i][...]
        if bias is not None:
            bias[:, part] = ins[i][units : units + 8, 0:units].astype(F32)


def feed_forward(low, groups, hid_ref, slope_ref, stat_ref, wi, wo, bias, units, slot):
    @pl.when(pl.program_id(0) == 0)
    def _():
        for g, (ins, outs) in enumerate(groups):
            join(ins, outs, wi.at[g], wo.at[g], bias.at[g], units)
        stat_ref[...] = jnp.zeros_like(stat_ref)

    out = None
    for g in range(len(groups)):
        pre = mm_nt(low, wi[g]) + bias[g, 0:1, :]
        hidden, slope = gelu_pair(pre)
        cols = slice(2 * units * g, 2 * units * (g + 1))
        sums = jnp.sum(hidden, axis=0, keepdims=True)
        piece = slice(units * g, units * (g + 1))
        stat_ref[slot : slot + 1, piece] += sums[:, 0:units]
        stat_ref[slot + 1 : slot + 2, piece] += sums[:, units : 2 * units]
        hidden = hidden.astype(BF16)
        hid_ref[:, cols] = hidden
        slope_ref[:, cols] = slope.astype(BF16)
        part = mm(hidden, wo[g])
        out = part if out is None else out + part
    return out


def ffn_near_kernel(
    low_ref, i0, o0, i1, o1, i2, o2, i3, o3, hid_ref, slope_ref, stat_ref, out_ref, wi, wo, bias, *, units
):
    groups = (((i0, i1), (o0, o1)), ((i2, i3), (o2, o3)))
    out_ref[...] = feed_forward(
        low_ref[...], groups, hid_ref, slope_ref, stat_ref, wi, wo, bias, units, 3
    )


def ffn_far_kernel(
    len_ref, low_ref, i0, o0, i1, o1, i2, o2, i3, o3, prev_ref, norm_ref, vec_ref, s0, s1, s2, s3,
    hid_ref, slope_ref, bundle_ref, out_ref, norm2_ref, inv2_ref, pool_ref, stat_ref, wi, wo, bias,
    *, units, blocks, share
):
    step = pl.program_id(0)
    sent, block = step // blocks, step % blocks
    groups = (((i0, i1), (o0, o1)), ((i2, i3), (o2, o3)))
    ffn = feed_forward(low_ref[...], groups, hid_ref, slope_ref, stat_ref, wi, wo, bias, units, 5)
    first = norm_ref[...] * vec_ref[1:2, :] + vec_ref[2:3, :]
    normal, inv = normalise(ffn + prev_ref[...] + vec_ref[3:4, :] + first)
    norm2_ref[...] = normal.astype(BF16)
    inv2_ref[...] = jnp.broadcast_to(inv, inv2_ref.shape)
    second = normal * vec_ref[4:5, :] + vec_ref[5:6, :]
    out_ref[...] = second.astype(BF16)
    rows = low_ref.shape[0]
    position = block * rows + lax.broadcasted_iota(jnp.int32, (rows, 1), 0)
    part = jnp.sum(jnp.where(position < len_ref[sent], second, 0.0), axis=0, keepdims=True)

    @pl.when(step == 0)
    def _():
        pool_ref[...] = jnp.zeros_like(pool_ref)

    pool_ref[pl.ds(sent, 1), :] += part / len_ref[sent].astype(F32)

    @pl.when(step == pl.num_programs(0) - 1)
    def _():
        bundle_ref[0:8, :] = share * (stat_ref[...] + s0[...] + s1[...] + s2[...] + s3[...])
        pool = pool_ref[...]
        unit = pool * lax.rsqrt(jnp.sum(pool * pool, axis=1, keepdims=True) + EPS_UNIT)
        count = bundle_ref.shape[0] - 8
        bundle_ref[8 : 8 + count, :] = unit[0:count, :]


def loss_kernel(
    len_ref, bits_ref, *refs, micro, blocks, fields
):
    unit_refs = refs[:blocks]
    (pool_ref, member_ref, norm_ref, inv_ref, vec_ref, dlow_ref, sums_ref, grad_scr) = refs[blocks:]
    step = pl.program_id(0)

    @pl.when(step == 0)
    def _():
        high = lax.Precision.HIGHEST
        units = jnp.concatenate([ref[...] for ref in unit_refs], axis=0)
        count = units.shape[0]
        sents = count // micro
        me = bits_ref[1]
        row = lax.broadcasted_iota(jnp.int32, (count, count), 0)
        col = lax.broadcasted_iota(jnp.int32, (count, count), 1)
        source = jnp.where(col // sents == row % micro, col % sents, -1)
        mask = jnp.zeros_like(row)
        for shift, largest, unit in fields:
            field = jnp.bitwise_and(lax.shift_right_logical(row // micro, shift), largest)
            mask = jnp.bitwise_xor(mask, field * unit)
        pick = (source == jnp.bitwise_xor(me, mask)).astype(F32)
        member = dot(pick, member_ref[...].astype(F32), 1, 0)
        same = dot(member, member, 1, 1)
        own = row == col
        apart = own | (row % micro != col % micro)
        positive = jnp.where(apart, 0.0, same)
        logits = COS_SCALE * dot(units, units, 1, 1, high)
        others = jnp.where(apart, NEG, logits)
        top = jnp.max(others, axis=1, keepdims=True)
        raised = jnp.exp(others - top)
        total = jnp.sum(raised, axis=1, keepdims=True)
        chosen = raised * positive
        total_pos = jnp.sum(chosen, axis=1, keepdims=True)
        each = jnp.log(total) - jnp.log(total_pos)
        loss = jnp.sum(each[0:micro], axis=0, keepdims=True)
        dlogits = raised / total - chosen / total_pos
        both = dlogits[0:micro, :] + dlogits.T[0:micro, :]
        dunits = COS_SCALE * dot(both, units, 1, 0, high)
        pooled = pool_ref[0:micro, :]
        rscale = lax.rsqrt(jnp.sum(pooled * pooled, axis=1, keepdims=True) + EPS_UNIT)
        unit = pooled * rscale
        grad_scr[0:micro, :] = rscale * (dunits - unit * jnp.sum(unit * dunits, axis=1, keepdims=True))
        sums_ref[...] = jnp.zeros_like(sums_ref)
        sums_ref[6:7, :] = jnp.broadcast_to(loss, (1, sums_ref.shape[1]))

    length = len_ref[step]
    spread = grad_scr[pl.ds(step, 1), :] * (1.0 / length.astype(F32))
    normal = norm_ref[...].astype(F32)
    g = spread * vec_ref[4:5, :]
    valid = lax.broadcasted_iota(jnp.int32, (SEQ, 1), 0) < length
    along = jnp.mean(g * normal, axis=1, keepdims=True)
    dpre = jnp.where(valid, inv_ref[:, 0:1] * (g - jnp.mean(g) - normal * along), 0.0)
    dlow_ref[...] = dpre.astype(BF16)
    sums_ref[3:4, :] += jnp.sum(dpre, axis=0, keepdims=True)
    sums_ref[4:5, :] += spread * jnp.sum(jnp.where(valid, normal, 0.0), axis=0, keepdims=True)
    sums_ref[5:6, :] += spread * length.astype(F32)


def ffn_back(dlow, low, hid_ref, slope_ref, outs, wo, acc, gb_ref, units, row):
    @pl.when(pl.program_id(0) == 0)
    def _():
        for i in range(2):
            wo[i * units : (i + 1) * units, :] = outs[i][...]
        acc[...] = jnp.zeros_like(acc)
        gb_ref[...] = jnp.zeros_like(gb_ref)

    di = mm_nt(dlow, wo[...]) * slope_ref[...].astype(F32)
    gb_ref[row : row + 1, :] += jnp.sum(di, axis=0, keepdims=True)
    dil = di.astype(BF16)
    acc[1] += mm_tn(hid_ref[...], dlow)
    acc[0] += mm_tn(dil, low)
    return dil


def centre_ffn(keep_ref, send_ref, acc, gb_ref, mean_ref, bsum, units, rows, row):
    for i, (r, g_ref) in enumerate(zip(rows, (keep_ref, send_ref))):
        part = slice(i * units, (i + 1) * units)
        g_ref[0:units, :] = (acc[0, part, :] - column(gb_ref[row : row + 1, part]) * mean_ref[1:2, :]).astype(BF16)
        centre = column(mean_ref[r[0] : r[0] + 1, r[1] : r[1] + units])
        g_ref[units : 2 * units, :] = (acc[1, part, :] - centre * bsum).astype(BF16)


def ffn_back_kernel(*refs, units, rows, row, parts, own, last):
    take = iter(refs)
    more = lambda count: [next(take) for _ in range(count)]
    dlow_ref, low_ref, hid_ref, slope_ref, o0, o1, mean_ref, bsum_ref = more(8)
    part_refs = more(parts)
    pieces = more(2 * (parts + own))
    prev_ref = next(take) if own else None
    norm_ref, inv_ref, vec_ref = more(3) if last else (None,) * 3
    keep_ref, send_ref, gb_ref = more(3)
    di_ref = None if own else next(take)
    dattn_ref, sums_ref = more(2) if last else (None,) * 2
    sum_ref = next(take) if parts + own and not last else None
    wo, acc = more(2)
    wi = next(take) if parts + own else None

    @pl.when(pl.program_id(0) == 0)
    def _():
        if last:
            sums_ref[...] = jnp.zeros_like(sums_ref)
        for i, ref in enumerate(pieces):
            wi[i * units : (i + 1) * units, :] = ref[0:units, :]

    dil = ffn_back(
        dlow_ref[...], low_ref[...], hid_ref, slope_ref, (o0, o1), wo, acc, gb_ref, units, row
    )
    if di_ref is not None:
        di_ref[...] = dil
    if parts + own:
        dfirst = prev_ref[...] if own else dlow_ref[...].astype(F32)
        for i, part in enumerate([ref[...] for ref in part_refs] + ([dil] if own else [])):
            dfirst = dfirst + mm(part, wi[2 * units * i : 2 * units * (i + 1), :])
        if not last:
            sum_ref[...] = dfirst
    if last:
        normal = norm_ref[...]
        g = dfirst * vec_ref[1:2, :]
        along = jnp.mean(g * normal, axis=1, keepdims=True)
        dpre = inv_ref[:, 0:1] * (g - jnp.mean(g, axis=1, keepdims=True) - normal * along)
        dattn_ref[...] = dpre.astype(BF16)
        sums_ref[0:1, :] += jnp.sum(dpre, axis=0, keepdims=True)
        sums_ref[1:2, :] += jnp.sum(dfirst * normal, axis=0, keepdims=True)
        sums_ref[2:3, :] += jnp.sum(dfirst, axis=0, keepdims=True)

    @pl.when(pl.program_id(0) == pl.num_programs(0) - 1)
    def _():
        centre_ffn(keep_ref, send_ref, acc, gb_ref, mean_ref, bsum_ref[3:4, :], units, rows, row)


def attend_back_kernel(
    len_ref, x_ref, dattn_ref, w_ref, qkv_ref, ctx_ref, lse_ref, mean_ref, bsum_ref,
    g_ref, gb_ref, grad_ref, acc, *, per, base, place
):
    step = pl.program_id(0)
    n = per * HEAD

    @pl.when(step == 0)
    def _():
        acc[...] = jnp.zeros_like(acc)
        gb_ref[...] = jnp.zeros_like(gb_ref)

    inv_root = 1.0 / math.sqrt(HEAD)
    scale = LOG2E * inv_root
    keys = key_rows(len_ref[step], 3)
    row = lax.broadcasted_iota(jnp.int32, (PAD, SEQ), 0)
    ones = jnp.where((row >= 1) & (row <= 3), 1.0, 0.0).astype(BF16)
    x = x_ref[...]
    dattn = dattn_ref[...]
    dctx = mm_nt(w_ref[3 * n : 4 * n, :], dattn).astype(BF16)
    acc[3 * n : 4 * n, :] += mm(ctx_ref[...], dattn)
    for h in range(per):
        c = h * HEAD
        q = qkv_ref[c : c + HEAD, :]
        k = qkv_ref[n + c : n + c + HEAD, :]
        v = qkv_ref[2 * n + c : 2 * n + c + HEAD, :]
        do = dctx[c : c + HEAD, :]
        o = ctx_ref[c : c + HEAD, :]
        lse = lse_ref[base * per + h : base * per + h + 1, :]
        weighted = jnp.sum(o.astype(F32) * do.astype(F32), axis=0, keepdims=True)
        s = mm_tn(stack(k, keys), stack(q, split_rows(1.0, -lse)))
        p = jnp.exp2(s * scale)
        dp = mm_tn(stack(v, ones), stack(do, split_rows(0.0, -weighted)))
        ds = (p * dp).astype(BF16)
        grad_ref[2 * n + c : 2 * n + c + HEAD, :] = mm_nt(do, p.astype(BF16)).astype(BF16)
        grad_ref[n + c : n + c + HEAD, :] = (mm_nt(q, ds) * inv_root).astype(BF16)
        grad_ref[c : c + HEAD, :] = (mm(k, ds) * inv_root).astype(BF16)
    grads = grad_ref[...]
    gb_ref[place : place + 1, 0 : 3 * n] += mm_nt(jnp.ones((8, SEQ), BF16), grads)[0:1, :]
    acc[0 : 3 * n, :] += mm(grads, x)

    @pl.when(step == pl.num_programs(0) - 1)
    def _():
        g_ref[0 : 3 * n, :] = (acc[0 : 3 * n, :] - column(gb_ref[place : place + 1, 0 : 3 * n]) * mean_ref[0:1, :]).astype(BF16)
        centre = column(mean_ref[2:3, place * n : (place + 1) * n])
        g_ref[3 * n : 4 * n, :] = (acc[3 * n : 4 * n, :] - centre * bsum_ref[0:1, :]).astype(BF16)


def input_grad_kernel(prev_ref, g0, g1, g2, g3, w0, w1, w2, w3, out_ref):
    out = prev_ref[...].astype(F32)
    for g, w in ((g0, w0), (g1, w1), (g2, w2), (g3, w3)):
        out = out + mm_tn(g[...], w[0 : g.shape[0], :])
    out_ref[...] = out


def ffn_final_kernel(bits_ref, in0, in1, out0, out1, small_ref, mean_ref, gin_ref, gout_ref):
    units = in0.shape[0]
    for p, (a, b) in enumerate(((in0, out0), (in1, out1))):
        spot = bits_ref[0] if p == 0 else 1 - bits_ref[0]
        spot = pl.multiple_of(spot * units, 128)
        part = slice(p * units, (p + 1) * units)
        grad = a[...].astype(F32) + column(small_ref[12 + p : 13 + p, 0:units]) * mean_ref[1:2, :]
        gin_ref[:, pl.ds(spot, units)] = grad.T
        gout_ref[pl.ds(spot, units), :] = (
            b[...].astype(F32) + column(mean_ref[3:4, part]) * small_ref[3:4, :]
        )


def fence(*values):
    return lax.optimization_barrier(values)


def shards(
    inputs, lengths, membership, w_query, b_query, w_key, w_value, b_value, w_output, b_output,
    gain_first, bias_first, w_inner, b_inner, w_outer, b_outer, gain_second, bias_second,
):
    total = lax.axis_size("dp") * lax.axis_size("mp")
    mp = lax.axis_index("mp")
    dp = lax.axis_index("dp")
    me = dp * lax.axis_size("mp") + mp
    xbit = dp % 2

    def flip(value, mask):
        return lax.ppermute(value, ("dp", "mp"), [(i, i ^ mask) for i in range(total)])

    def flip_hbm(value, mask):
        return flip(pltpu.with_memory_space_constraint(value, pltpu.HBM), mask)

    def ordered(a, b, axis=0):
        return jnp.where(xbit == 0, jnp.concatenate([a, b], axis), jnp.concatenate([b, a], axis))

    micro, own, width = inputs.shape
    rows = micro * own
    n = w_query.shape[1]
    per = n // HEAD
    units = w_inner.shape[1] // 2
    att_rows = 4 * n + 64
    att_piece = att_rows // 4
    in_size = units + PAD

    rest = 2 * XBIT
    zbit = (me // rest) % 2
    if 2 * rest < total:
        zbit = (zbit + (me // (2 * rest)) % 2) % 2
    bits = jnp.stack([xbit, me, zbit, 2 * xbit + (me // rest) % 2]).astype(jnp.int32)
    sent_lengths = lax.dynamic_slice_in_dim(lengths, mp, 1, 1).reshape(-1)
    x = inputs.reshape(rows, width)
    vectors = jnp.stack(
        [b_output, gain_first, bias_first, b_outer, gain_second, bias_second, b_outer, b_outer]
    ).astype(F32)

    row_block = lambda r, c: ((r, c), lambda s, *_: (s, 0))
    sent_block = lambda a: ((None, a, SEQ), lambda s, *_: (s, 0, 0))
    piece = lambda r, p: ((r, width), lambda s, *_: (p, 0))

    att_own, att_send = call(
        pack_att_kernel, (1,), [None] * 5,
        [((att_rows, width), BF16), ((att_piece, width), BF16)],
        prefetch=1, name="pack_att", us=2, mib=14, keep=(1,),
    )(bits, w_query.T, w_key.T, w_value.T, w_output,
      jnp.concatenate([b_query, jnp.zeros_like(b_query), b_value])[None])
    att_own, att_send, x, w_inner = fence(att_own, att_send, x, w_inner)

    def attn_outs(count):
        return [
            ((micro, 3 * n * count, SEQ), BF16, *sent_block(3 * n * count)),
            ((micro, n * count, SEQ), BF16, *sent_block(n * count)),
            ((micro, per * count, SEQ), F32, *sent_block(per * count)),
            ((8, width), F32),
        ]

    att_0 = flip(att_send, YBIT)
    att_sib = flip_hbm(att_own, CORE)
    in_own, out_own, in_send, out_send = call(
        pack_ffn_kernel, (1,), [None] * 3,
        [
            ((2 * in_size, width), BF16), ((2 * units, width), BF16),
            ((in_size, width), BF16), ((units, width), BF16),
        ],
        prefetch=1, name="pack_ffn", us=3, mib=16, keep=(2, 3),
    )(bits, w_inner, b_inner[None], w_outer)
    att_0, att_sib, x, in_own, out_own, in_send, out_send = fence(
        att_0, att_sib, x, in_own, out_own, in_send, out_send
    )
    att_2 = flip(att_0, XBIT)
    att_1 = flip(att_0, rest)
    in_y = flip(in_send, YBIT)
    sib_0 = flip(att_0, CORE)
    rows_out = ((rows, width), F32, *row_block(SEQ, width))
    qkv_0, ctx_0, lse_0, stat_0 = call(
        functools.partial(attend_first_kernel, per=per), (micro,),
        [row_block(SEQ, width), None], attn_outs(1),
        prefetch=1, name="attend_own", mib=60, held=(0,),
    )(sent_lengths, x, att_own)
    att_1, att_2, sib_0, x, qkv_0, ctx_0, lse_0, stat_0 = fence(
        att_1, att_2, sib_0, x, qkv_0, ctx_0, lse_0, stat_0
    )
    att_3 = flip(att_1, XBIT)
    sib_1 = flip(att_1, CORE)
    sib_2 = flip(att_2, CORE)
    qkv_1, ctx_1, lse_1, stat_1 = call(
        functools.partial(attend_next_kernel, per=per), (micro,),
        [row_block(SEQ, width), None], attn_outs(1),
        prefetch=1, name="attend_sibling", mib=60, held=(0, 1),
    )(sent_lengths, x, att_sib)
    att_3, sib_1, sib_2, in_y, x, qkv_1, ctx_1, lse_1, stat_1, in_own, out_own = fence(
        att_3, sib_1, sib_2, in_y, x, qkv_1, ctx_1, lse_1, stat_1, in_own, out_own
    )
    sib_3 = flip(att_3, CORE)
    in_x = flip(in_y, XBIT)
    out_y = flip(out_send, YBIT)
    in_sib = flip_hbm(in_own, CORE)
    out_sib = flip_hbm(out_own, CORE)
    qkv_b, ctx_b, lse_b, stat_2, att_far, norm1, inv1, low = call(
        functools.partial(attend_last_kernel, per=per), (micro,),
        [row_block(SEQ, width)] + [None] * 10 + [sent_block(n), sent_block(n), None],
        attn_outs(2) + [
            ((2, att_rows, width), BF16),
            rows_out,
            ((rows, 128), F32, *row_block(SEQ, 128)),
            ((rows, width), BF16, *row_block(SEQ, width)),
        ],
        scratch=[pltpu.VMEM((4 * n, width), BF16), pltpu.VMEM((4 * n, SEQ), BF16)],
        prefetch=2, name="attend_far", us=14, mib=60, held=tuple(range(9)) + (10,),
    )(
        sent_lengths, bits, x, att_0, att_1, att_2, att_3, sib_0, sib_1, sib_2, sib_3, att_own, att_sib,
        ctx_0, ctx_1, vectors,
    )
    low, norm1, inv1, in_x, out_y, in_sib, out_sib, in_y = fence(
        low, norm1, inv1, in_x, out_y, in_sib, out_sib, in_y
    )

    out_x = flip(out_y, XBIT)
    in_y_sib = flip(in_y, CORE)
    in_x_sib = flip(in_x, CORE)
    out_y_sib = flip(out_y, CORE)
    block = 256
    steps = rows // block
    ffn_outs = [
        ((rows, 4 * units), BF16, *row_block(block, 4 * units)),
        ((rows, 4 * units), BF16, *row_block(block, 4 * units)),
    ]
    ffn_scratch = [
        pltpu.VMEM((2, 2 * units, width), BF16),
        pltpu.VMEM((2, 2 * units, width), BF16),
        pltpu.VMEM((2, 8, 2 * units), F32),
    ]
    near_specs = []
    near = []
    for p in range(2):
        near_specs += [piece(in_size, p), piece(units, p)] * 2
        near += [in_own, out_own, in_sib, out_sib]
    hid_near, slope_near, stat_3, ffn_a = call(
        functools.partial(ffn_near_kernel, units=units), (steps,),
        [row_block(block, width)] + near_specs,
        ffn_outs + [((8, width), F32), ((rows, width), F32, *row_block(block, width))],
        scratch=ffn_scratch, name="ffn_near", mib=60, held=(3, 4, 7, 8),
    )(low, *near)
    out_x, in_x_sib, out_y_sib, in_y_sib, ffn_a, hid_near, slope_near, stat_3 = fence(
        out_x, in_x_sib, out_y_sib, in_y_sib, ffn_a, hid_near, slope_near, stat_3
    )
    out_x_sib = flip(out_x, CORE)

    far = [in_y, out_y, in_y_sib, out_y_sib, in_x, out_x, in_x_sib, out_x_sib]
    hid_far, slope_far, bundle, out_rows, norm2, inv2, pooled = call(
        functools.partial(
            ffn_far_kernel, units=units, blocks=SEQ // block, share=1.0 / (rows * total)
        ), (steps,),
        [row_block(block, width)] + [None] * 8
        + [row_block(block, width), row_block(block, width)] + [None] * 5,
        ffn_outs + [
            ((8 + micro, width), F32),
            ((rows, width), BF16, *row_block(block, width)),
            ((rows, width), BF16, *row_block(block, width)),
            ((rows, 128), F32, *row_block(block, 128)),
            ((8, width), F32),
        ],
        scratch=[pltpu.VMEM((8, width), F32)] + ffn_scratch, prefetch=1, name="ffn_far", mib=60, held=(1, 2, 3, 4, 5, 6, 7, 8),
    )(sent_lengths, low, *far, ffn_a, norm1, vectors, stat_0, stat_1, stat_2, stat_3)

    def rows_in(v, order):
        return [v[i : i + 1] for i in order]

    def other_means(v, mask):
        if mask == XBIT:
            rows = jnp.concatenate([v[3:7, units : 2 * units], v[3:7, :units]], axis=1)
            return jnp.concatenate([v[0:3], rows, v[7:8]], axis=0)
        order = (1, 0, 3, 2) if mask == CORE else (2, 3, 0, 1)
        slots = jnp.concatenate([v[2:3, i * n : (i + 1) * n] for i in order], axis=1)
        return jnp.concatenate([v[0:2], slots] + rows_in(v, [3 + i for i in order]) + [v[7:8]], axis=0)

    def groups_of(first, last):
        found, mask = [], first
        while mask < last:
            found.append((mask, 2 * mask, 3 * mask) if 2 * mask < last else (mask,))
            mask *= 4
        return found

    mp_stages, x_stages, z_stages = groups_of(1, XBIT), [(XBIT,)], [(rest,)]
    if 2 * rest < total:
        z_stages += [(2 * rest,)] + groups_of(4 * rest, total)

    def sum_step(v, masks, reorder):
        parts = [v]
        for m in masks:
            part = flip(v, m)
            for single in (CORE, YBIT, XBIT):
                if m & single:
                    part = reorder(part, single)
            parts.append(part)
        while len(parts) > 1:
            parts = [parts[i] + parts[i + 1] for i in range(0, len(parts), 2)]
        return parts[0]

    stages = z_stages + mp_stages + x_stages
    fields, shift = [], 0
    for index, masks in enumerate(stages):
        others = [flip(bundle, m) for m in masks]
        parts = [bundle[0:8]]
        for m, other in zip(masks, others):
            part = other[0:8]
            for single in (CORE, YBIT, XBIT):
                if m & single:
                    part = other_means(part, single)
            parts.append(part)
        while len(parts) > 1:
            parts = [parts[i] + parts[i + 1] for i in range(0, len(parts), 2)]
        mine = parts[0]
        unit_blocks = [bundle[8:]] + [o[8:] for o in others]
        fields.append((shift, len(masks), masks[0]))
        shift += (len(masks) + 1) // 2
        if index < len(stages) - 1:
            bundle = jnp.concatenate([mine] + unit_blocks, axis=0)
    means = mine

    dlow, sums2 = call(
        functools.partial(loss_kernel, micro=micro, blocks=len(unit_blocks), fields=fields), (micro,),
        [None] * (len(unit_blocks) + 2) + [row_block(SEQ, width), row_block(SEQ, 128), None],
        [
            ((rows, width), BF16, *row_block(SEQ, width)),
            ((8, width), F32),
        ],
        scratch=[pltpu.VMEM((8, width), F32)], prefetch=2, name="loss", mib=28,
    )(sent_lengths, bits, *unit_blocks, pooled, membership.reshape(-1, membership.shape[2]), norm2, inv2, vectors)

    back_rows = SEQ

    def ffn_part(half, p, dlow, row, parts=(), pieces=(), own=False, prev=None, last=False):
        hidden, slope, arrays, specs, base = half
        part = lambda s, *_: (s, p)
        block_of = lambda c: row_block(back_rows, c)
        ins = [block_of(width), block_of(width)] + [((back_rows, 2 * units), part)] * 2
        ins += [specs[1], specs[3], None, None] + [block_of(2 * units)] * len(parts)
        args = [dlow, low, hidden, slope, arrays[1], arrays[3], means, sums2, *parts]
        free = [4, 5] + list(range(len(args), len(args) + len(pieces)))
        ins += [spec for _, spec in pieces]
        args += [a for a, _ in pieces]
        places = ((base, p * units), (base + 1, p * units))
        outs = [((2 * units, width), BF16)] * 2 + [((8, 2 * units), F32)]
        scratch = [pltpu.VMEM((2 * units, width), BF16), pltpu.VMEM((2, 2 * units, width), F32)]
        rows_f32 = ((rows, width), F32, *block_of(width))
        if not own:
            outs += [((rows, 2 * units), BF16, *block_of(2 * units))]
        if own:
            ins += [block_of(width)]
            args += [prev]
        if pieces:
            scratch += [pltpu.VMEM((len(pieces) * units, width), BF16)]
        if last:
            ins += [block_of(width), block_of(128), None]
            args += [norm1, inv1, vectors]
            outs += [((rows, width), BF16, *block_of(width)), ((8, width), F32)]
        elif pieces:
            outs += [rows_f32]
        return call(
            functools.partial(
                ffn_back_kernel, units=units, rows=places, row=row, parts=len(parts), own=own, last=last
            ),
            (rows // back_rows,), ins, outs, scratch=scratch, name="ffn_back",
            us=8 + 2 * len(pieces), mib=44, keep=(0, 1), held=free,
        )(*args)

    near_half = lambda p: (
        hid_near, slope_near, near[0:4], [piece(in_size, p), piece(units, p)] * 2, 3
    )
    far_half = lambda p: (hid_far, slope_far, far[4 * p : 4 * p + 4], [None] * 4, 5)

    def add(*values):
        out = values[0].astype(F32)
        for v in values[1:]:
            out = out + v.astype(F32)
        return out.astype(BF16)

    def rest_split(a, mask):
        half = a.shape[0] // 2
        bit = (me // mask) % 2
        if 2 * mask < total:
            bit = (bit + (me // (2 * mask)) % 2) % 2
        keep = lax.dynamic_slice_in_dim(a, bit * half, half, 0)
        send = lax.dynamic_slice_in_dim(a, (1 - bit) * half, half, 0)
        return bit, keep, send

    def rest_finish(bit, part, mask):
        inner = mask * 2
        while inner < total:
            part = add(part, flip(part, inner | mask if inner == 2 * mask else inner))
            inner *= 2
        other = flip(part, mask)
        return jnp.where(
            bit == 0, jnp.concatenate([part, other], 0), jnp.concatenate([other, part], 0)
        )

    def merged(bit, mine, other):
        return jnp.where(
            bit == 0, jnp.concatenate([mine, other], 0), jnp.concatenate([other, mine], 0)
        )

    def inner_flip(a):
        return flip(a, 3 * rest) if 2 * rest < total else jnp.zeros_like(a)

    def inner_rest(a):
        mask = 4 * rest
        while mask < total:
            a = add(a, flip(a, mask))
            mask *= 2
        return a

    full, part = units, units // 2
    top, bottom = slice(0, full), slice(full, 2 * full)

    def halves(a, bit):
        half = a.shape[0] // 2
        kept = lax.dynamic_slice_in_dim(a, bit * half, half, 0)
        return kept, lax.dynamic_slice_in_dim(a, (1 - bit) * half, half, 0)

    def halves_z(a):
        return halves(a, zbit)

    far_in = lambda p: [(far[4 * p], None), (far[4 * p + 2], None)]
    near_in = lambda p: [(near[0], piece(in_size, p)), (near[2], piece(in_size, p))]
    k_f1, s_f1, gb_f1, di_f1 = ffn_part(far_half(1), 1, dlow, 7)
    c_f1 = flip(s_f1, CORE)
    f1a = add(k_f1[top], c_f1[top])
    f1a, c_f1, k_f1, dlow = fence(f1a, c_f1, k_f1, dlow)

    y1a = flip(f1a, YBIT)
    k_f0, s_f0, gb_f0, di_f0, acc = ffn_part(
        far_half(0), 0, dlow, 6, (di_f1,), far_in(1)
    )
    f1b = add(k_f1[bottom], c_f1[bottom])
    y1a, f1b, k_f0, s_f0, gb_f0, di_f0, acc, dlow = fence(
        y1a, f1b, k_f0, s_f0, gb_f0, di_f0, acc, dlow
    )

    y1b = flip(f1b, YBIT)
    c_f0 = flip(s_f0, CORE)
    k_n1, s_n1, gb_n1, acc = ffn_part(
        near_half(1), 1, dlow, 5, (di_f0,), far_in(0) + near_in(1), own=True, prev=acc
    )
    y1b, c_f0, k_n1, s_n1, gb_n1, acc, dlow = fence(y1b, c_f0, k_n1, s_n1, gb_n1, acc, dlow)
    c_n1 = flip(s_n1, CORE)
    f0a = add(k_f0[top], c_f0[top])
    f0b = add(k_f0[bottom], c_f0[bottom])
    c_n1, f0a, f0b, dlow = fence(c_n1, f0a, f0b, dlow)
    y0a = flip(f0a, YBIT)
    s1a = add(k_n1[top], c_n1[top], y1a)
    s1b = add(k_n1[bottom], c_n1[bottom], y1b)
    s1a, s1b, dlow = fence(s1a, s1b, dlow)

    x1a = flip(s1a, XBIT)
    x1b = flip(s1b, XBIT)
    k_n0, s_n0, gb_n0, dattn, sums1 = ffn_part(
        near_half(0), 0, dlow, 4, (), near_in(0), own=True, prev=acc, last=True
    )
    y0a, x1a, k_n0, s_n0, gb_n0, dattn, sums1, f0b = fence(
        y0a, x1a, k_n0, s_n0, gb_n0, dattn, sums1, f0b
    )
    def other_sums(v, mask):
        if mask == CORE:
            ffn = jnp.concatenate([v[8:16, units : 2 * units], v[8:16, :units]], axis=1)
            return jnp.concatenate([v[:8], ffn] + rows_in(v, (17, 16, 19, 18)) + [v[20:24]], axis=0)
        if mask == YBIT:
            order = (14, 15, 12, 13)
            return jnp.concatenate([v[:12]] + rows_in(v, order + (18, 19, 16, 17)) + [v[20:24]], axis=0)
        return jnp.concatenate([v[:12]] + rows_in(v, (13, 12, 15, 14)) + [v[16:24]], axis=0)

    def sums_step(v, mask):
        return sum_step(v, (mask,), other_sums) if mask < total else v

    c_n0 = flip(s_n0, CORE)
    keep_a, send_a = halves_z(add(k_n0[top], c_n0[top], y0a, x1a))
    keep_a, send_a, c_n0, dattn, f0b = fence(keep_a, send_a, c_n0, dattn, f0b)

    def attend_part(w, qkv, ctx, lse, base, place, dattn):
        w_spec = None if w.ndim == 2 else ((None, att_rows, width), lambda s, *_: (base, 0, 0))
        quarter_block = lambda a: ((None, a, SEQ), lambda s, *_: (s, base, 0))
        return call(
            functools.partial(attend_back_kernel, per=per, base=base, place=place), (micro,),
            [
                row_block(SEQ, width), row_block(SEQ, width), w_spec, quarter_block(3 * n),
                quarter_block(n), sent_block(lse.shape[1]), None, None,
            ],
            [
                ((4 * n, width), BF16), ((8, width), F32),
                ((micro, 3 * n, SEQ), BF16, *sent_block(3 * n)),
            ],
            scratch=[pltpu.VMEM((4 * n, width), F32)],
            prefetch=1, name="attend_back", mib=24, keep=(0,),
            held=() if w is not att_sib else (2,),
        )(sent_lengths, x, dattn, w, qkv, ctx, lse, means, sums1)

    y0b = flip(f0b, YBIT)
    z_a = flip(send_a, rest)
    g_3, gb_3, dq_3 = attend_part(att_far, qkv_b, ctx_b, lse_b, 1, 3, dattn)
    y0b, x1b, z_a, g_3, gb_3, dq_3, dattn = fence(
        y0b, x1b, z_a, g_3, gb_3, dq_3, dattn
    )
    keep_b, send_b = halves_z(add(k_n0[bottom], c_n0[bottom], y0b, x1b))
    r_a = add(keep_a, z_a)
    r_a, send_b, keep_b, g_3, dattn = fence(r_a, send_b, keep_b, g_3, dattn)

    i_a = inner_flip(r_a)
    z_b = flip(send_b, rest)
    c_3 = flip(g_3, CORE)
    g_2, gb_2, dq_2 = attend_part(att_far, qkv_b, ctx_b, lse_b, 0, 2, dattn)
    c_3, i_a, z_b, g_2, gb_2, dq_2, dattn = fence(
        c_3, i_a, z_b, g_2, gb_2, dq_2, dattn
    )
    af_a = add(g_2[top], c_3[top])
    r_a = inner_rest(add(r_a, i_a))
    r_b = add(keep_b, z_b)
    af_a, g_2, c_3, r_a, r_b, dattn = fence(af_a, g_2, c_3, r_a, r_b, dattn)

    y_afa = flip(af_a, YBIT)
    z_a = flip(r_a, rest)
    i_b = inner_flip(r_b)
    g_1, gb_1, dq_1 = attend_part(att_sib, qkv_1, ctx_1, lse_1, 0, 1, dattn)
    af_b = add(g_2[bottom], c_3[bottom])
    y_afa, i_b, z_a, g_1, gb_1, dq_1, dattn, af_b = fence(
        y_afa, i_b, z_a, g_1, gb_1, dq_1, dattn, af_b
    )
    r_in = merged(zbit, r_a, z_a)
    r_b = inner_rest(add(r_b, i_b))
    r_in, r_b, g_1, dattn, af_b = fence(r_in, r_b, g_1, dattn, af_b)

    y_afb = flip(af_b, YBIT)
    c_1 = flip(g_1, CORE)
    r_in_x = flip(r_in, XBIT)
    z_b = flip(r_b, rest)
    g_0, gb_0, dq_0 = attend_part(att_own, qkv_0, ctx_0, lse_0, 0, 0, dattn)
    y_afb, c_1, r_in_x, z_b, g_0, gb_0, dq_0, dattn = fence(
        y_afb, c_1, r_in_x, z_b, g_0, gb_0, dq_0, dattn
    )
    sums = jnp.concatenate(
        [sums1 + sums2, gb_n0 + gb_n1 + gb_f0 + gb_f1, gb_0 + gb_1 + gb_2 + gb_3], axis=0
    )
    sums = sums_step(sums, CORE)

    t_keep, t_send = halves(add(g_0[top], c_1[top], y_afa), xbit)
    b_keep, b_send = halves_z(add(g_0[bottom], c_1[bottom], y_afb))
    r_out = merged(zbit, r_b, z_b)
    t_send, b_send, t_keep, b_keep, r_out, dattn, sums = fence(
        t_send, b_send, t_keep, b_keep, r_out, dattn, sums
    )
    t_x = flip(t_send, XBIT)
    b_z = flip(b_send, rest)
    sums = sums_step(sums, YBIT)
    second = lambda i: ((None, att_rows, width), lambda s, *_: (i, 0, 0))
    (dx,) = call(
        input_grad_kernel, (2 * micro,),
        [row_block(SEQ // 2, width)]
        + [((None, 3 * n, SEQ // 2), lambda s, *_: (s // 2, 0, s % 2))] * 4
        + [None, None, second(0), second(1)],
        [((rows, width), F32, *row_block(SEQ // 2, width))], name="input_grad", mib=28, held=(6,),
    )(dattn, dq_0, dq_1, dq_2, dq_3, att_own, att_sib, att_far, att_far)

    t_x, b_z, dx, sums, r_out = fence(t_x, b_z, dx, sums, r_out)
    t2_keep, t2_send = halves_z(add(t_keep, t_x))
    b2_keep, b2_send = halves(add(b_keep, b_z), xbit)
    t2_send, b2_send, t2_keep, b2_keep, sums = fence(t2_send, b2_send, t2_keep, b2_keep, sums)
    t2_z = flip(t2_send, rest)
    b2_x = flip(b2_send, XBIT)
    sums = sums_step(sums_step(sums, XBIT), rest)
    t2_z, b2_x, sums, r_out = fence(t2_z, b2_x, sums, r_out)
    r_out_x = flip(r_out, XBIT)
    t2 = add(t2_keep, t2_z)
    b2 = add(b2_keep, b2_x)
    t2, b2, sums = fence(t2, b2, sums)
    t2_i = inner_flip(t2)
    b2_i = inner_flip(b2)
    t2_i, b2_i, sums = fence(t2_i, b2_i, sums)
    t2 = inner_rest(add(t2, t2_i))
    b2 = inner_rest(add(b2, b2_i))
    t2, b2, sums = fence(t2, b2, sums)
    t2_z = flip(t2, rest)
    b2_x = flip(b2, XBIT)
    sums = sums_step(sums, 2 * rest)
    mask = 4 * rest
    while mask < total:
        sums = sums_step(sums, mask)
        mask *= 2
    t2_z, b2_x, sums = fence(t2_z, b2_x, sums)
    t1 = merged(zbit, t2, t2_z)
    b1 = merged(xbit, b2, b2_x)
    t1, b1, sums, r_out_x = fence(t1, b1, sums, r_out_x)
    t1_x = flip(t1, XBIT)
    b1_z = flip(b1, rest)
    grad_inner, grad_outer = call(
        ffn_final_kernel, (1,), [None] * 6, [((width, 2 * units), F32), ((2 * units, width), F32)],
        prefetch=1, name="ffn_final", mib=20, held=range(4),
    )(bits, r_in, r_in_x, r_out, r_out_x, sums, means)
    t1_x, b1_z, grad_inner, grad_outer = fence(t1_x, b1_z, grad_inner, grad_outer)

    shared = sums[0:8]
    b_att = sums[16, : 3 * n]
    grad_binner = ordered(sums[12, :units], sums[13, :units])
    g_top = ordered(t1, t1_x).astype(F32)
    g_bottom = merged(zbit, b1, b1_z).astype(F32)
    outer = lambda a, b: b_att[a:b, None] * means[0][None]
    grad_wout = g_bottom[n:] + means[2, :n][:, None] * shared[0][None]

    return (
        out_rows.reshape(micro, own, width),
        sums[6, 0],
        dx.reshape(micro, own, width),
        (g_top[:n] + outer(0, n)).T,
        b_att[:n],
        (g_top[n:] + outer(n, 2 * n)).T,
        (g_bottom[:n] + outer(2 * n, 3 * n)).T,
        b_att[2 * n :],
        grad_wout,
        shared[0],
        shared[1],
        shared[2],
        grad_inner,
        grad_binner,
        grad_outer,
        shared[3],
        shared[4],
        shared[5],
    )


def solution(mesh):
    rows = P(None, ("dp", "mp"), None)
    cols = P(None, "mp")
    split = P("mp")
    whole = P()
    placed = (rows, P(None, "dp"), whole, cols, split, cols, cols, split, P("mp", None))
    placed += (whole, whole, whole, cols, split, P("mp", None), whole, whole, whole)
    results = (rows, whole, rows, cols, split, cols, cols, split, P("mp", None))
    results += (whole, whole, whole, cols, split, P("mp", None), whole, whole, whole)
    return jax.shard_map(shards, mesh=mesh, in_specs=placed, out_specs=results, check_vma=False)
```
